128 devices in a mesh: role: 4 (over x), dp: 32 (over z, y, core).
Axes of the slice: x: 4, y: 4, z: 4, core: 2. Of those that a mesh axis runs over, the one named last changes fastest.
Arguments:
- wavlm_hidden: bfloat16 [64, 512, 1024], P('dp'), may hold values from -6 to 6
- whisper_hidden: bfloat16 [64, 512, 1280], P('dp'), may hold values from -6 to 6
- wavlm_qkv: bfloat16 [1024, 3072], P(None, 'dp'), may hold values from -8 to 8
- whisper_qkv: bfloat16 [1280, 3840], P(None, 'dp'), may hold values from -8 to 8
- wavlm_out: bfloat16 [1024, 1024], replicated, may hold values from -0.1875 to 0.1875
- whisper_out: bfloat16 [1280, 1280], replicated, may hold values from -0.15625 to 0.15625
- frames_valid: int32 [64], replicated, may hold values from 128 to 512, as said below
- slot_clip: int32 [64], replicated, may hold values from 0 to 63, each once
- latent: bfloat16 [2, 32, 128, 512], P(None, 'dp'), may hold values from -6 to 6
- wavlm_head: bfloat16 [512, 1024], replicated, may hold values from -0.25 to 0.25
- whisper_head: bfloat16 [512, 1280], replicated, may hold values from -0.25 to 0.25
Outputs:
- grad_wavlm_head: float32 [512, 1024], replicated
- grad_whisper_head: float32 [512, 1280], replicated
The draws below stay inside these ranges and needn't reach their ends.
Inputs may be any that keep to these rules, and one draw needn't show every extreme that they name: `frames_valid`: a multiple of 4; some clip has all 512 frames valid. `slot_clip`: every clip stands in exactly one slot.
All inputs are finite; a program needn't handle non-finite values.
Results may differ from the reference program's by a relative error of at most 0.002.
Values may be sent and summed in bfloat16 or wider, within the bound.
No kernel may reach another device: no remote copies, remote signals or barrier semaphores. Data moves between devices by JAX's collectives and lax.ppermute only.
A program may use at most 128 MiB of HBM per device.

```python
import jax
import jax.numpy as jnp
from jax import lax

WAVLM_D = 1024
WHISPER_D = 1280
STU_D = 512
HEAD = 64
FRAMES = 512
POOL = 4
POOLED = 128
CLIPS = 64


def projection_draw(key, full_width):
    normal_key = jax.random.fold_in(jax.random.fold_in(key, 31), 0)
    weight = jax.random.normal(normal_key, (full_width, 3 * full_width), jnp.float32) * full_width ** (-0.5)
    return jnp.clip(weight, -8.0, 8.0).astype(jnp.bfloat16)


def draw_wavlm_qkv(key, part):
    return projection_draw(jax.random.fold_in(key, 5), WAVLM_D)


def draw_whisper_qkv(key, part):
    return projection_draw(jax.random.fold_in(key, 9), WHISPER_D)


def draw_frames_valid(key, part):
    count_key, full_key = jax.random.split(jax.random.fold_in(key, 17))
    pooled_counts = jax.random.randint(count_key, (CLIPS,), POOLED // 4, POOLED + 1)
    longest = jax.random.randint(full_key, (), 0, CLIPS)
    pooled_counts = pooled_counts.at[longest].set(POOLED)
    return (pooled_counts * POOL).astype(jnp.int32)


def steps_of(own_key, extent, shards, smallest, largest):
    gain = 1.0
    for dim, shards_of in shards:
        draws = jax.random.uniform(jax.random.fold_in(jax.random.fold_in(own_key, 6), dim), (shards_of,), jnp.float32, smallest / len(shards), largest / len(shards))
        gain = gain * jnp.repeat(jnp.exp(draws), extent[dim] // shards_of).reshape((-1,) + (1,) * (len(extent) - 1 - dim))
    return gain


def scatter_about(stream_key, shape, deviation, limit, shards=(), held_as=jnp.bfloat16):
    values = deviation * jax.random.normal(stream_key, shape, jnp.float32)
    if shards:
        values = values * steps_of(stream_key, shape, shards, -0.22, 0.18)
    return jnp.clip(values, -limit, limit).astype(held_as)


def setup_inputs(seed: int = 0) -> dict:
    seeds = jax.random.split(jax.random.key(seed), 12)
    wavlm_hidden = scatter_about(seeds[0], (CLIPS, FRAMES, WAVLM_D), 1.0, 6.0, ((0, 32),))
    whisper_hidden = scatter_about(seeds[1], (CLIPS, FRAMES, WHISPER_D), 1.0, 6.0, ((0, 32),))
    wavlm_qkv = draw_wavlm_qkv(jax.random.fold_in(seeds[11], 71), 0)
    whisper_qkv = draw_whisper_qkv(jax.random.fold_in(seeds[11], 71), 0)
    wavlm_out = scatter_about(seeds[4], (WAVLM_D, WAVLM_D), WAVLM_D ** -0.5, 0.1875)
    whisper_out = scatter_about(seeds[5], (WHISPER_D, WHISPER_D), WHISPER_D ** -0.5, 0.15625)
    frames_valid = draw_frames_valid(jax.random.fold_in(seeds[11], 71), 0)
    slot_clip = jax.random.permutation(seeds[7], CLIPS).astype(jnp.int32)
    latent = scatter_about(seeds[8], (2, CLIPS // 2, POOLED, STU_D), 1.0, 6.0, ((1, 32),))
    wavlm_head = scatter_about(seeds[9], (STU_D, WAVLM_D), STU_D ** -0.5, 0.25)
    whisper_head = scatter_about(seeds[10], (STU_D, WHISPER_D), STU_D ** -0.5, 0.25)
    return {"wavlm_hidden": wavlm_hidden, "whisper_hidden": whisper_hidden, "wavlm_qkv": wavlm_qkv, "whisper_qkv": whisper_qkv, "wavlm_out": wavlm_out, "whisper_out": whisper_out, "frames_valid": frames_valid, "slot_clip": slot_clip, "latent": latent, "wavlm_head": wavlm_head, "whisper_head": whisper_head}


epsilon_norm = 1e-05
epsilon_cos = 1e-06

def layer_norm(hidden):
    hidden_f = hidden.astype(jnp.float32)
    centred = hidden_f - lax.optimization_barrier(jnp.mean(hidden_f, axis=-1, keepdims=True))
    variance = lax.optimization_barrier(jnp.mean(centred * centred, axis=-1, keepdims=True))
    return (centred * lax.rsqrt(variance + epsilon_norm)).astype(jnp.bfloat16)

def teacher_clip(hidden, valid_frames, qkv_weight, out_weight):
    full_width = hidden.shape[-1]
    head_count = full_width // HEAD
    frame_count = hidden.shape[0]
    normed = layer_norm(hidden)
    projected = jnp.dot(normed, qkv_weight, preferred_element_type=jnp.float32).astype(jnp.bfloat16)
    query_rows = projected[:, :full_width].reshape(frame_count, head_count, HEAD).astype(jnp.float32)
    key_rows = projected[:, full_width:2 * full_width].reshape(frame_count, head_count, HEAD).astype(jnp.float32)
    value_rows = projected[:, 2 * full_width:].reshape(frame_count, head_count, HEAD).astype(jnp.float32)
    scores = jnp.einsum('qhd,khd->hqk', query_rows, key_rows) * HEAD ** (-0.5)
    key_mask = jnp.arange(frame_count) < valid_frames
    scores = jnp.where(key_mask[None, None, :], scores, -1e+30)
    row_max = lax.optimization_barrier(jnp.max(scores, axis=-1, keepdims=True))
    raised = jnp.exp(scores - row_max)
    weights = (raised / lax.optimization_barrier(jnp.sum(raised, axis=-1, keepdims=True))).astype(jnp.bfloat16)
    attended = jnp.einsum('hqk,khd->qhd', weights.astype(jnp.float32), value_rows)
    attended = attended.astype(jnp.bfloat16).reshape(frame_count, full_width)
    result = hidden.astype(jnp.float32) + jnp.dot(attended, out_weight, preferred_element_type=jnp.float32)
    return lax.optimization_barrier(jnp.mean(result.reshape(frame_count // POOL, POOL, full_width), axis=1)).astype(jnp.bfloat16)

def head_gradient(latent_rows, target_rows, head_weight, row_mask):
    predicted = jnp.dot(latent_rows, head_weight, preferred_element_type=jnp.float32)
    target_f = target_rows.astype(jnp.float32)
    width_scale = 1.0 / target_rows.shape[-1]
    pred_norm = jnp.sqrt(lax.optimization_barrier(jnp.sum(predicted * predicted, axis=-1)) + epsilon_cos)
    target_norm = jnp.sqrt(lax.optimization_barrier(jnp.sum(target_f * target_f, axis=-1)) + epsilon_cos)
    cosine = lax.optimization_barrier(jnp.sum(predicted * target_f, axis=-1)) / (pred_norm * target_norm)
    slope = (cosine / (pred_norm * pred_norm))[:, None] * predicted - target_f / (pred_norm * target_norm)[:, None]
    slope = slope + (predicted - target_f) * width_scale
    slope = jnp.where(row_mask[:, None], slope, 0.0).astype(jnp.bfloat16)
    return jnp.einsum('nd,nw->dw', latent_rows.astype(jnp.float32), slope.astype(jnp.float32))

def reference(wavlm_hidden, whisper_hidden, wavlm_qkv, whisper_qkv, wavlm_out, whisper_out, frames_valid, slot_clip, latent, wavlm_head, whisper_head):

    def wavlm_one(clip_args):
        return teacher_clip(clip_args[0], clip_args[1], wavlm_qkv, wavlm_out)

    def whisper_one(clip_args):
        return teacher_clip(clip_args[0], clip_args[1], whisper_qkv, whisper_out)
    wavlm_pooled = lax.map(wavlm_one, (wavlm_hidden, frames_valid))
    whisper_pooled = lax.map(whisper_one, (whisper_hidden, frames_valid))
    wavlm_target = jnp.take(wavlm_pooled, slot_clip, axis=0).reshape(CLIPS * POOLED, WAVLM_D)
    whisper_target = jnp.take(whisper_pooled, slot_clip, axis=0).reshape(CLIPS * POOLED, WHISPER_D)
    latent_rows = latent.reshape(CLIPS * POOLED, STU_D)
    slot_valid = jnp.take(frames_valid, slot_clip) // POOL
    row_mask = (jnp.arange(POOLED)[None, :] < slot_valid[:, None]).reshape(-1)
    grad_wavlm = head_gradient(latent_rows, wavlm_target, wavlm_head, row_mask)
    grad_whisper = head_gradient(latent_rows, whisper_target, whisper_head, row_mask)
    return (grad_wavlm, grad_whisper)
```

```python
import jax
import jax.numpy as jnp
from jax import lax
from jax.experimental import pallas as pl
from jax.experimental.pallas import tpu as pltpu
from jax.sharding import PartitionSpec as P

WAVLM_D = 1024
WHISPER_D = 1280
STU_D = 512
HEAD = 64
FRAMES = 512
POOL = 4
POOLED = 128
CLIPS = 64
ROLES = 4
A_HEADS = WAVLM_D // HEAD // ROLES
W_HEADS = WHISPER_D // HEAD // ROLES
A_COLS = A_HEADS * HEAD
W_COLS = W_HEADS * HEAD
OUT_COLS = 640
ROWS = 64

epsilon_norm = 1e-05
epsilon_cos = 1e-06


bf16 = jnp.bfloat16
f32 = jnp.float32


def dp_send(x, dz, dy, dc):
    pairs = []
    for i in range(32):
        z, y, c = i // 8, (i // 2) % 4, i % 2
        target = ((z + dz) % 4) * 8 + ((y + dy) % 4) * 2 + (c + dc) % 2
        pairs.append((i, target))
    return lax.ppermute(x, "dp", pairs)


def role_send(x, k):
    return lax.ppermute(x, "role", [(i, (i + k) % ROLES) for i in range(ROLES)])


def layer_norm(hidden):
    hidden_f = hidden.astype(f32)
    centred = hidden_f - jnp.mean(hidden_f, axis=-1, keepdims=True)
    variance = jnp.mean(centred * centred, axis=-1, keepdims=True)
    return (centred * lax.rsqrt(variance + epsilon_norm)).astype(bf16)


def weight_chunks(wavlm_qkv, whisper_qkv):
    wa = wavlm_qkv.T.reshape(3, 32, 4, 2, 128).transpose(2, 3, 0, 1, 4)
    ww = jnp.pad(whisper_qkv.T, ((0, 8), (0, 0)))
    ww = ww.reshape(4, 32, 2, 5, 128).transpose(0, 2, 3, 1, 4)
    return jnp.concatenate([wa, ww], axis=2)


def attend_kernel(info, *refs):
    pieces = refs[:16]
    norm_a, norm_w = refs[16:18]
    outs = refs[18:22]
    wt_a, wt_w, qkv_a, qkv_w, proj, att_a, att_w, pooled, sem_a, sem_w = refs[22:]
    role, z, y, c = info[0], info[1], info[2], info[3]
    for n, piece in enumerate(pieces):
        core = (c + n // 8) % 2
        half = (n % 8) // 4
        k = n % 4
        for step in range(4):
            if half == 0:
                zs, ys = (z - step) % 4, (y - k) % 4
            else:
                zs, ys = (z - k) % 4, (y - step) % 4
            block = ys * 2 + core
            pltpu.make_async_copy(
                piece.at[step, pl.ds(0, 3)], wt_a.at[2 * zs + half, pl.ds(3 * block, 3)], sem_a
            ).start()
            pltpu.make_async_copy(
                piece.at[step, pl.ds(3, 5)],
                wt_w.at[pl.ds(5 * half, 5), block * 4 + zs],
                sem_w,
            ).start()
    ones_row = jnp.where(
        lax.broadcasted_iota(jnp.int32, (16, FRAMES), 0) == 0, 1.0, 0.0
    ).astype(bf16)
    pool_mat = jnp.where(
        lax.broadcasted_iota(jnp.int32, (POOLED, FRAMES), 1) // POOL
        == lax.broadcasted_iota(jnp.int32, (POOLED, FRAMES), 0),
        1.0 / POOL,
        0.0,
    ).astype(bf16)
    nt = (((1,), (1,)), ((), ()))
    tn = (((0,), (0,)), ((), ()))

    def put(qkv, kind, clip, head, value):
        scale = jnp.where(kind == 0, HEAD ** (-0.5), 1.0).astype(f32)
        qkv[kind, clip, head] = (value.astype(bf16).astype(f32) * scale).astype(bf16)

    def attention(qkv, att, heads):
        def one(i, carry):
            clip = i // heads
            head = i % heads
            valid = info[4 + clip]
            query = qkv[0, clip, head]
            key = qkv[1, clip, head]
            value = qkv[2, clip, head]
            rows = lax.broadcasted_iota(jnp.int32, (16, FRAMES), 0)
            frame = lax.broadcasted_iota(jnp.int32, (16, FRAMES), 1)
            bias = jnp.where((rows == 0) & (frame >= valid), -1e30, 0.0).astype(bf16)
            key_x = jnp.concatenate([key, bias], axis=0)
            query_x = jnp.concatenate([query, ones_row], axis=0)
            value_x = jnp.concatenate([value, ones_row], axis=0)
            scores = lax.dot_general(key_x, query_x, tn, preferred_element_type=f32)
            top = jnp.max(scores, axis=0, keepdims=True)
            raised = jnp.exp(scores - top).astype(bf16)
            mixed = jnp.dot(value_x, raised, preferred_element_type=f32)
            total = mixed[HEAD : HEAD + 1]
            att[clip, head] = (mixed[:HEAD] * (1.0 / total)).astype(bf16)
            return carry

        lax.fori_loop(0, 2 * heads, one, 0)

    pltpu.make_async_copy(wt_a, wt_a, sem_a).wait()
    for clip in range(2):
        for s in range(3):
            kind = (s - role + 6) % 3
            lhs = jnp.concatenate(
                [wt_a[t, 8 * s : 8 * s + 8].reshape(A_COLS, 128) for t in range(8)], axis=1
            )
            value = lax.dot_general(lhs, norm_a[clip], nt, preferred_element_type=f32)
            for h in range(A_HEADS):
                put(qkv_a, kind, clip, h, value[h * HEAD : (h + 1) * HEAD])
    attention(qkv_a, att_a, A_HEADS)
    for clip in range(2):
        rows = att_a[clip].reshape(A_COLS, FRAMES)
        mean = lax.dot_general(pool_mat, rows, nt, preferred_element_type=f32).astype(bf16)
        pooled[:, clip * 32 : clip * 32 + 32, :A_COLS] = mean.reshape(ROLES, 32, A_COLS)

    pltpu.make_async_copy(wt_w, wt_w, sem_w).wait()
    for clip in range(2):
        for b in range(4):
            lhs = jnp.concatenate(
                [wt_w[t, 8 * b : 8 * b + 8].reshape(256, 128) for t in range(10)], axis=1
            )
            proj[256 * b : 256 * b + 256] = lax.dot_general(
                lhs, norm_w[clip], nt, preferred_element_type=f32
            )
        for s in range(3):
            kind = (s - role + 6) % 3
            for h in range(W_HEADS):
                start = s * W_COLS + h * HEAD
                parts = []
                while start < s * W_COLS + (h + 1) * HEAD:
                    block, inner = start // 120, start % 120
                    take = min(120 - inner, s * W_COLS + (h + 1) * HEAD - start)
                    parts.append(proj[block * 128 + inner : block * 128 + inner + take])
                    start += take
                value = parts[0] if len(parts) == 1 else jnp.concatenate(parts, axis=0)
                put(qkv_w, kind, clip, h, value)
    attention(qkv_w, att_w, W_HEADS)
    for clip in range(2):
        rows = att_w[clip].reshape(W_COLS, FRAMES)
        mean = lax.dot_general(pool_mat, rows, nt, preferred_element_type=f32).astype(bf16)
        mean = jnp.concatenate([mean, jnp.zeros((POOLED, 64), bf16)], axis=1)
        pooled[:, clip * 32 : clip * 32 + 32, A_COLS:] = mean.reshape(ROLES, 32, 384)
    for k in range(ROLES):
        outs[k][...] = pooled[(role + k) % ROLES]


def attend(info, pieces, norm_a, norm_w):
    vmem = pl.BlockSpec(memory_space=pltpu.VMEM)
    return pl.pallas_call(
        attend_kernel,
        out_shape=[jax.ShapeDtypeStruct((ROWS, OUT_COLS), bf16)] * ROLES,
        in_specs=[pl.BlockSpec(memory_space=pltpu.SMEM)]
        + [pl.BlockSpec(memory_space=pl.ANY)] * 16
        + [vmem, vmem],
        out_specs=[vmem] * ROLES,
        scratch_shapes=[
            pltpu.VMEM((8, 24, 32, 128), bf16),
            pltpu.VMEM((10, 32, 32, 128), bf16),
            pltpu.VMEM((3, 2, A_HEADS, HEAD, FRAMES), bf16),
            pltpu.VMEM((3, 2, W_HEADS, HEAD, FRAMES), bf16),
            pltpu.VMEM((1024, FRAMES), f32),
            pltpu.VMEM((2, A_HEADS, HEAD, FRAMES), bf16),
            pltpu.VMEM((2, W_HEADS, HEAD, FRAMES), bf16),
            pltpu.VMEM((ROLES, ROWS, OUT_COLS), bf16),
            pltpu.SemaphoreType.DMA,
            pltpu.SemaphoreType.DMA,
        ],
        name="attend",
    )(info, *pieces, norm_a, norm_w)


def slope_kernel(info, *refs):
    parts = refs[:4]
    out_a, out_w, mean_a, mean_w, pred_a, pred_w = refs[4:10]
    outs = refs[10:14]
    grouped = refs[14]
    role = info[0]
    row = lax.broadcasted_iota(jnp.int32, (ROWS, 1), 0)
    valid = jnp.where(row < 32, info[4], info[5]) // POOL
    keep = (row % 32 + role * 32) < valid

    def slope_of(mean, out, pred, cols, first):
        width = mean.shape[-1]
        total = mean[...]
        for k in range(ROLES):
            start = pl.multiple_of(((role - k + ROLES) % ROLES) * cols, 64)
            total = total + jnp.dot(
                parts[k][:, first : first + cols],
                out[pl.ds(start, cols), :],
                preferred_element_type=f32,
            )
        target = total.astype(bf16).astype(f32)
        predicted = pred[...]
        pred_sq = jnp.sum(predicted * predicted, axis=-1, keepdims=True) + epsilon_cos
        targ_sq = jnp.sum(target * target, axis=-1, keepdims=True) + epsilon_cos
        pred_norm = jnp.sqrt(pred_sq)
        both = pred_norm * jnp.sqrt(targ_sq)
        cosine = jnp.sum(predicted * target, axis=-1, keepdims=True) / both
        slope = (cosine / (pred_norm * pred_norm)) * predicted - target / both
        slope = slope + (predicted - target) * (1.0 / width)
        return jnp.where(keep, slope, 0.0).astype(bf16)

    slope_a = slope_of(mean_a, out_a, pred_a, A_COLS, 0)
    for g in range(ROLES):
        grouped[g, :, :A_COLS] = slope_a[:, g * A_COLS : (g + 1) * A_COLS]
    slope_w = slope_of(mean_w, out_w, pred_w, W_COLS, A_COLS)
    for g in range(ROLES):
        grouped[g, :, A_COLS:] = jnp.concatenate(
            [slope_w[:, g * W_COLS : (g + 1) * W_COLS], jnp.zeros((ROWS, 64), bf16)], axis=1
        )
    for k in range(ROLES):
        outs[k][...] = grouped[(role + k) % ROLES]


def slopes(info, parts, out_a, out_w, mean_a, mean_w, pred_a, pred_w):
    vmem = pl.BlockSpec(memory_space=pltpu.VMEM)
    return pl.pallas_call(
        slope_kernel,
        out_shape=[jax.ShapeDtypeStruct((ROWS, OUT_COLS), bf16)] * ROLES,
        in_specs=[pl.BlockSpec(memory_space=pltpu.SMEM)] + [vmem] * 10,
        out_specs=[vmem] * ROLES,
        scratch_shapes=[pltpu.VMEM((ROLES, ROWS, OUT_COLS), bf16)],
        name="slopes",
    )(info, *parts, out_a, out_w, mean_a, mean_w, pred_a, pred_w)


def outer_kernel(*refs):
    lat = jnp.concatenate([refs[k][...] for k in range(4)], axis=0)
    slo = jnp.concatenate([refs[4 + k][...] for k in range(4)], axis=0)
    grad = lax.dot_general(lat, slo, (((0,), (0,)), ((), ())), preferred_element_type=f32)
    refs[8][...] = grad.astype(bf16).reshape(32, 16, OUT_COLS)


def outer(lats, slos):
    vmem = pl.BlockSpec(memory_space=pltpu.VMEM)
    return pl.pallas_call(
        outer_kernel,
        out_shape=jax.ShapeDtypeStruct((32, 16, OUT_COLS), bf16),
        in_specs=[vmem] * 8,
        out_specs=vmem,
        name="outer",
    )(*lats, *slos)


def sum_kernel(x, out_a, out_w):
    total = jnp.sum(x[...].astype(f32), axis=0)
    out_a[...] = total[:, :A_COLS].astype(bf16)
    out_w[...] = total[:, A_COLS:].astype(bf16)


def reduce_parts(x):
    vmem = pl.BlockSpec(memory_space=pltpu.VMEM)
    return pl.pallas_call(
        sum_kernel,
        out_shape=[
            jax.ShapeDtypeStruct((16, A_COLS), bf16),
            jax.ShapeDtypeStruct((16, OUT_COLS - A_COLS), bf16),
        ],
        in_specs=[vmem],
        out_specs=[vmem, vmem],
        name="reduce_parts",
    )(x)


def place_kernel(info, *refs):
    pieces = refs[:16]
    out_a, out_w = refs[16:18]
    all_a, all_w, sem_a, sem_w = refs[18:]
    role, z, y, c = info[0], info[1], info[2], info[3]
    for n, piece in enumerate(pieces):
        core = (c + n // 8) % 2
        half = (n % 8) // 4
        k = n % 4
        for step in range(4):
            if half == 0:
                zs, ys = (z - k) % 4, (y - step) % 4
                dst, sem = all_a, sem_a
            else:
                zs, ys = (z - step) % 4, (y - k) % 4
                dst, sem = all_w, sem_w
            pltpu.make_async_copy(piece.at[step], dst.at[zs * 8 + ys * 2 + core], sem).start()
    pltpu.make_async_copy(all_a, all_a, sem_a).wait()
    for g in range(ROLES):
        block = all_a[:, (role - g + ROLES) % ROLES].reshape(STU_D, A_COLS)
        out_a[:, g * A_COLS : (g + 1) * A_COLS] = block.astype(f32)
    pltpu.make_async_copy(all_w, all_w, sem_w).wait()
    blocks = [
        all_w[:, (role - g + ROLES) % ROLES].reshape(STU_D, 384).astype(f32)[:, :W_COLS]
        for g in range(ROLES)
    ]
    out_w[...] = jnp.concatenate(blocks, axis=1)


def place(info, pieces):
    vmem = pl.BlockSpec(memory_space=pltpu.VMEM)
    return pl.pallas_call(
        place_kernel,
        out_shape=[
            jax.ShapeDtypeStruct((STU_D, WAVLM_D), f32),
            jax.ShapeDtypeStruct((STU_D, WHISPER_D), f32),
        ],
        in_specs=[pl.BlockSpec(memory_space=pltpu.SMEM)]
        + [pl.BlockSpec(memory_space=pl.ANY)] * 16,
        out_specs=[vmem, vmem],
        scratch_shapes=[
            pltpu.VMEM((32, ROLES, 16, A_COLS), bf16),
            pltpu.VMEM((32, ROLES, 16, 384), bf16),
            pltpu.SemaphoreType.DMA,
            pltpu.SemaphoreType.DMA,
        ],
        name="place",
    )(info, *pieces)


def gather_both(first, second):
    a1 = [first] + [dp_send(first, k, 0, 0) for k in (1, 3, 2)]
    b1 = [second] + [dp_send(second, 0, k, 0) for k in (1, 3, 2)]
    a1 = jnp.stack([a1[0], a1[1], a1[3], a1[2]])
    b1 = jnp.stack([b1[0], b1[1], b1[3], b1[2]])
    a2 = {0: a1}
    b2 = {0: b1}
    for k in (1, 3, 2):
        a2[k] = dp_send(a1, 0, k, 0)
        b2[k] = dp_send(b1, k, 0, 0)
    mine = [a2[k] for k in range(4)] + [b2[k] for k in range(4)]
    return mine + [dp_send(x, 0, 0, 1) for x in mine]


def per_device(
    wavlm_hidden,
    whisper_hidden,
    wavlm_qkv,
    whisper_qkv,
    wavlm_out,
    whisper_out,
    frames_valid,
    slot_clip,
    latent,
    wavlm_head,
    whisper_head,
):
    role = lax.axis_index("role")
    column = lax.axis_index("dp")
    z, y, c = column // 8, (column // 2) % 4, column % 2
    valid_here = lax.dynamic_slice_in_dim(frames_valid, column * 2, 2)
    info = jnp.concatenate([jnp.stack([role, z, y, c]), valid_here]).astype(jnp.int32)

    chunks = weight_chunks(wavlm_qkv, whisper_qkv)
    row_a = jnp.arange(96)
    seg_a = (96 * (2 * y + c) + row_a) // A_COLS
    seg_w = (120 * (2 * y + c) + 32 * z + jnp.arange(32)) // W_COLS
    segment = jnp.concatenate([seg_a.reshape(3, 32), jnp.broadcast_to(seg_w, (5, 32))])
    source = (role + 4 * ((segment - role + 6) % 3)) // 3
    source = source[None, :, :, None]
    share = jnp.zeros(chunks.shape[1:], bf16)
    for k in range(4):
        chunk = lax.dynamic_index_in_dim(chunks, (z + k) % 4, 0, keepdims=False)
        if k:
            chunk = dp_send(chunk, k, 0, 0)
        share = jnp.where(source == (z - k + 4) % 4, chunk, share)
    pieces = gather_both(share[0], share[1])

    norm_a = layer_norm(wavlm_hidden)
    norm_w = layer_norm(whisper_hidden)

    quarter = lax.dynamic_slice_in_dim(latent[:, 0], role * 32, 32, 1)
    lat1 = jnp.stack([quarter] + [dp_send(quarter, 0, k, 0) for k in (1, 2, 3)])
    lat2 = jnp.concatenate([lat1] + [dp_send(lat1, k, 0, 0) for k in (1, 2, 3)])
    lat2 = lat2.reshape(32, 32, STU_D)

    def pick(clip):
        slot = jnp.sum(jnp.where(slot_clip == clip, jnp.arange(CLIPS), 0))
        h, j = slot // 32, slot % 32
        dz, dy = (z - j // 8 + 4) % 4, (y - (j // 2) % 4 + 4) % 4
        rows = lax.dynamic_index_in_dim(lat2, dz * 8 + dy * 2 + h, 0, keepdims=False)
        return jnp.where(j % 2 == c, rows, jnp.zeros_like(rows)), j % 2 == c

    own = [pick(column * 2 + i) for i in range(2)]
    other = [pick((column + 1 - 2 * c) * 2 + i) for i in range(2)]
    passed = dp_send(jnp.concatenate([rows for rows, _ in other]), 0, 0, 1)
    lat = jnp.concatenate(
        [jnp.where(hit, rows, passed[i * 32 : i * 32 + 32]) for i, (rows, hit) in enumerate(own)]
    )
    lats = [lat] + [role_send(lat, k) for k in (1, 2, 3)]
    pred_a = jnp.dot(lat, wavlm_head, preferred_element_type=f32)
    pred_w = jnp.dot(lat, whisper_head, preferred_element_type=f32)

    def frame_mean(hidden):
        rows = lax.dynamic_slice_in_dim(hidden, role * 128, 128, 1).astype(f32)
        return jnp.mean(rows.reshape(2, 32, POOL, hidden.shape[-1]), axis=2).reshape(ROWS, -1)

    mean_a = frame_mean(wavlm_hidden)
    mean_w = frame_mean(whisper_hidden)

    pooled = attend(info, pieces, norm_a, norm_w)
    parts = [pooled[0]] + [role_send(pooled[k], k) for k in (1, 2, 3)]
    sloped = slopes(info, parts, wavlm_out, whisper_out, mean_a, mean_w, pred_a, pred_w)
    slos = [sloped[0]] + [role_send(sloped[k], k) for k in (1, 2, 3)]
    grads = outer(lats, slos)
    arrived = lax.all_to_all(grads, "dp", split_axis=0, concat_axis=0, tiled=True)
    mine_a, mine_w = reduce_parts(arrived)

    both = jnp.concatenate([mine_a, mine_w], axis=1)
    lined = jnp.stack([both] + [role_send(both, k) for k in (1, 2, 3)])
    line_a, line_w = lined[:, :, :A_COLS], lined[:, :, A_COLS:]
    got = gather_both(line_w, line_a)
    w_first, a_first = got[0:4], got[4:8]
    w_other, a_other = got[8:12], got[12:16]
    return tuple(place(info, a_first + w_first + a_other + w_other))


def solution(mesh):
    in_specs = (
        P("dp", None, None),
        P("dp", None, None),
        P(None, "dp"),
        P(None, "dp"),
        P(),
        P(),
        P(),
        P(),
        P(None, "dp", None, None),
        P(),
        P(),
    )
    out_specs = (P(), P())
    return jax.shard_map(
        per_device, mesh=mesh, in_specs=in_specs, out_specs=out_specs, check_vma=False
    )
```

```python
import jax
import jax.numpy as jnp
from jax import lax
from jax.experimental import pallas as pl
from jax.experimental.pallas import tpu as pltpu
from jax.sharding import PartitionSpec as P

WAVLM_D = 1024
WHISPER_D = 1280
STU_D = 512
HEAD = 64
FRAMES = 512
POOL = 4
POOLED = 128
CLIPS = 64
ROLES = 4
A_HEADS = WAVLM_D // HEAD // ROLES
W_HEADS = WHISPER_D // HEAD // ROLES
A_COLS = A_HEADS * HEAD
W_COLS = W_HEADS * HEAD
OUT_COLS = 640
ROWS = 64

epsilon_norm = 1e-05
epsilon_cos = 1e-06


bf16 = jnp.bfloat16
f32 = jnp.float32


def dp_send(x, dz, dy, dc):
    pairs = []
    for i in range(32):
        z, y, c = i // 8, (i // 2) % 4, i % 2
        target = ((z + dz) % 4) * 8 + ((y + dy) % 4) * 2 + (c + dc) % 2
        pairs.append((i, target))
    return lax.ppermute(x, "dp", pairs)


def role_send(x, k):
    return lax.ppermute(x, "role", [(i, (i + k) % ROLES) for i in range(ROLES)])


def layer_norm(hidden):
    hidden_f = hidden.astype(f32)
    centred = hidden_f - jnp.mean(hidden_f, axis=-1, keepdims=True)
    variance = jnp.mean(centred * centred, axis=-1, keepdims=True)
    return (centred * lax.rsqrt(variance + epsilon_norm)).astype(bf16)


def chunk_kernel(info, qkv_a, qkv_w, *refs):
    outs, chunks = refs[:4], refs[4]
    wa = qkv_a[...].T
    ww = jnp.concatenate([qkv_w[...].T, jnp.zeros((8, WHISPER_D), bf16)], axis=0)
    for part in range(4):
        for t in range(2):
            lane = (2 * part + t) * 128
            chunks[part, 3 * t : 3 * t + 3] = wa[:, lane : lane + 128].reshape(3, 32, 128)
        for t in range(10):
            chunks[part, 6 + t] = ww[32 * part : 32 * part + 32, 128 * t : 128 * t + 128]
    for k in range(4):
        outs[k][...] = chunks[(info[1] + k) % 4]


def weight_chunks(info, wavlm_qkv, whisper_qkv):
    vmem = pl.BlockSpec(memory_space=pltpu.VMEM)
    return pl.pallas_call(
        chunk_kernel,
        out_shape=[jax.ShapeDtypeStruct((16, 32, 128), bf16)] * 4,
        in_specs=[pl.BlockSpec(memory_space=pltpu.SMEM), vmem, vmem],
        out_specs=[vmem] * 4,
        scratch_shapes=[pltpu.VMEM((4, 16, 32, 128), bf16)],
        name="weight_chunks",
    )(info, wavlm_qkv, whisper_qkv)


def attend_kernel(info, *refs):
    pieces = refs[:2]
    norm_a, norm_w = refs[2:4]
    outs = refs[4:8]
    wt_a, wt_w, qkv_a, qkv_w, proj, att_a, att_w, pooled, sem_a, sem_w = refs[8:]
    role, c = info[0], info[3]

    def fetch(p, carry):
        zs = p // 4
        for n, piece in enumerate(pieces):
            block = (p % 4) * 2 + (c + n) % 2
            for t in range(2):
                pltpu.make_async_copy(
                    piece.at[p, pl.ds(3 * t, 3)], wt_a.at[2 * zs + t, pl.ds(3 * block, 3)], sem_a
                ).start()
            pltpu.make_async_copy(
                piece.at[p, pl.ds(6, 10)], wt_w.at[:, block * 4 + zs], sem_w
            ).start()
        return carry

    lax.fori_loop(0, 16, fetch, 0)
    ones_row = jnp.where(
        lax.broadcasted_iota(jnp.int32, (16, FRAMES), 0) == 0, 1.0, 0.0
    ).astype(bf16)
    pool_mat = jnp.where(
        lax.broadcasted_iota(jnp.int32, (POOLED, FRAMES), 1) // POOL
        == lax.broadcasted_iota(jnp.int32, (POOLED, FRAMES), 0),
        1.0 / POOL,
        0.0,
    ).astype(bf16)
    nt = (((1,), (1,)), ((), ()))
    tn = (((0,), (0,)), ((), ()))

    def put(qkv, kind, clip, head, value):
        scale = jnp.where(kind == 0, HEAD ** (-0.5), 1.0).astype(f32)
        qkv[kind, clip, head] = (value.astype(bf16).astype(f32) * scale).astype(bf16)

    def attention(qkv, att, heads):
        def one(i, carry):
            clip = i // heads
            head = i % heads
            valid = info[4 + clip]
            query = qkv[0, clip, head]
            key = qkv[1, clip, head]
            value = qkv[2, clip, head]
            rows = lax.broadcasted_iota(jnp.int32, (16, FRAMES), 0)
            frame = lax.broadcasted_iota(jnp.int32, (16, FRAMES), 1)
            bias = jnp.where((rows == 0) & (frame >= valid), -1e30, 0.0).astype(bf16)
            key_x = jnp.concatenate([key, bias], axis=0)
            query_x = jnp.concatenate([query, ones_row], axis=0)
            value_x = jnp.concatenate([value, ones_row], axis=0)
            scores = lax.dot_general(key_x, query_x, tn, preferred_element_type=f32)
            top = jnp.max(scores, axis=0, keepdims=True)
            raised = jnp.exp(scores - top).astype(bf16)
            mixed = jnp.dot(value_x, raised, preferred_element_type=f32)
            total = mixed[HEAD : HEAD + 1]
            att[clip, head] = (mixed[:HEAD] * (1.0 / total)).astype(bf16)
            return carry

        lax.fori_loop(0, 2 * heads, one, 0)

    pltpu.make_async_copy(wt_a, wt_a, sem_a).wait()
    for clip in range(2):
        for s in range(3):
            kind = (s - role + 6) % 3
            lhs = jnp.concatenate(
                [wt_a[t, 8 * s : 8 * s + 8].reshape(A_COLS, 128) for t in range(8)], axis=1
            )
            value = lax.dot_general(lhs, norm_a[clip], nt, preferred_element_type=f32)
            for h in range(A_HEADS):
                put(qkv_a, kind, clip, h, value[h * HEAD : (h + 1) * HEAD])
    attention(qkv_a, att_a, A_HEADS)
    for clip in range(2):
        rows = att_a[clip].reshape(A_COLS, FRAMES)
        mean = lax.dot_general(pool_mat, rows, nt, preferred_element_type=f32).astype(bf16)
        pooled[:, clip * 32 : clip * 32 + 32, :A_COLS] = mean.reshape(ROLES, 32, A_COLS)

    pltpu.make_async_copy(wt_w, wt_w, sem_w).wait()
    for clip in range(2):
        for b in range(4):
            lhs = jnp.concatenate(
                [wt_w[t, 8 * b : 8 * b + 8].reshape(256, 128) for t in range(10)], axis=1
            )
            proj[256 * b : 256 * b + 256] = lax.dot_general(
                lhs, norm_w[clip], nt, preferred_element_type=f32
            )
        for s in range(3):
            kind = (s - role + 6) % 3
            for h in range(W_HEADS):
                start = s * W_COLS + h * HEAD
                parts = []
                while start < s * W_COLS + (h + 1) * HEAD:
                    block, inner = start // 120, start % 120
                    take = min(120 - inner, s * W_COLS + (h + 1) * HEAD - start)
                    parts.append(proj[block * 128 + inner : block * 128 + inner + take])
                    start += take
                value = parts[0] if len(parts) == 1 else jnp.concatenate(parts, axis=0)
                put(qkv_w, kind, clip, h, value)
    attention(qkv_w, att_w, W_HEADS)
    for clip in range(2):
        rows = att_w[clip].reshape(W_COLS, FRAMES)
        mean = lax.dot_general(pool_mat, rows, nt, preferred_element_type=f32).astype(bf16)
        mean = jnp.concatenate([mean, jnp.zeros((POOLED, 64), bf16)], axis=1)
        pooled[:, clip * 32 : clip * 32 + 32, A_COLS:] = mean.reshape(ROLES, 32, 384)
    for k in range(ROLES):
        outs[k][...] = pooled[(role + k) % ROLES]


def attend(info, pieces, norm_a, norm_w):
    vmem = pl.BlockSpec(memory_space=pltpu.VMEM)
    return pl.pallas_call(
        attend_kernel,
        out_shape=[jax.ShapeDtypeStruct((ROWS, OUT_COLS), bf16)] * ROLES,
        in_specs=[pl.BlockSpec(memory_space=pltpu.SMEM)]
        + [pl.BlockSpec(memory_space=pl.ANY)] * 2
        + [vmem, vmem],
        out_specs=[vmem] * ROLES,
        scratch_shapes=[
            pltpu.VMEM((8, 24, 32, 128), bf16),
            pltpu.VMEM((10, 32, 32, 128), bf16),
            pltpu.VMEM((3, 2, A_HEADS, HEAD, FRAMES), bf16),
            pltpu.VMEM((3, 2, W_HEADS, HEAD, FRAMES), bf16),
            pltpu.VMEM((1024, FRAMES), f32),
            pltpu.VMEM((2, A_HEADS, HEAD, FRAMES), bf16),
            pltpu.VMEM((2, W_HEADS, HEAD, FRAMES), bf16),
            pltpu.VMEM((ROLES, ROWS, OUT_COLS), bf16),
            pltpu.SemaphoreType.DMA,
            pltpu.SemaphoreType.DMA,
        ],
        name="attend",
    )(info, *pieces, norm_a, norm_w)


def slope_kernel(info, *refs):
    parts = refs[:4]
    out_a, out_w, mean_a, mean_w, pred_a, pred_w = refs[4:10]
    outs = refs[10:14]
    grouped = refs[14]
    role = info[0]
    row = lax.broadcasted_iota(jnp.int32, (ROWS, 1), 0)
    valid = jnp.where(row < 32, info[4], info[5]) // POOL
    keep = (row % 32 + role * 32) < valid

    def slope_of(mean, out, pred, cols, first):
        width = mean.shape[-1]
        total = mean[...]
        for k in range(ROLES):
            start = pl.multiple_of(((role - k + ROLES) % ROLES) * cols, 64)
            total = total + jnp.dot(
                parts[k][:, first : first + cols],
                out[pl.ds(start, cols), :],
                preferred_element_type=f32,
            )
        target = total.astype(bf16).astype(f32)
        predicted = pred[...]
        pred_sq = jnp.sum(predicted * predicted, axis=-1, keepdims=True) + epsilon_cos
        targ_sq = jnp.sum(target * target, axis=-1, keepdims=True) + epsilon_cos
        pred_norm = jnp.sqrt(pred_sq)
        both = pred_norm * jnp.sqrt(targ_sq)
        cosine = jnp.sum(predicted * target, axis=-1, keepdims=True) / both
        slope = (cosine / (pred_norm * pred_norm)) * predicted - target / both
        slope = slope + (predicted - target) * (1.0 / width)
        return jnp.where(keep, slope, 0.0).astype(bf16)

    slope_a = slope_of(mean_a, out_a, pred_a, A_COLS, 0)
    for g in range(ROLES):
        grouped[g, :, :A_COLS] = slope_a[:, g * A_COLS : (g + 1) * A_COLS]
    slope_w = slope_of(mean_w, out_w, pred_w, W_COLS, A_COLS)
    for g in range(ROLES):
        grouped[g, :, A_COLS:] = jnp.concatenate(
            [slope_w[:, g * W_COLS : (g + 1) * W_COLS], jnp.zeros((ROWS, 64), bf16)], axis=1
        )
    for k in range(ROLES):
        outs[k][...] = grouped[(role + k) % ROLES]


def slopes(info, parts, out_a, out_w, mean_a, mean_w, pred_a, pred_w):
    vmem = pl.BlockSpec(memory_space=pltpu.VMEM)
    return pl.pallas_call(
        slope_kernel,
        out_shape=[jax.ShapeDtypeStruct((ROWS, OUT_COLS), bf16)] * ROLES,
        in_specs=[pl.BlockSpec(memory_space=pltpu.SMEM)] + [vmem] * 10,
        out_specs=[vmem] * ROLES,
        scratch_shapes=[pltpu.VMEM((ROLES, ROWS, OUT_COLS), bf16)],
        name="slopes",
    )(info, *parts, out_a, out_w, mean_a, mean_w, pred_a, pred_w)


def outer_kernel(info, *refs):
    lat = jnp.concatenate([refs[k][...] for k in range(4)], axis=0)
    slo = jnp.concatenate([refs[4 + k][...] for k in range(4)], axis=0)
    keep, send, both = refs[8:]
    grad = lax.dot_general(lat, slo, (((0,), (0,)), ((), ())), preferred_element_type=f32)
    both[...] = grad.reshape(2, 16, 16, OUT_COLS)
    keep[...] = both[info[3]]
    send[...] = both[1 - info[3]]


def outer(info, lats, slos):
    vmem = pl.BlockSpec(memory_space=pltpu.VMEM)
    return pl.pallas_call(
        outer_kernel,
        out_shape=[jax.ShapeDtypeStruct((16, 16, OUT_COLS), f32)] * 2,
        in_specs=[pl.BlockSpec(memory_space=pltpu.SMEM)] + [vmem] * 8,
        out_specs=[vmem] * 2,
        scratch_shapes=[pltpu.VMEM((2, 16, 16, OUT_COLS), f32)],
        name="outer",
    )(info, *lats, *slos)


def sum_kernel(x, out):
    total = jnp.sum(x[...], axis=0).astype(bf16)
    out[...] = jnp.broadcast_to(total[None], out.shape)


def reduce_parts(x):
    vmem = pl.BlockSpec(memory_space=pltpu.VMEM)
    return pl.pallas_call(
        sum_kernel,
        out_shape=jax.ShapeDtypeStruct((64, 16, OUT_COLS), bf16),
        in_specs=[vmem],
        out_specs=vmem,
        name="reduce_parts",
    )(x)


def place_kernel(info, own, other, out_a, out_w):
    for n, piece in enumerate((own, other)):
        core = (info[3] + n) % 2
        blocks = []
        for g in range(ROLES):
            block = piece[g].reshape(64, OUT_COLS).astype(f32)
            out_a[core, :, g * A_COLS : (g + 1) * A_COLS] = block[:, :A_COLS]
            blocks.append(block[:, A_COLS : A_COLS + W_COLS])
        out_w[core] = jnp.concatenate(blocks, axis=1)


def place(info, own, other):
    spec = pl.BlockSpec((ROLES, 4, 16, OUT_COLS), lambda i: (0, i, 0, 0))
    return pl.pallas_call(
        place_kernel,
        grid=(4,),
        out_shape=[
            jax.ShapeDtypeStruct((2, 256, WAVLM_D), f32),
            jax.ShapeDtypeStruct((2, 256, WHISPER_D), f32),
        ],
        in_specs=[pl.BlockSpec(memory_space=pltpu.SMEM), spec, spec],
        out_specs=[
            pl.BlockSpec((2, 64, WAVLM_D), lambda i: (0, i, 0)),
            pl.BlockSpec((2, 64, WHISPER_D), lambda i: (0, i, 0)),
        ],
        name="place",
    )(info, own, other)


PLANE = [[z * 8 + y * 2 + c for z in range(4) for y in range(4)] for c in range(2)]
SLICE = [[r * 32 + i for r in range(ROLES) for i in plane] for plane in PLANE]


def per_device(
    wavlm_hidden,
    whisper_hidden,
    wavlm_qkv,
    whisper_qkv,
    wavlm_out,
    whisper_out,
    frames_valid,
    slot_clip,
    latent,
    wavlm_head,
    whisper_head,
):
    role = lax.axis_index("role")
    column = lax.axis_index("dp")
    z, y, c = column // 8, (column // 2) % 4, column % 2
    valid_here = lax.dynamic_slice_in_dim(frames_valid, column * 2, 2)
    info = jnp.concatenate([jnp.stack([role, z, y, c]), valid_here]).astype(jnp.int32)

    chunks = weight_chunks(info, wavlm_qkv, whisper_qkv)
    seg_a = (96 * (2 * y + c) + jnp.arange(96)) // A_COLS
    seg_w = (120 * (2 * y + c) + 32 * z + jnp.arange(32)) // W_COLS
    segment = jnp.concatenate(
        [jnp.tile(seg_a.reshape(3, 32), (2, 1)), jnp.broadcast_to(seg_w, (10, 32))]
    )
    source = ((role + 4 * ((segment - role + 6) % 3)) // 3)[:, :, None]
    share = jnp.zeros(chunks[0].shape, bf16)
    for k in range(4):
        chunk = dp_send(chunks[k], k, 0, 0) if k else chunks[0]
        share = jnp.where(source == (z - k + 4) % 4, chunk, share)
    copies = jnp.broadcast_to(share[None], (16,) + share.shape)
    copies, latent, wavlm_hidden, whisper_hidden = lax.optimization_barrier(
        (copies, latent, wavlm_hidden, whisper_hidden)
    )
    own_weights = lax.all_to_all(
        copies, "dp", split_axis=0, concat_axis=0, tiled=True, axis_index_groups=PLANE
    )
    other_weights = dp_send(own_weights, 0, 0, 1)

    norm_a = layer_norm(wavlm_hidden)
    norm_w = layer_norm(whisper_hidden)

    quarter = lax.dynamic_slice_in_dim(latent[:, 0], role * 32, 32, 1)
    lat1 = jnp.stack([quarter] + [dp_send(quarter, 0, k, 0) for k in (1, 2, 3)])
    lat2 = jnp.concatenate([lat1] + [dp_send(lat1, k, 0, 0) for k in (1, 2, 3)])
    lat2 = lat2.reshape(32, 32, STU_D)

    def pick(clip):
        slot = jnp.sum(jnp.where(slot_clip == clip, jnp.arange(CLIPS), 0))
        h, j = slot // 32, slot % 32
        dz, dy = (z - j // 8 + 4) % 4, (y - (j // 2) % 4 + 4) % 4
        rows = lax.dynamic_index_in_dim(lat2, dz * 8 + dy * 2 + h, 0, keepdims=False)
        return jnp.where(j % 2 == c, rows, jnp.zeros_like(rows)), j % 2 == c

    own = [pick(column * 2 + i) for i in range(2)]
    other = [pick((column + 1 - 2 * c) * 2 + i) for i in range(2)]
    passed = dp_send(jnp.concatenate([rows for rows, _ in other]), 0, 0, 1)
    lat = jnp.concatenate(
        [jnp.where(hit, rows, passed[i * 32 : i * 32 + 32]) for i, (rows, hit) in enumerate(own)]
    )
    lats = [lat] + [role_send(lat, k) for k in (1, 2, 3)]
    pred_a = jnp.dot(lat, wavlm_head, preferred_element_type=f32)
    pred_w = jnp.dot(lat, whisper_head, preferred_element_type=f32)

    def frame_mean(hidden):
        rows = lax.dynamic_slice_in_dim(hidden, role * 128, 128, 1).astype(f32)
        return jnp.mean(rows.reshape(2, 32, POOL, hidden.shape[-1]), axis=2).reshape(ROWS, -1)

    mean_a = frame_mean(wavlm_hidden)
    mean_w = frame_mean(whisper_hidden)

    ready = lax.optimization_barrier((other_weights, *lats, pred_a, pred_w, mean_a, mean_w))
    other_weights, lats, (pred_a, pred_w, mean_a, mean_w) = ready[0], ready[1:5], ready[5:]
    pooled = attend(info, (own_weights, other_weights), norm_a, norm_w)
    parts = [pooled[0]] + [role_send(pooled[k], k) for k in (1, 2, 3)]
    sloped = slopes(info, parts, wavlm_out, whisper_out, mean_a, mean_w, pred_a, pred_w)
    slos = [sloped[0]] + [role_send(sloped[k], k) for k in (1, 2, 3)]
    keep, send = outer(info, lats, slos)
    halves = keep + dp_send(send, 0, 0, 1)
    arrived = lax.all_to_all(
        halves, "dp", split_axis=0, concat_axis=0, tiled=True, axis_index_groups=PLANE
    )
    summed = lax.all_to_all(
        reduce_parts(arrived),
        ("role", "dp"),
        split_axis=0,
        concat_axis=0,
        tiled=True,
        axis_index_groups=SLICE,
    ).reshape(ROLES, 16, 16, OUT_COLS)
    grad_a, grad_w = place(info, summed, dp_send(summed, 0, 0, 1))
    return grad_a.reshape(STU_D, WAVLM_D), grad_w.reshape(STU_D, WHISPER_D)


def solution(mesh):
    in_specs = (
        P("dp", None, None),
        P("dp", None, None),
        P(None, "dp"),
        P(None, "dp"),
        P(),
        P(),
        P(),
        P(),
        P(None, "dp", None, None),
        P(),
        P(),
    )
    out_specs = (P(), P())
    return jax.shard_map(
        per_device, mesh=mesh, in_specs=in_specs, out_specs=out_specs, check_vma=False
    )
```

```python
import jax
import jax.numpy as jnp
from jax import lax
from jax.experimental import pallas as pl
from jax.experimental.pallas import tpu as pltpu
from jax.sharding import PartitionSpec as P


WAVLM_D = 1024
WHISPER_D = 1280
STU_D = 512
HEAD = 64
FRAMES = 512
POOL = 4
POOLED = 128
CLIPS = 64
ROLES = 4
A_HEADS = WAVLM_D // HEAD // ROLES
W_HEADS = WHISPER_D // HEAD // ROLES
A_COLS = A_HEADS * HEAD
W_COLS = W_HEADS * HEAD
OUT_COLS = 640
ROWS = 64

epsilon_norm = 1e-05
epsilon_cos = 1e-06


bf16 = jnp.bfloat16
f32 = jnp.float32


def dp_send(x, dz, dy, dc):
    pairs = []
    for i in range(32):
        z, y, c = i // 8, (i // 2) % 4, i % 2
        target = ((z + dz) % 4) * 8 + ((y + dy) % 4) * 2 + (c + dc) % 2
        pairs.append((i, target))
    return lax.ppermute(x, "dp", pairs)


def role_send(x, k):
    return lax.ppermute(x, "role", [(i, (i + k) % ROLES) for i in range(ROLES)])


def place_of(column):
    return column // 8, (column // 2) % 4, column % 2


def norm_kernel(wavlm, whisper, norm_a, norm_w, mean_a, mean_w):
    pool_mat = jnp.where(
        lax.broadcasted_iota(jnp.int32, (32, 128), 1) // POOL
        == lax.broadcasted_iota(jnp.int32, (32, 128), 0),
        1.0 / POOL,
        0.0,
    ).astype(bf16)
    for hidden, norm, mean in ((wavlm, norm_a, mean_a), (whisper, norm_w, mean_w)):
        rows = hidden[0].astype(f32)
        centred = rows - jnp.mean(rows, axis=-1, keepdims=True)
        variance = jnp.mean(centred * centred, axis=-1, keepdims=True)
        norm[0] = (centred * lax.rsqrt(variance + epsilon_norm)).astype(bf16)

        @pl.when(pl.program_id(1) == lax.axis_index("role"))
        def _():
            mean[...] = jnp.dot(pool_mat, hidden[0], preferred_element_type=f32)


def norms(wavlm, whisper):
    rows = lambda width: pl.BlockSpec((1, 128, width), lambda i, j: (i, j, 0))
    mean = lambda width: pl.BlockSpec((32, width), lambda i, j: (i, 0))
    return pl.pallas_call(
        norm_kernel,
        grid=(2, 4),
        out_shape=[
            jax.ShapeDtypeStruct(wavlm.shape, bf16),
            jax.ShapeDtypeStruct(whisper.shape, bf16),
            jax.ShapeDtypeStruct((ROWS, WAVLM_D), f32),
            jax.ShapeDtypeStruct((ROWS, WHISPER_D), f32),
        ],
        in_specs=[rows(WAVLM_D), rows(WHISPER_D)],
        out_specs=[rows(WAVLM_D), rows(WHISPER_D), mean(WAVLM_D), mean(WHISPER_D)],
        cost_estimate=pl.CostEstimate(
            flops=60_000_000, bytes_accessed=24_000_000, transcendentals=4096
        ),
        name="norms",
    )(wavlm, whisper)


def chunk_kernel(qkv_a, qkv_w, *refs):
    outs, chunks = refs[:4], refs[4]
    z = place_of(lax.axis_index("dp"))[0]
    for part in range(4):
        for t in range(2):
            lane = (2 * part + t) * 128
            chunks[part, 3 * t : 3 * t + 3] = qkv_a[:, lane : lane + 128].reshape(3, 32, 128)
        for t in range(10):
            if part < 3:
                chunks[part, 6 + t] = qkv_w[32 * part : 32 * part + 32, 128 * t : 128 * t + 128]
            else:
                chunks[part, 6 + t] = jnp.concatenate(
                    [qkv_w[96:120, 128 * t : 128 * t + 128], jnp.zeros((8, 128), bf16)], axis=0
                )
    for k in range(4):
        outs[k][...] = chunks[(z + k) % 4]


def weight_chunks(qkv_a, qkv_w):
    vmem = pl.BlockSpec(memory_space=pltpu.VMEM)
    return pl.pallas_call(
        chunk_kernel,
        out_shape=[jax.ShapeDtypeStruct((16, 32, 128), bf16)] * 4,
        in_specs=[vmem, vmem],
        out_specs=[vmem] * 4,
        scratch_shapes=[pltpu.VMEM((4, 16, 32, 128), bf16)],
        name="weight_chunks",
    )(qkv_a, qkv_w)


def share_kernel(*refs):
    parts, out = refs[:4], refs[4]
    role = lax.axis_index("role")
    z, y, c = place_of(lax.axis_index("dp"))
    row = lax.broadcasted_iota(jnp.int32, (32, 128), 0)
    sources = [(role + 4 * ((s - role + 6) % 3)) // 3 for s in range(3)]
    for g in range(4):
        if g < 3:
            column, width = 96 * (2 * y + c) + 32 * g + row, A_COLS
        else:
            column, width = 120 * (2 * y + c) + 32 * z + row, W_COLS
        source = jnp.where(
            column < width, sources[0], jnp.where(column < 2 * width, sources[1], sources[2])
        )
        groups = (g, g + 3) if g < 3 else range(6, 16)
        for group in groups:
            value = parts[0][group].astype(f32)
            for k in range(1, 4):
                value = jnp.where(
                    source == (z - k + 4) % 4, parts[k][group].astype(f32), value
                )
            value = value.astype(bf16)
            out[:, group] = jnp.broadcast_to(value[None], (16, 32, 128))


def shares(parts):
    vmem = pl.BlockSpec(memory_space=pltpu.VMEM)
    return pl.pallas_call(
        share_kernel,
        out_shape=jax.ShapeDtypeStruct((16, 16, 32, 128), bf16),
        in_specs=[vmem] * 4,
        out_specs=vmem,
        cost_estimate=pl.CostEstimate(flops=0, bytes_accessed=5_000_000, transcendentals=0),
        name="shares",
    )(*parts)


def spread_kernel(latent, out):
    out[...] = jnp.broadcast_to(latent[:, 0][None], (16, 2, 32, STU_D))


def spread(latent):
    return pl.pallas_call(
        spread_kernel,
        grid=(1,),
        out_shape=jax.ShapeDtypeStruct((16, 2, 32, STU_D), bf16),
        in_specs=[
            pl.BlockSpec((2, 1, 32, STU_D), lambda i: (0, 0, lax.axis_index("role"), 0))
        ],
        out_specs=pl.BlockSpec((16, 2, 32, STU_D), lambda i: (0, 0, 0, 0)),
        name="spread",
    )(latent)


def pick_kernel(slot_clip, rows, own, other, slots):
    column = lax.axis_index("dp")
    c = column % 2
    base = (column // 2) * 4

    def find(s, carry):
        local = slot_clip[s] - base

        @pl.when((local >= 0) & (local < 4))
        def _():
            slots[jnp.clip(local, 0, 3)] = s

        return carry

    lax.fori_loop(0, CLIPS, find, 0)
    for out, owner in ((own, c), (other, 1 - c)):
        for i in range(2):
            slot = slots[2 * owner + i]
            h, j = slot // 32, slot % 32
            value = rows[j // 2, h]
            hit = (j % 2 == c).astype(f32)
            out[i * 32 : i * 32 + 32] = jnp.where(hit > 0, value.astype(f32), 0.0).astype(bf16)


def pick(slot_clip, rows):
    vmem = pl.BlockSpec(memory_space=pltpu.VMEM)
    return pl.pallas_call(
        pick_kernel,
        out_shape=[jax.ShapeDtypeStruct((ROWS, STU_D), bf16)] * 2,
        in_specs=[pl.BlockSpec(memory_space=pltpu.SMEM), vmem],
        out_specs=[vmem] * 2,
        scratch_shapes=[pltpu.SMEM((4,), jnp.int32)],
        cost_estimate=pl.CostEstimate(flops=0, bytes_accessed=6_000_000, transcendentals=0),
        name="pick",
    )(slot_clip, rows)


def attend_kernel(frames_valid, *refs):
    pieces = refs[:2]
    norm_a, norm_w = refs[2:4]
    outs = refs[4:8]
    wt_a, wt_w, qkv_a, qkv_w, proj, att_a, att_w, pooled, sem_a, sem_w = refs[8:]
    role = lax.axis_index("role")
    column = lax.axis_index("dp")
    c = column % 2

    def fetch(p, carry):
        zs = p // 4
        for n, piece in enumerate(pieces):
            block = (p % 4) * 2 + (c + n) % 2
            for t in range(2):
                pltpu.make_async_copy(
                    piece.at[p, pl.ds(3 * t, 3)], wt_a.at[2 * zs + t, pl.ds(3 * block, 3)], sem_a
                ).start()
            pltpu.make_async_copy(
                piece.at[p, pl.ds(6, 10)], wt_w.at[:, block * 4 + zs], sem_w
            ).start()
        return carry

    lax.fori_loop(0, 16, fetch, 0)
    ones_row = jnp.where(
        lax.broadcasted_iota(jnp.int32, (16, FRAMES), 0) == 0, 1.0, 0.0
    ).astype(bf16)
    pool_mat = jnp.where(
        lax.broadcasted_iota(jnp.int32, (POOLED, FRAMES), 1) // POOL
        == lax.broadcasted_iota(jnp.int32, (POOLED, FRAMES), 0),
        1.0 / POOL,
        0.0,
    ).astype(bf16)
    nt = (((1,), (1,)), ((), ()))
    tn = (((0,), (0,)), ((), ()))

    def put(qkv, kind, clip, head, value):
        scale = jnp.where(kind == 0, HEAD ** (-0.5), 1.0).astype(f32)
        qkv[kind, clip, head] = (value.astype(bf16).astype(f32) * scale).astype(bf16)

    def attention(qkv, att, heads):
        def one(i, carry):
            clip = i // heads
            head = i % heads
            valid = frames_valid[column * 2 + clip]
            query = qkv[0, clip, head]
            key = qkv[1, clip, head]
            value = qkv[2, clip, head]
            rows = lax.broadcasted_iota(jnp.int32, (16, FRAMES), 0)
            frame = lax.broadcasted_iota(jnp.int32, (16, FRAMES), 1)
            bias = jnp.where((rows == 0) & (frame >= valid), -1e30, 0.0).astype(bf16)
            key_x = jnp.concatenate([key, bias], axis=0)
            query_x = jnp.concatenate([query, ones_row], axis=0)
            value_x = jnp.concatenate([value, ones_row], axis=0)
            scores = lax.dot_general(key_x, query_x, tn, preferred_element_type=f32)
            top = jnp.max(scores, axis=0, keepdims=True)
            raised = jnp.exp(scores - top).astype(bf16)
            mixed = jnp.dot(value_x, raised, preferred_element_type=f32)
            total = mixed[HEAD : HEAD + 1]
            att[clip, head] = (mixed[:HEAD] * (1.0 / total)).astype(bf16)
            return carry

        lax.fori_loop(0, 2 * heads, one, 0)

    pltpu.make_async_copy(wt_a, wt_a, sem_a).wait()
    for clip in range(2):
        for s in range(3):
            kind = (s - role + 6) % 3
            lhs = jnp.concatenate(
                [wt_a[t, 8 * s : 8 * s + 8].reshape(A_COLS, 128) for t in range(8)], axis=1
            )
            value = lax.dot_general(lhs, norm_a[clip], nt, preferred_element_type=f32)
            for h in range(A_HEADS):
                put(qkv_a, kind, clip, h, value[h * HEAD : (h + 1) * HEAD])
    attention(qkv_a, att_a, A_HEADS)
    for clip in range(2):
        rows = att_a[clip].reshape(A_COLS, FRAMES)
        mean = lax.dot_general(pool_mat, rows, nt, preferred_element_type=f32).astype(bf16)
        pooled[:, clip * 32 : clip * 32 + 32, :A_COLS] = mean.reshape(ROLES, 32, A_COLS)

    pltpu.make_async_copy(wt_w, wt_w, sem_w).wait()
    for clip in range(2):
        for b in range(4):
            lhs = jnp.concatenate(
                [wt_w[t, 8 * b : 8 * b + 8].reshape(256, 128) for t in range(10)], axis=1
            )
            proj[256 * b : 256 * b + 256] = lax.dot_general(
                lhs, norm_w[clip], nt, preferred_element_type=f32
            )
        for s in range(3):
            kind = (s - role + 6) % 3
            for h in range(W_HEADS):
                start = s * W_COLS + h * HEAD
                parts = []
                while start < s * W_COLS + (h + 1) * HEAD:
                    block, inner = start // 120, start % 120
                    take = min(120 - inner, s * W_COLS + (h + 1) * HEAD - start)
                    parts.append(proj[block * 128 + inner : block * 128 + inner + take])
                    start += take
                value = parts[0] if len(parts) == 1 else jnp.concatenate(parts, axis=0)
                put(qkv_w, kind, clip, h, value)
    attention(qkv_w, att_w, W_HEADS)
    for clip in range(2):
        rows = att_w[clip].reshape(W_COLS, FRAMES)
        mean = lax.dot_general(pool_mat, rows, nt, preferred_element_type=f32).astype(bf16)
        mean = jnp.concatenate([mean, jnp.zeros((POOLED, 64), bf16)], axis=1)
        pooled[:, clip * 32 : clip * 32 + 32, A_COLS:] = mean.reshape(ROLES, 32, 384)
    for k in range(ROLES):
        outs[k][...] = pooled[(role + k) % ROLES]


def attend(frames_valid, pieces, norm_a, norm_w):
    vmem = pl.BlockSpec(memory_space=pltpu.VMEM)
    return pl.pallas_call(
        attend_kernel,
        out_shape=[jax.ShapeDtypeStruct((ROWS, OUT_COLS), bf16)] * ROLES,
        in_specs=[pl.BlockSpec(memory_space=pltpu.SMEM)]
        + [pl.BlockSpec(memory_space=pl.ANY)] * 2
        + [vmem, vmem],
        out_specs=[vmem] * ROLES,
        scratch_shapes=[
            pltpu.VMEM((8, 24, 32, 128), bf16),
            pltpu.VMEM((10, 32, 32, 128), bf16),
            pltpu.VMEM((3, 2, A_HEADS, HEAD, FRAMES), bf16),
            pltpu.VMEM((3, 2, W_HEADS, HEAD, FRAMES), bf16),
            pltpu.VMEM((1024, FRAMES), f32),
            pltpu.VMEM((2, A_HEADS, HEAD, FRAMES), bf16),
            pltpu.VMEM((2, W_HEADS, HEAD, FRAMES), bf16),
            pltpu.VMEM((ROLES, ROWS, OUT_COLS), bf16),
            pltpu.SemaphoreType.DMA,
            pltpu.SemaphoreType.DMA,
        ],
        cost_estimate=pl.CostEstimate(
            flops=8_000_000_000, bytes_accessed=12_000_000, transcendentals=5_000_000
        ),
        name="attend",
    )(frames_valid, *pieces, norm_a, norm_w)


def slope_kernel(frames_valid, *refs):
    parts = refs[:4]
    out_a, out_w, mean_a, mean_w, pred_a, pred_w = refs[4:10]
    outs = refs[10:14]
    grouped = refs[14]
    role = lax.axis_index("role")
    clip = lax.axis_index("dp") * 2
    row = lax.broadcasted_iota(jnp.int32, (ROWS, 1), 0)
    valid = jnp.where(row < 32, frames_valid[clip], frames_valid[clip + 1]) // POOL
    keep = (row % 32 + role * 32) < valid

    def slope_of(mean, out, pred, cols, first):
        width = mean.shape[-1]
        total = mean[...]
        extra = cols - 256
        left, right = [], []
        for k in range(ROLES):
            start = pl.multiple_of(((role - k + ROLES) % ROLES) * cols, 64)
            total = total + jnp.dot(
                parts[k][:, first : first + 256],
                out[pl.ds(start, 256), :],
                preferred_element_type=f32,
            )
            if extra:
                left.append(parts[k][:, first + 256 : first + cols])
                right.append(out[pl.ds(start + 256, extra), :])
        if extra:
            total = total + jnp.dot(
                jnp.concatenate(left, axis=1),
                jnp.concatenate(right, axis=0),
                preferred_element_type=f32,
            )
        target = total.astype(bf16).astype(f32)
        predicted = pred[...]
        pred_sq = jnp.sum(predicted * predicted, axis=-1, keepdims=True) + epsilon_cos
        targ_sq = jnp.sum(target * target, axis=-1, keepdims=True) + epsilon_cos
        pred_norm = jnp.sqrt(pred_sq)
        both = pred_norm * jnp.sqrt(targ_sq)
        cosine = jnp.sum(predicted * target, axis=-1, keepdims=True) / both
        slope = (cosine / (pred_norm * pred_norm)) * predicted - target / both
        slope = slope + (predicted - target) * (1.0 / width)
        return jnp.where(keep, slope, 0.0).astype(bf16)

    slope_a = slope_of(mean_a, out_a, pred_a, A_COLS, 0)
    for g in range(ROLES):
        grouped[g, :, :A_COLS] = slope_a[:, g * A_COLS : (g + 1) * A_COLS]
    slope_w = slope_of(mean_w, out_w, pred_w, W_COLS, A_COLS)
    for g in range(ROLES):
        grouped[g, :, A_COLS:] = jnp.concatenate(
            [slope_w[:, g * W_COLS : (g + 1) * W_COLS], jnp.zeros((ROWS, 64), bf16)], axis=1
        )
    for k in range(ROLES):
        outs[k][...] = grouped[(role + k) % ROLES]


def slopes(frames_valid, parts, out_a, out_w, mean_a, mean_w, pred_a, pred_w):
    vmem = pl.BlockSpec(memory_space=pltpu.VMEM)
    return pl.pallas_call(
        slope_kernel,
        out_shape=[jax.ShapeDtypeStruct((ROWS, OUT_COLS), bf16)] * ROLES,
        in_specs=[pl.BlockSpec(memory_space=pltpu.SMEM)] + [vmem] * 10,
        out_specs=[vmem] * ROLES,
        scratch_shapes=[pltpu.VMEM((ROLES, ROWS, OUT_COLS), bf16)],
        name="slopes",
    )(frames_valid, *parts, out_a, out_w, mean_a, mean_w, pred_a, pred_w)


def half_gradient(refs, half):
    start = pl.multiple_of(half * 256, 256)
    lat = jnp.concatenate([refs[k][:, pl.ds(start, 256)] for k in range(4)], axis=0)
    slo = jnp.concatenate([refs[4 + k][...] for k in range(4)], axis=0)
    grad = lax.dot_general(lat, slo, (((0,), (0,)), ((), ())), preferred_element_type=f32)
    return grad.reshape(16, 16, OUT_COLS)


def partner_kernel(*refs):
    refs[8][...] = half_gradient(refs, 1 - lax.axis_index("dp") % 2)


def keep_kernel(*refs):
    refs[9][...] = half_gradient(refs, lax.axis_index("dp") % 2) + refs[8][...]


def outer(kernel, *args):
    vmem = pl.BlockSpec(memory_space=pltpu.VMEM)
    return pl.pallas_call(
        kernel,
        out_shape=jax.ShapeDtypeStruct((16, 16, OUT_COLS), f32),
        in_specs=[vmem] * len(args),
        out_specs=vmem,
    )(*args)


def sum_kernel(x, out):
    total = jnp.sum(x[...], axis=0).astype(bf16)
    out[...] = jnp.broadcast_to(total[None], out.shape)


def reduce_parts(x):
    vmem = pl.BlockSpec(memory_space=pltpu.VMEM)
    return pl.pallas_call(
        sum_kernel,
        out_shape=jax.ShapeDtypeStruct((64, 16, OUT_COLS), bf16),
        in_specs=[vmem],
        out_specs=vmem,
        name="reduce_parts",
    )(x)


def place_kernel(own, other, out_a, out_w):
    for n, piece in enumerate((own, other)):
        core = (lax.axis_index("dp") + n) % 2
        blocks = []
        for g in range(ROLES):
            block = piece[g].reshape(64, OUT_COLS).astype(f32)
            out_a[core, :, g * A_COLS : (g + 1) * A_COLS] = block[:, :A_COLS]
            blocks.append(block[:, A_COLS : A_COLS + W_COLS])
        out_w[core] = jnp.concatenate(blocks, axis=1)


def place(own, other):
    spec = pl.BlockSpec((ROLES, 4, 16, OUT_COLS), lambda i: (0, i, 0, 0))
    return pl.pallas_call(
        place_kernel,
        grid=(4,),
        out_shape=[
            jax.ShapeDtypeStruct((2, 256, WAVLM_D), f32),
            jax.ShapeDtypeStruct((2, 256, WHISPER_D), f32),
        ],
        in_specs=[spec, spec],
        out_specs=[
            pl.BlockSpec((2, 64, WAVLM_D), lambda i: (0, i, 0)),
            pl.BlockSpec((2, 64, WHISPER_D), lambda i: (0, i, 0)),
        ],
        name="place",
    )(own, other)


PLANE = [[z * 8 + y * 2 + c for z in range(4) for y in range(4)] for c in range(2)]
SLICE = [[r * 32 + i for r in range(ROLES) for i in plane] for plane in PLANE]


def per_device(
    wavlm_hidden,
    whisper_hidden,
    wavlm_qkv,
    whisper_qkv,
    wavlm_out,
    whisper_out,
    frames_valid,
    slot_clip,
    latent,
    wavlm_head,
    whisper_head,
):
    chunks = weight_chunks(wavlm_qkv.T, whisper_qkv.T)
    chunks = [chunks[0]] + [dp_send(chunks[k], k, 0, 0) for k in (1, 2, 3)]
    lat_copies = spread(latent)
    all_lat = lax.all_to_all(
        lat_copies, "dp", split_axis=0, concat_axis=0, tiled=True, axis_index_groups=PLANE
    )
    copies = shares(chunks)
    own_weights = lax.all_to_all(
        copies, "dp", split_axis=0, concat_axis=0, tiled=True, axis_index_groups=PLANE
    )
    other_weights = dp_send(own_weights, 0, 0, 1)

    lat_own, lat_other = pick(slot_clip, all_lat)
    lat = lat_own + dp_send(lat_other, 0, 0, 1)
    lats = [lat] + [role_send(lat, k) for k in (1, 2, 3)]
    norm_a, norm_w, mean_a, mean_w = norms(wavlm_hidden, whisper_hidden)
    pred_a = jnp.dot(lat, wavlm_head, preferred_element_type=f32)
    pred_w = jnp.dot(lat, whisper_head, preferred_element_type=f32)
    ready = lax.optimization_barrier((other_weights, *lats, pred_a, pred_w))
    other_weights, lats, (pred_a, pred_w) = ready[0], ready[1:5], ready[5:]

    pooled = attend(frames_valid, (own_weights, other_weights), norm_a, norm_w)
    parts = [pooled[0]] + [role_send(pooled[k], k) for k in (1, 2, 3)]
    sloped = slopes(
        frames_valid, parts, wavlm_out, whisper_out, mean_a, mean_w, pred_a, pred_w
    )
    slos = [sloped[0]] + [role_send(sloped[k], k) for k in (1, 2, 3)]
    partner = outer(partner_kernel, *lats, *slos)
    halves = outer(keep_kernel, *lats, *slos, dp_send(partner, 0, 0, 1))
    arrived = lax.all_to_all(
        halves, "dp", split_axis=0, concat_axis=0, tiled=True, axis_index_groups=PLANE
    )
    summed = lax.all_to_all(
        reduce_parts(arrived),
        ("role", "dp"),
        split_axis=0,
        concat_axis=0,
        tiled=True,
        axis_index_groups=SLICE,
    ).reshape(ROLES, 16, 16, OUT_COLS)
    grad_a, grad_w = place(summed, dp_send(summed, 0, 0, 1))
    return grad_a.reshape(STU_D, WAVLM_D), grad_w.reshape(STU_D, WHISPER_D)


def solution(mesh):
    in_specs = (
        P("dp", None, None),
        P("dp", None, None),
        P(None, "dp"),
        P(None, "dp"),
        P(),
        P(),
        P(),
        P(),
        P(None, "dp", None, None),
        P(),
        P(),
    )
    out_specs = (P(), P())

    return jax.shard_map(
        per_device, mesh=mesh, in_specs=in_specs, out_specs=out_specs, check_vma=False
    )
```

```python
import jax
import jax.numpy as jnp
from jax import lax
from jax.experimental import pallas as pl
from jax.experimental.pallas import tpu as pltpu
from jax.sharding import PartitionSpec as P


WAVLM_D = 1024
WHISPER_D = 1280
STU_D = 512
HEAD = 64
FRAMES = 512
POOL = 4
POOLED = 128
CLIPS = 64
ROLES = 4
A_HEADS = WAVLM_D // HEAD // ROLES
W_HEADS = WHISPER_D // HEAD // ROLES
A_COLS = A_HEADS * HEAD
W_COLS = W_HEADS * HEAD
OUT_COLS = 640
ROWS = 64

epsilon_norm = 1e-05
epsilon_cos = 1e-06


bf16 = jnp.bfloat16
f32 = jnp.float32


def dp_send(x, dz, dy, dc):
    pairs = []
    for i in range(32):
        z, y, c = i // 8, (i // 2) % 4, i % 2
        target = ((z + dz) % 4) * 8 + ((y + dy) % 4) * 2 + (c + dc) % 2
        pairs.append((i, target))
    return lax.ppermute(x, "dp", pairs)


def role_send(x, k):
    return lax.ppermute(x, "role", [(i, (i + k) % ROLES) for i in range(ROLES)])


def place_of(column):
    return column // 8, (column // 2) % 4, column % 2


def norm_kernel(wavlm, whisper, norm_a, norm_w, mean_a, mean_w):
    pool_mat = jnp.where(
        lax.broadcasted_iota(jnp.int32, (32, 128), 1) // POOL
        == lax.broadcasted_iota(jnp.int32, (32, 128), 0),
        1.0 / POOL,
        0.0,
    ).astype(bf16)
    for hidden, norm, mean in ((wavlm, norm_a, mean_a), (whisper, norm_w, mean_w)):
        rows = hidden[0].astype(f32)
        centred = rows - jnp.mean(rows, axis=-1, keepdims=True)
        variance = jnp.mean(centred * centred, axis=-1, keepdims=True)
        norm[0] = (centred * lax.rsqrt(variance + epsilon_norm)).astype(bf16)

        @pl.when(pl.program_id(1) == lax.axis_index("role"))
        def _():
            mean[...] = jnp.dot(pool_mat, hidden[0], preferred_element_type=f32)


def norms(wavlm, whisper):
    rows = lambda width: pl.BlockSpec((1, 128, width), lambda i, j: (i, j, 0))
    mean = lambda width: pl.BlockSpec((32, width), lambda i, j: (i, 0))
    return pl.pallas_call(
        norm_kernel,
        grid=(2, 4),
        out_shape=[
            jax.ShapeDtypeStruct(wavlm.shape, bf16),
            jax.ShapeDtypeStruct(whisper.shape, bf16),
            jax.ShapeDtypeStruct((ROWS, WAVLM_D), f32),
            jax.ShapeDtypeStruct((ROWS, WHISPER_D), f32),
        ],
        in_specs=[rows(WAVLM_D), rows(WHISPER_D)],
        out_specs=[rows(WAVLM_D), rows(WHISPER_D), mean(WAVLM_D), mean(WHISPER_D)],
        cost_estimate=pl.CostEstimate(
            flops=60_000_000, bytes_accessed=24_000_000, transcendentals=4096
        ),
        name="norms",
    )(wavlm, whisper)


def chunk_kernel(qkv_a, qkv_w, *refs):
    outs, chunks = refs[:4], refs[4]
    z = place_of(lax.axis_index("dp"))[0]
    for part in range(4):
        for t in range(2):
            lane = (2 * part + t) * 128
            chunks[part, 3 * t : 3 * t + 3] = qkv_a[:, lane : lane + 128].reshape(3, 32, 128)
        for t in range(10):
            if part < 3:
                chunks[part, 6 + t] = qkv_w[32 * part : 32 * part + 32, 128 * t : 128 * t + 128]
            else:
                chunks[part, 6 + t] = jnp.concatenate(
                    [qkv_w[96:120, 128 * t : 128 * t + 128], jnp.zeros((8, 128), bf16)], axis=0
                )
    for k in range(4):
        outs[k][...] = chunks[(z + k) % 4]


def weight_chunks(qkv_a, qkv_w):
    vmem = pl.BlockSpec(memory_space=pltpu.VMEM)
    return pl.pallas_call(
        chunk_kernel,
        out_shape=[jax.ShapeDtypeStruct((16, 32, 128), bf16)] * 4,
        in_specs=[vmem, vmem],
        out_specs=[vmem] * 4,
        scratch_shapes=[pltpu.VMEM((4, 16, 32, 128), bf16)],
        name="weight_chunks",
    )(qkv_a, qkv_w)


def share_kernel(*refs):
    parts, latent, out = refs[:4], refs[4], refs[5]
    role = lax.axis_index("role")
    z, y, c = place_of(lax.axis_index("dp"))
    row = lax.broadcasted_iota(jnp.int32, (32, 128), 0)
    sources = [(role + 4 * ((s - role + 6) % 3)) // 3 for s in range(3)]
    for g in range(4):
        if g < 3:
            column, width = 96 * (2 * y + c) + 32 * g + row, A_COLS
        else:
            column, width = 120 * (2 * y + c) + 32 * z + row, W_COLS
        source = jnp.where(
            column < width, sources[0], jnp.where(column < 2 * width, sources[1], sources[2])
        )
        groups = (g, g + 3) if g < 3 else range(6, 16)
        for group in groups:
            value = parts[0][group].astype(f32)
            for k in range(1, 4):
                value = jnp.where(
                    source == (z - k + 4) % 4, parts[k][group].astype(f32), value
                )
            value = value.astype(bf16)
            out[:, group] = jnp.broadcast_to(value[None], (16, 32, 128))


    for h in range(2):
        for t in range(4):
            value = latent[h, 0, :, 128 * t : 128 * t + 128]
            out[:, 16 + 4 * h + t] = jnp.broadcast_to(value[None], (16, 32, 128))


def shares(parts, latent):
    whole = pl.BlockSpec((16, 32, 128), lambda i: (0, 0, 0))
    return pl.pallas_call(
        share_kernel,
        grid=(1,),
        out_shape=jax.ShapeDtypeStruct((16, 24, 32, 128), bf16),
        in_specs=[whole] * 4
        + [pl.BlockSpec((2, 1, 32, STU_D), lambda i: (0, 0, lax.axis_index("role"), 0))],
        out_specs=pl.BlockSpec((16, 24, 32, 128), lambda i: (0, 0, 0, 0)),
        name="shares",
    )(*parts, latent)


def pick_kernel(slot_clip, own, other, out, slots, rows, sem):
    column = lax.axis_index("dp")
    c = column % 2
    base = (column // 2) * 4

    def find(s, carry):
        local = slot_clip[s] - base

        @pl.when((local >= 0) & (local < 4))
        def _():
            slots[jnp.clip(local, 0, 3)] = s

        return carry

    lax.fori_loop(0, CLIPS, find, 0)
    for i in range(4):
        slot = slots[(2 * c + i) % 4]
        h, j = slot // 32, slot % 32
        groups = pl.ds(16 + 4 * h, 4)

        @pl.when(j % 2 == c)
        def _():
            pltpu.make_async_copy(own.at[j // 2, groups], rows.at[i], sem.at[i]).start()

        @pl.when(j % 2 != c)
        def _():
            pltpu.make_async_copy(other.at[j // 2, groups], rows.at[i], sem.at[i]).start()

    for i in range(4):
        pltpu.make_async_copy(rows.at[i], rows.at[i], sem.at[i]).wait()
        out[i * 32 : i * 32 + 32] = jnp.concatenate([rows[i, t] for t in range(4)], axis=1)


def pick(slot_clip, own, other):
    hbm = pl.BlockSpec(memory_space=pl.ANY)
    return pl.pallas_call(
        pick_kernel,
        out_shape=jax.ShapeDtypeStruct((2 * ROWS, STU_D), bf16),
        in_specs=[pl.BlockSpec(memory_space=pltpu.SMEM), hbm, hbm],
        out_specs=pl.BlockSpec(memory_space=pltpu.VMEM),
        scratch_shapes=[
            pltpu.SMEM((4,), jnp.int32),
            pltpu.VMEM((4, 4, 32, 128), bf16),
            pltpu.SemaphoreType.DMA((4,)),
        ],
        name="pick",
    )(slot_clip, own, other)


def attend_kernel(frames_valid, *refs):
    pieces = refs[:2]
    norm_a_hbm, norm_w_hbm, pooled = refs[2:5]
    norm_a, norm_w, wt_a, wt_w, qkv_a, qkv_w, proj, att_a, att_w = refs[5:14]
    score_refs, sems = refs[14:16], refs[16]
    sem_a, sem_w = sems.at[0], sems.at[1]
    copy_a = pltpu.make_async_copy(norm_a_hbm, norm_a, sems.at[2])
    copy_w = pltpu.make_async_copy(norm_w_hbm, norm_w, sems.at[3])
    role = lax.axis_index("role")
    column = lax.axis_index("dp")
    c = column % 2

    def fetch(p, carry):
        zs = p // 4
        for n, piece in enumerate(pieces):
            block = (p % 4) * 2 + (c + n) % 2
            for t in range(2):
                pltpu.make_async_copy(
                    piece.at[p, pl.ds(3 * t, 3)], wt_a.at[2 * zs + t, pl.ds(3 * block, 3)], sem_a
                ).start()
            pltpu.make_async_copy(
                piece.at[p, pl.ds(6, 10)], wt_w.at[:, block * 4 + zs], sem_w
            ).start()
        return carry

    lax.fori_loop(0, 16, fetch, 0)
    copy_a.start()
    copy_w.start()
    ones_row = jnp.where(
        lax.broadcasted_iota(jnp.int32, (16, FRAMES), 0) == 0, 1.0, 0.0
    ).astype(bf16)
    pool_mat = jnp.where(
        lax.broadcasted_iota(jnp.int32, (POOLED, FRAMES), 1) // POOL
        == lax.broadcasted_iota(jnp.int32, (POOLED, FRAMES), 0),
        1.0 / POOL,
        0.0,
    ).astype(bf16)
    nt = (((1,), (1,)), ((), ()))
    tn = (((0,), (0,)), ((), ()))

    def put(qkv, kind, clip, head, value):
        scale = jnp.where(kind == 0, HEAD ** (-0.5), 1.0).astype(f32)
        qkv[kind, clip, head] = (value.astype(bf16).astype(f32) * scale).astype(bf16)

    def attention(qkv, att, heads):
        rows = lax.broadcasted_iota(jnp.int32, (16, FRAMES), 0)
        frame = lax.broadcasted_iota(jnp.int32, (16, FRAMES), 1)

        bias = [
            jnp.where(
                (rows == 0) & (frame >= frames_valid[column * 2 + clip]), -1e30, 0.0
            ).astype(bf16)
            for clip in range(2)
        ]

        def score(item, scores):
            clip, head = item % 2, item // 2
            key_x = jnp.concatenate([qkv[1, clip, head], bias[clip]], axis=0)
            query_x = jnp.concatenate([qkv[0, clip, head], ones_row], axis=0)
            value = lax.dot_general(key_x, query_x, tn, preferred_element_type=f32)
            scores[...] = value
            return jnp.max(value, axis=0, keepdims=True)

        def mix(item, scores, top):
            clip, head = item % 2, item // 2
            value_x = jnp.concatenate([qkv[2, clip, head], ones_row], axis=0)
            raised = jnp.exp(scores[...] - top).astype(bf16)
            mixed = jnp.dot(value_x, raised, preferred_element_type=f32)
            total = mixed[HEAD : HEAD + 1]
            att[clip, head] = (mixed[:HEAD] * (1.0 / total)).astype(bf16)

        top = score(0, score_refs[0])
        for item in range(2 * heads):
            if item + 1 < 2 * heads:
                next_top = score(item + 1, score_refs[(item + 1) % 2])
            mix(item, score_refs[item % 2], top)
            top = next_top

    pltpu.make_async_copy(wt_a, wt_a, sem_a).wait()
    copy_a.wait()
    for clip in range(2):
        lhs = jnp.concatenate([wt_a[t].reshape(3 * A_COLS, 128) for t in range(8)], axis=1)
        value = lax.dot_general(lhs, norm_a[clip], nt, preferred_element_type=f32)
        for s in range(3):
            kind = (s - role + 6) % 3
            for h in range(A_HEADS):
                start = s * A_COLS + h * HEAD
                put(qkv_a, kind, clip, h, value[start : start + HEAD])
    attention(qkv_a, att_a, A_HEADS)
    for clip in range(2):
        rows = att_a[clip].reshape(A_COLS, FRAMES)
        mean = lax.dot_general(pool_mat, rows, nt, preferred_element_type=f32).astype(bf16)
        pooled[:, clip * 32 : clip * 32 + 32, :A_COLS] = mean.reshape(ROLES, 32, A_COLS)

    pltpu.make_async_copy(wt_w, wt_w, sem_w).wait()
    copy_w.wait()
    for clip in range(2):
        lhs = jnp.concatenate([wt_w[t].reshape(1024, 128) for t in range(10)], axis=1)
        proj[...] = lax.dot_general(lhs, norm_w[clip], nt, preferred_element_type=f32)
        for s in range(3):
            kind = (s - role + 6) % 3
            for h in range(W_HEADS):
                start = s * W_COLS + h * HEAD
                parts = []
                while start < s * W_COLS + (h + 1) * HEAD:
                    block, inner = start // 120, start % 120
                    take = min(120 - inner, s * W_COLS + (h + 1) * HEAD - start)
                    parts.append(proj[block * 128 + inner : block * 128 + inner + take])
                    start += take
                value = parts[0] if len(parts) == 1 else jnp.concatenate(parts, axis=0)
                put(qkv_w, kind, clip, h, value)
    attention(qkv_w, att_w, W_HEADS)
    for clip in range(2):
        rows = att_w[clip].reshape(W_COLS, FRAMES)
        mean = lax.dot_general(pool_mat, rows, nt, preferred_element_type=f32).astype(bf16)
        mean = jnp.concatenate([mean, jnp.zeros((POOLED, 64), bf16)], axis=1)
        pooled[:, clip * 32 : clip * 32 + 32, A_COLS:] = mean.reshape(ROLES, 32, 384)


def attend(frames_valid, pieces, norm_a, norm_w):
    vmem = pl.BlockSpec(memory_space=pltpu.VMEM)
    return pl.pallas_call(
        attend_kernel,
        out_shape=jax.ShapeDtypeStruct((ROLES, ROWS, OUT_COLS), bf16),
        in_specs=[pl.BlockSpec(memory_space=pltpu.SMEM)]
        + [pl.BlockSpec(memory_space=pl.ANY)] * 4,
        out_specs=vmem,
        scratch_shapes=[
            pltpu.VMEM((2, FRAMES, WAVLM_D), bf16),
            pltpu.VMEM((2, FRAMES, WHISPER_D), bf16),
            pltpu.VMEM((8, 24, 32, 128), bf16),
            pltpu.VMEM((10, 32, 32, 128), bf16),
            pltpu.VMEM((3, 2, A_HEADS, HEAD, FRAMES), bf16),
            pltpu.VMEM((3, 2, W_HEADS, HEAD, FRAMES), bf16),
            pltpu.VMEM((1024, FRAMES), f32),
            pltpu.VMEM((2, A_HEADS, HEAD, FRAMES), bf16),
            pltpu.VMEM((2, W_HEADS, HEAD, FRAMES), bf16),
            pltpu.VMEM((FRAMES, FRAMES), f32),
            pltpu.VMEM((FRAMES, FRAMES), f32),
            pltpu.SemaphoreType.DMA((4,)),
        ],
        cost_estimate=pl.CostEstimate(
            flops=8_000_000_000, bytes_accessed=12_000_000, transcendentals=5_000_000
        ),
        name="attend",
    )(frames_valid, *pieces, norm_a, norm_w)


def slope_kernel(frames_valid, parts, out_a_hbm, out_w_hbm, *refs):
    mean_a, mean_w, pred_a, pred_w, grouped, out_a, out_w, sems = refs
    copy_a = pltpu.make_async_copy(out_a_hbm, out_a, sems.at[0])
    copy_w = pltpu.make_async_copy(out_w_hbm, out_w, sems.at[1])
    copy_a.start()
    copy_w.start()
    role = lax.axis_index("role")
    clip = lax.axis_index("dp") * 2
    row = lax.broadcasted_iota(jnp.int32, (ROWS, 1), 0)
    valid = jnp.where(row < 32, frames_valid[clip], frames_valid[clip + 1]) // POOL
    keep = (row % 32 + role * 32) < valid

    def slope_of(mean, copy, out, pred, cols, first):
        width = mean.shape[-1]
        attended = jnp.concatenate(
            [parts[r, :, first : first + cols] for r in range(ROLES)], axis=1
        )
        copy.wait()
        total = mean[...] + jnp.dot(attended, out[...], preferred_element_type=f32)
        target = total.astype(bf16).astype(f32)
        predicted = pred[...]
        pred_sq = jnp.sum(predicted * predicted, axis=-1, keepdims=True) + epsilon_cos
        targ_sq = jnp.sum(target * target, axis=-1, keepdims=True) + epsilon_cos
        pred_norm = jnp.sqrt(pred_sq)
        both = pred_norm * jnp.sqrt(targ_sq)
        cosine = jnp.sum(predicted * target, axis=-1, keepdims=True) / both
        slope = (cosine / (pred_norm * pred_norm)) * predicted - target / both
        slope = slope + (predicted - target) * (1.0 / width)
        return jnp.where(keep, slope, 0.0).astype(bf16)

    slope_a = slope_of(mean_a, copy_a, out_a, pred_a, A_COLS, 0)
    for g in range(ROLES):
        grouped[g, :, :A_COLS] = slope_a[:, g * A_COLS : (g + 1) * A_COLS]
    slope_w = slope_of(mean_w, copy_w, out_w, pred_w, W_COLS, A_COLS)
    for g in range(ROLES):
        grouped[g, :, A_COLS:] = jnp.concatenate(
            [slope_w[:, g * W_COLS : (g + 1) * W_COLS], jnp.zeros((ROWS, 64), bf16)], axis=1
        )


def slopes(frames_valid, parts, out_a, out_w, mean_a, mean_w, pred_a, pred_w):
    vmem = pl.BlockSpec(memory_space=pltpu.VMEM)
    hbm = pl.BlockSpec(memory_space=pl.ANY)
    return pl.pallas_call(
        slope_kernel,
        out_shape=jax.ShapeDtypeStruct((ROLES, ROWS, OUT_COLS), bf16),
        in_specs=[pl.BlockSpec(memory_space=pltpu.SMEM), vmem, hbm, hbm] + [vmem] * 4,
        out_specs=vmem,
        scratch_shapes=[
            pltpu.VMEM((WAVLM_D, WAVLM_D), bf16),
            pltpu.VMEM((WHISPER_D, WHISPER_D), bf16),
            pltpu.SemaphoreType.DMA((2,)),
        ],
        name="slopes",
    )(frames_valid, parts, out_a, out_w, mean_a, mean_w, pred_a, pred_w)


def outer_kernel(*refs):
    lats, own, other, out = refs[:4], refs[4], refs[5], refs[6]
    role = lax.axis_index("role")
    start = pl.multiple_of((lax.axis_index("dp") % 2) * 256, 256)
    lat = jnp.concatenate([lats[k][:, pl.ds(start, 256)] for k in range(ROLES)], axis=0)
    rows = []
    for k in range(ROLES):
        source = (role - k + ROLES) % ROLES
        rows += [own[source], other[source]]
    grad = lax.dot_general(
        lat, jnp.concatenate(rows, axis=0), (((0,), (0,)), ((), ())), preferred_element_type=f32
    )
    out[...] = grad.reshape(16, 16, OUT_COLS)


def outer(lats, own, other):
    vmem = pl.BlockSpec(memory_space=pltpu.VMEM)
    return pl.pallas_call(
        outer_kernel,
        out_shape=jax.ShapeDtypeStruct((16, 16, OUT_COLS), f32),
        in_specs=[vmem] * 6,
        out_specs=vmem,
        name="outer",
    )(*lats, own, other)


def sum_kernel(x, out):
    total = jnp.sum(x[...], axis=0).astype(bf16)
    out[...] = jnp.broadcast_to(total[None], out.shape)


def reduce_parts(x):
    vmem = pl.BlockSpec(memory_space=pltpu.VMEM)
    return pl.pallas_call(
        sum_kernel,
        out_shape=jax.ShapeDtypeStruct((64, 16, OUT_COLS), bf16),
        in_specs=[vmem],
        out_specs=vmem,
        name="reduce_parts",
    )(x)


def place_kernel(piece, *refs):
    out_a, out_w = refs[-2:]
    blocks = []
    for g in range(ROLES):
        block = piece[g].reshape(128, OUT_COLS).astype(f32)
        out_a[0, :, g * A_COLS : (g + 1) * A_COLS] = block[:, :A_COLS]
        blocks.append(block[:, A_COLS : A_COLS + W_COLS])
    out_w[0] = jnp.concatenate(blocks, axis=1)


def place(piece, partner, held=()):
    half = lambda: (lax.axis_index("dp") + partner) % 2
    hbm = pl.BlockSpec(memory_space=pl.ANY)
    return pl.pallas_call(
        place_kernel,
        grid=(2,),
        out_shape=[
            jax.ShapeDtypeStruct((2, 256, WAVLM_D), f32),
            jax.ShapeDtypeStruct((2, 256, WHISPER_D), f32),
        ],
        in_specs=[pl.BlockSpec((ROLES, 8, 16, OUT_COLS), lambda i: (0, i, 0, 0))]
        + [hbm] * len(held),
        out_specs=[
            pl.BlockSpec((1, 128, WAVLM_D), lambda i: (half(), i, 0)),
            pl.BlockSpec((1, 128, WHISPER_D), lambda i: (half(), i, 0)),
        ],
        input_output_aliases={1: 0, 2: 1} if held else {},
        name="place_partner" if partner else "place_own",
    )(piece, *held)


PLANE = [[z * 8 + y * 2 + c for z in range(4) for y in range(4)] for c in range(2)]
SLICE = [[r * 32 + i for r in range(ROLES) for i in plane] for plane in PLANE]


def per_device(
    wavlm_hidden,
    whisper_hidden,
    wavlm_qkv,
    whisper_qkv,
    wavlm_out,
    whisper_out,
    frames_valid,
    slot_clip,
    latent,
    wavlm_head,
    whisper_head,
):
    chunks = weight_chunks(wavlm_qkv.T, whisper_qkv.T)
    chunks = [chunks[0]] + [dp_send(chunks[k], k, 0, 0) for k in (1, 2, 3)]
    copies = shares(chunks, latent)
    own_rows = lax.all_to_all(
        copies, "dp", split_axis=0, concat_axis=0, tiled=True, axis_index_groups=PLANE
    )
    other_rows = dp_send(own_rows, 0, 0, 1)
    norm_a, norm_w, mean_a, mean_w = norms(wavlm_hidden, whisper_hidden)

    pooled = attend(frames_valid, (own_rows, other_rows), norm_a, norm_w)
    parts = lax.all_to_all(pooled, "role", split_axis=0, concat_axis=0, tiled=True)
    lat = pick(slot_clip, own_rows, other_rows)
    lats = [lat] + [role_send(lat, k) for k in (1, 2, 3)]
    pred_a = jnp.dot(lat[:ROWS], wavlm_head, preferred_element_type=f32)
    pred_w = jnp.dot(lat[:ROWS], whisper_head, preferred_element_type=f32)
    sloped = slopes(
        frames_valid, parts, wavlm_out, whisper_out, mean_a, mean_w, pred_a, pred_w
    )
    slope_own = lax.all_to_all(sloped, "role", split_axis=0, concat_axis=0, tiled=True)
    slope_other = dp_send(slope_own, 0, 0, 1)
    halves = outer(lats, slope_own, slope_other)
    arrived = lax.all_to_all(
        halves, "dp", split_axis=0, concat_axis=0, tiled=True, axis_index_groups=PLANE
    )
    summed = lax.all_to_all(
        reduce_parts(arrived),
        ("role", "dp"),
        split_axis=0,
        concat_axis=0,
        tiled=True,
        axis_index_groups=SLICE,
    ).reshape(ROLES, 16, 16, OUT_COLS)
    partner = dp_send(summed, 0, 0, 1)
    held = place(summed, 0)
    grad_a, grad_w = place(partner, 1, held)
    return grad_a.reshape(STU_D, WAVLM_D), grad_w.reshape(STU_D, WHISPER_D)


def solution(mesh):
    in_specs = (
        P("dp", None, None),
        P("dp", None, None),
        P(None, "dp"),
        P(None, "dp"),
        P(),
        P(),
        P(),
        P(),
        P(None, "dp", None, None),
        P(),
        P(),
    )
    out_specs = (P(), P())

    return jax.shard_map(
        per_device, mesh=mesh, in_specs=in_specs, out_specs=out_specs, check_vma=False
    )
```

```python
import jax
import jax.numpy as jnp
from jax import lax
from jax.experimental import pallas as pl
from jax.experimental.pallas import tpu as pltpu
from jax.sharding import PartitionSpec as P


WAVLM_D = 1024
WHISPER_D = 1280
STU_D = 512
HEAD = 64
FRAMES = 512
POOL = 4
POOLED = 128
CLIPS = 64
ROLES = 4
A_HEADS = WAVLM_D // HEAD // ROLES
W_HEADS = WHISPER_D // HEAD // ROLES
A_COLS = A_HEADS * HEAD
W_COLS = W_HEADS * HEAD
OUT_COLS = 640
ROWS = 64

epsilon_norm = 1e-05
epsilon_cos = 1e-06


bf16 = jnp.bfloat16
f32 = jnp.float32


def dp_send(x, dz, dy, dc):
    pairs = []
    for i in range(32):
        z, y, c = i // 8, (i // 2) % 4, i % 2
        target = ((z + dz) % 4) * 8 + ((y + dy) % 4) * 2 + (c + dc) % 2
        pairs.append((i, target))
    return lax.ppermute(x, "dp", pairs)


def role_send(x, k):
    return lax.ppermute(x, "role", [(i, (i + k) % ROLES) for i in range(ROLES)])


def place_of(column):
    return column // 8, (column // 2) % 4, column % 2


def norm_kernel(wavlm, whisper, norm_a, norm_w, mean_a, mean_w):
    pool_mat = jnp.where(
        lax.broadcasted_iota(jnp.int32, (32, 128), 1) // POOL
        == lax.broadcasted_iota(jnp.int32, (32, 128), 0),
        1.0 / POOL,
        0.0,
    ).astype(bf16)
    for hidden, norm, mean in ((wavlm, norm_a, mean_a), (whisper, norm_w, mean_w)):
        rows = hidden[0].astype(f32)
        centred = rows - jnp.mean(rows, axis=-1, keepdims=True)
        variance = jnp.mean(centred * centred, axis=-1, keepdims=True)
        norm[0] = (centred * lax.rsqrt(variance + epsilon_norm)).astype(bf16)

        @pl.when(pl.program_id(1) == lax.axis_index("role"))
        def _():
            mean[...] = jnp.dot(pool_mat, hidden[0], preferred_element_type=f32)


def norms(wavlm, whisper):
    rows = lambda width: pl.BlockSpec((1, 128, width), lambda i, j: (i, j, 0))
    mean = lambda width: pl.BlockSpec((32, width), lambda i, j: (i, 0))
    return pl.pallas_call(
        norm_kernel,
        grid=(2, 4),
        out_shape=[
            jax.ShapeDtypeStruct(wavlm.shape, bf16),
            jax.ShapeDtypeStruct(whisper.shape, bf16),
            jax.ShapeDtypeStruct((ROWS, WAVLM_D), f32),
            jax.ShapeDtypeStruct((ROWS, WHISPER_D), f32),
        ],
        in_specs=[rows(WAVLM_D), rows(WHISPER_D)],
        out_specs=[rows(WAVLM_D), rows(WHISPER_D), mean(WAVLM_D), mean(WHISPER_D)],
        cost_estimate=pl.CostEstimate(
            flops=60_000_000, bytes_accessed=24_000_000, transcendentals=4096
        ),
        name="norms",
    )(wavlm, whisper)


def chunk_kernel(qkv_a, qkv_w, *refs):
    outs, chunks = refs[:4], refs[4]
    z = place_of(lax.axis_index("dp"))[0]
    for part in range(4):
        for t in range(2):
            lane = (2 * part + t) * 128
            chunks[part, 8 * t : 8 * t + 3] = qkv_a[:, lane : lane + 128].reshape(3, 32, 128)
        for t in range(10):
            if part < 3:
                chunks[part, 3 + t + 3 * (t // 5)] = qkv_w[32 * part : 32 * part + 32, 128 * t : 128 * t + 128]
            else:
                chunks[part, 3 + t + 3 * (t // 5)] = jnp.concatenate(
                    [qkv_w[96:120, 128 * t : 128 * t + 128], jnp.zeros((8, 128), bf16)], axis=0
                )
    for k in range(4):
        outs[k][...] = chunks[(z + k) % 4]


def weight_chunks(qkv_a, qkv_w):
    vmem = pl.BlockSpec(memory_space=pltpu.VMEM)
    return pl.pallas_call(
        chunk_kernel,
        out_shape=[jax.ShapeDtypeStruct((16, 32, 128), bf16)] * 4,
        in_specs=[vmem, vmem],
        out_specs=[vmem] * 4,
        scratch_shapes=[pltpu.VMEM((4, 16, 32, 128), bf16)],
        name="weight_chunks",
    )(qkv_a, qkv_w)


def share_kernel(*refs):
    parts, latent, outs = refs[:4], refs[4], refs[5:]
    role = lax.axis_index("role")
    z, y, c = place_of(lax.axis_index("dp"))
    row = lax.broadcasted_iota(jnp.int32, (32, 128), 0)
    sources = [(role + 4 * ((s - role + 6) % 3)) // 3 for s in range(3)]
    for g in range(4):
        if g < 3:
            column, width = 96 * (2 * y + c) + 32 * g + row, A_COLS
        else:
            column, width = 120 * (2 * y + c) + 32 * z + row, W_COLS
        source = jnp.where(
            column < width, sources[0], jnp.where(column < 2 * width, sources[1], sources[2])
        )
        for half in range(2):
            for group in (g,) if g < 3 else range(3, 8):
                value = parts[0][8 * half + group].astype(f32)
                for k in range(1, 4):
                    other = parts[k][8 * half + group].astype(f32)
                    value = jnp.where(source == (z - k + 4) % 4, other, value)
                outs[half][group] = value.astype(bf16)
    for half in range(2):
        for t in range(4):
            outs[half][8 + t] = latent[half, 0, :, 128 * t : 128 * t + 128]


def shares(parts, latent):
    whole = pl.BlockSpec((16, 32, 128), lambda i: (0, 0, 0))
    half = pl.BlockSpec((12, 32, 128), lambda i: (0, 0, 0))
    return pl.pallas_call(
        share_kernel,
        grid=(1,),
        out_shape=[jax.ShapeDtypeStruct((12, 32, 128), bf16)] * 2,
        in_specs=[whole] * 4
        + [pl.BlockSpec((2, 1, 32, STU_D), lambda i: (0, 0, lax.axis_index("role"), 0))],
        out_specs=[half] * 2,
        name="shares",
    )(*parts, latent)


def spread_line(first, second):
    got = {}
    for k in (1, 3, 2):
        got[k] = dp_send(first, k, 0, 0), dp_send(second, 0, k, 0)
    lines = [first] + [got[k][0] for k in (1, 2, 3)], [second] + [got[k][1] for k in (1, 2, 3)]
    return jnp.stack(lines[0]), jnp.stack(lines[1])


def spread_cross(first, second):
    send_a = lambda x, k: dp_send(x, 0, k, 0)
    send_b = lambda x, k: dp_send(x, k, 0, 0)
    a1, b1 = send_a(first, 1), send_b(second, 1)
    a3, b3 = send_a(first, 3), send_b(second, 3)
    a2, b2 = send_a(a1[:2], 1), send_b(b1[:2], 1)
    a2x, b2x = send_a(a3[2:], 3), send_b(b3[2:], 3)
    return [first, a1, a3, a2, a2x, second, b1, b3, b2, b2x]


CROSS = [(0, 0), (1, 0), (3, 0), (2, 0), (2, 2)]


def pick_latents(slot_clip, rows, slots, out):
    column = lax.axis_index("dp")
    c = column % 2
    base = (column // 2) * 4

    def find(s, carry):
        local = slot_clip[s] - base

        @pl.when((local >= 0) & (local < 4))
        def _():
            slots[jnp.clip(local, 0, 3)] = s

        return carry

    lax.fori_loop(0, CLIPS, find, 0)
    for i in range(4):
        slot = slots[(2 * c + i) % 4]
        h, j = slot // 32, slot % 32
        out[i * 32 : i * 32 + 32] = jnp.concatenate(
            [rows[j, 12 * h + 8 + t] for t in range(4)], axis=1
        )


def attend_kernel(frames_valid, slot_clip, *refs):
    pieces = refs[:20]
    norm_a_hbm, norm_w_hbm, pooled, lat = refs[20:24]
    norm_a, norm_w, rows_in, qkv_a, qkv_w, proj, att_a, att_w = refs[24:32]
    score_refs, slots, sems = refs[32:34], refs[34], refs[35]
    copy_a = pltpu.make_async_copy(norm_a_hbm, norm_a, sems.at[2])
    copy_w = pltpu.make_async_copy(norm_w_hbm, norm_w, sems.at[3])
    role = lax.axis_index("role")
    column = lax.axis_index("dp")
    z, y, c = place_of(column)
    for first, count, sem in ((0, 3, sems.at[0]), (3, 9, sems.at[1])):
        for n, piece in enumerate(pieces):
            core = (c + n // 10) % 2
            half = (n % 10) // 5
            far, entry = CROSS[n % 5]
            for e in range(piece.shape[0]):
                near = entry + e
                dz, dy = (near, far) if half == 0 else (far, near)
                device = ((z - dz) % 4) * 8 + ((y - dy) % 4) * 2 + core
                pltpu.make_async_copy(
                    piece.at[e, pl.ds(first, count)],
                    rows_in.at[device, pl.ds(12 * half + first, count)],
                    sem,
                ).start()
        if first == 0:
            copy_a.start()
    copy_w.start()
    wait_a = pltpu.make_async_copy(
        rows_in.at[:, pl.ds(0, 6)], rows_in.at[:, pl.ds(0, 6)], sems.at[0]
    )
    wait_w = pltpu.make_async_copy(
        rows_in.at[:, pl.ds(0, 18)], rows_in.at[:, pl.ds(0, 18)], sems.at[1]
    )
    ones_row = jnp.where(
        lax.broadcasted_iota(jnp.int32, (16, FRAMES), 0) == 0, 1.0, 0.0
    ).astype(bf16)
    pool_mat = jnp.where(
        lax.broadcasted_iota(jnp.int32, (POOLED, FRAMES), 1) // POOL
        == lax.broadcasted_iota(jnp.int32, (POOLED, FRAMES), 0),
        1.0 / POOL,
        0.0,
    ).astype(bf16)
    nt = (((1,), (1,)), ((), ()))
    tn = (((0,), (0,)), ((), ()))

    def put(qkv, kind, clip, head, value):
        scale = jnp.where(kind == 0, HEAD ** (-0.5), 1.0).astype(f32)
        qkv[kind, clip, head] = (value.astype(bf16).astype(f32) * scale).astype(bf16)

    def attention(qkv, att, heads):
        rows = lax.broadcasted_iota(jnp.int32, (16, FRAMES), 0)
        frame = lax.broadcasted_iota(jnp.int32, (16, FRAMES), 1)

        bias = [
            jnp.where(
                (rows == 0) & (frame >= frames_valid[column * 2 + clip]), -1e30, 0.0
            ).astype(bf16)
            for clip in range(2)
        ]

        def score(item, scores):
            clip, head = item % 2, item // 2
            key_x = jnp.concatenate([qkv[1, clip, head], bias[clip]], axis=0)
            query_x = jnp.concatenate([qkv[0, clip, head], ones_row], axis=0)
            value = lax.dot_general(key_x, query_x, tn, preferred_element_type=f32)
            scores[...] = value
            return jnp.max(value, axis=0, keepdims=True)

        def mix(item, scores, top):
            clip, head = item % 2, item // 2
            value_x = jnp.concatenate([qkv[2, clip, head], ones_row], axis=0)
            raised = jnp.exp(scores[...] - top).astype(bf16)
            mixed = jnp.dot(value_x, raised, preferred_element_type=f32)
            total = mixed[HEAD : HEAD + 1]
            att[clip, head] = (mixed[:HEAD] * (1.0 / total)).astype(bf16)

        top = score(0, score_refs[0])
        for item in range(2 * heads):
            if item + 1 < 2 * heads:
                next_top = score(item + 1, score_refs[(item + 1) % 2])
            mix(item, score_refs[item % 2], top)
            top = next_top

    wait_a.wait()
    copy_a.wait()
    for clip in range(2):
        lhs = jnp.concatenate(
            [
                jnp.concatenate(
                    [
                        rows_in[8 * (t // 2) + block, 12 * (t % 2) : 12 * (t % 2) + 3].reshape(
                            96, 128
                        )
                        for block in range(8)
                    ],
                    axis=0,
                )
                for t in range(8)
            ],
            axis=1,
        )
        value = lax.dot_general(lhs, norm_a[clip], nt, preferred_element_type=f32)
        for s in range(3):
            kind = (s - role + 6) % 3
            for h in range(A_HEADS):
                start = s * A_COLS + h * HEAD
                put(qkv_a, kind, clip, h, value[start : start + HEAD])
    attention(qkv_a, att_a, A_HEADS)
    for clip in range(2):
        rows = att_a[clip].reshape(A_COLS, FRAMES)
        mean = lax.dot_general(pool_mat, rows, nt, preferred_element_type=f32).astype(bf16)
        pooled[:, clip * 32 : clip * 32 + 32, :A_COLS] = mean.reshape(ROLES, 32, A_COLS)

    wait_w.wait()
    copy_w.wait()
    for clip in range(2):
        lhs = jnp.concatenate(
            [
                jnp.concatenate(
                    [
                        rows_in[8 * zs + block, 12 * (t // 5) + 3 + t % 5]
                        for block in range(8)
                        for zs in range(4)
                    ],
                    axis=0,
                )
                for t in range(10)
            ],
            axis=1,
        )
        proj[...] = lax.dot_general(lhs, norm_w[clip], nt, preferred_element_type=f32)
        for s in range(3):
            kind = (s - role + 6) % 3
            for h in range(W_HEADS):
                start = s * W_COLS + h * HEAD
                parts = []
                while start < s * W_COLS + (h + 1) * HEAD:
                    block, inner = start // 120, start % 120
                    take = min(120 - inner, s * W_COLS + (h + 1) * HEAD - start)
                    parts.append(proj[block * 128 + inner : block * 128 + inner + take])
                    start += take
                value = parts[0] if len(parts) == 1 else jnp.concatenate(parts, axis=0)
                put(qkv_w, kind, clip, h, value)
    attention(qkv_w, att_w, W_HEADS)
    for clip in range(2):
        rows = att_w[clip].reshape(W_COLS, FRAMES)
        mean = lax.dot_general(pool_mat, rows, nt, preferred_element_type=f32).astype(bf16)
        mean = jnp.concatenate([mean, jnp.zeros((POOLED, 64), bf16)], axis=1)
        pooled[:, clip * 32 : clip * 32 + 32, A_COLS:] = mean.reshape(ROLES, 32, 384)
    pick_latents(slot_clip, rows_in, slots, lat)


def attend(frames_valid, slot_clip, pieces, norm_a, norm_w):
    vmem = pl.BlockSpec(memory_space=pltpu.VMEM)
    return pl.pallas_call(
        attend_kernel,
        out_shape=[
            jax.ShapeDtypeStruct((ROLES, ROWS, OUT_COLS), bf16),
            jax.ShapeDtypeStruct((2 * ROWS, STU_D), bf16),
        ],
        in_specs=[pl.BlockSpec(memory_space=pltpu.SMEM)] * 2
        + [pl.BlockSpec(memory_space=pl.ANY)] * 22,
        out_specs=[vmem] * 2,
        scratch_shapes=[
            pltpu.VMEM((2, FRAMES, WAVLM_D), bf16),
            pltpu.VMEM((2, FRAMES, WHISPER_D), bf16),
            pltpu.VMEM((32, 24, 32, 128), bf16),
            pltpu.VMEM((3, 2, A_HEADS, HEAD, FRAMES), bf16),
            pltpu.VMEM((3, 2, W_HEADS, HEAD, FRAMES), bf16),
            pltpu.VMEM((1024, FRAMES), f32),
            pltpu.VMEM((2, A_HEADS, HEAD, FRAMES), bf16),
            pltpu.VMEM((2, W_HEADS, HEAD, FRAMES), bf16),
            pltpu.VMEM((FRAMES, FRAMES), f32),
            pltpu.VMEM((FRAMES, FRAMES), f32),
            pltpu.SMEM((4,), jnp.int32),
            pltpu.SemaphoreType.DMA((4,)),
        ],
        cost_estimate=pl.CostEstimate(
            flops=8_000_000_000, bytes_accessed=12_000_000, transcendentals=5_000_000
        ),
        name="attend",
    )(frames_valid, slot_clip, *pieces, norm_a, norm_w)


def slope_kernel(frames_valid, parts, out_a_hbm, out_w_hbm, *refs):
    mean_a, mean_w, pred_a, pred_w, grouped, out_a, out_w, sems = refs
    copy_a = pltpu.make_async_copy(out_a_hbm, out_a, sems.at[0])
    copy_w = pltpu.make_async_copy(out_w_hbm, out_w, sems.at[1])
    copy_a.start()
    copy_w.start()
    role = lax.axis_index("role")
    clip = lax.axis_index("dp") * 2
    row = lax.broadcasted_iota(jnp.int32, (ROWS, 1), 0)
    valid = jnp.where(row < 32, frames_valid[clip], frames_valid[clip + 1]) // POOL
    keep = (row % 32 + role * 32) < valid

    def slope_of(mean, copy, out, pred, cols, first):
        width = mean.shape[-1]
        attended = jnp.concatenate(
            [parts[r, :, first : first + cols] for r in range(ROLES)], axis=1
        )
        copy.wait()
        total = mean[...] + jnp.dot(attended, out[...], preferred_element_type=f32)
        target = total.astype(bf16).astype(f32)
        predicted = pred[...]
        pred_sq = jnp.sum(predicted * predicted, axis=-1, keepdims=True) + epsilon_cos
        targ_sq = jnp.sum(target * target, axis=-1, keepdims=True) + epsilon_cos
        pred_norm = jnp.sqrt(pred_sq)
        both = pred_norm * jnp.sqrt(targ_sq)
        cosine = jnp.sum(predicted * target, axis=-1, keepdims=True) / both
        slope = (cosine / (pred_norm * pred_norm)) * predicted - target / both
        slope = slope + (predicted - target) * (1.0 / width)
        return jnp.where(keep, slope, 0.0).astype(bf16)

    slope_a = slope_of(mean_a, copy_a, out_a, pred_a, A_COLS, 0)
    for g in range(ROLES):
        grouped[g, :, :A_COLS] = slope_a[:, g * A_COLS : (g + 1) * A_COLS]
    slope_w = slope_of(mean_w, copy_w, out_w, pred_w, W_COLS, A_COLS)
    for g in range(ROLES):
        grouped[g, :, A_COLS:] = jnp.concatenate(
            [slope_w[:, g * W_COLS : (g + 1) * W_COLS], jnp.zeros((ROWS, 64), bf16)], axis=1
        )


def slopes(frames_valid, parts, out_a, out_w, mean_a, mean_w, pred_a, pred_w):
    vmem = pl.BlockSpec(memory_space=pltpu.VMEM)
    hbm = pl.BlockSpec(memory_space=pl.ANY)
    return pl.pallas_call(
        slope_kernel,
        out_shape=jax.ShapeDtypeStruct((ROLES, ROWS, OUT_COLS), bf16),
        in_specs=[pl.BlockSpec(memory_space=pltpu.SMEM), vmem, hbm, hbm] + [vmem] * 4,
        out_specs=vmem,
        scratch_shapes=[
            pltpu.VMEM((WAVLM_D, WAVLM_D), bf16),
            pltpu.VMEM((WHISPER_D, WHISPER_D), bf16),
            pltpu.SemaphoreType.DMA((2,)),
        ],
        name="slopes",
    )(frames_valid, parts, out_a, out_w, mean_a, mean_w, pred_a, pred_w)


def pass_kernel(x, out):
    out[...] = x[...]


def passed(x):
    vmem = pl.BlockSpec(memory_space=pltpu.VMEM)
    return pl.pallas_call(
        pass_kernel,
        out_shape=jax.ShapeDtypeStruct(x.shape, x.dtype),
        in_specs=[vmem],
        out_specs=vmem,
        name="passed",
    )(x)


def outer_kernel(*refs):
    lats, own, other, out = refs[:4], refs[4], refs[5], refs[6]
    role = lax.axis_index("role")
    start = pl.multiple_of((lax.axis_index("dp") % 2) * 256, 256)
    lat = jnp.concatenate([lats[k][:, pl.ds(start, 256)] for k in range(ROLES)], axis=0)
    rows = []
    for k in range(ROLES):
        source = (role - k + ROLES) % ROLES
        rows += [own[source], other[source]]
    grad = lax.dot_general(
        lat, jnp.concatenate(rows, axis=0), (((0,), (0,)), ((), ())), preferred_element_type=f32
    )
    out[...] = grad.reshape(16, 16, OUT_COLS)


def outer(lats, own, other):
    vmem = pl.BlockSpec(memory_space=pltpu.VMEM)
    return pl.pallas_call(
        outer_kernel,
        out_shape=jax.ShapeDtypeStruct((16, 16, OUT_COLS), f32),
        in_specs=[vmem] * 6,
        out_specs=vmem,
        name="outer",
    )(*lats, own, other)


def sum_kernel(x, out):
    total = jnp.sum(x[...], axis=0).astype(bf16)
    out[...] = jnp.broadcast_to(total[None], out.shape)


def reduce_parts(x):
    vmem = pl.BlockSpec(memory_space=pltpu.VMEM)
    return pl.pallas_call(
        sum_kernel,
        out_shape=jax.ShapeDtypeStruct((64, 16, OUT_COLS), bf16),
        in_specs=[vmem],
        out_specs=vmem,
        name="reduce_parts",
    )(x)


def place_kernel(piece, *refs):
    out_a, out_w = refs[-2:]
    blocks = []
    for g in range(ROLES):
        block = piece[g].reshape(128, OUT_COLS).astype(f32)
        out_a[0, :, g * A_COLS : (g + 1) * A_COLS] = block[:, :A_COLS]
        blocks.append(block[:, A_COLS : A_COLS + W_COLS])
    out_w[0] = jnp.concatenate(blocks, axis=1)


def place(piece, partner, held=()):
    half = lambda: (lax.axis_index("dp") + partner) % 2
    hbm = pl.BlockSpec(memory_space=pl.ANY)
    return pl.pallas_call(
        place_kernel,
        grid=(2,),
        out_shape=[
            jax.ShapeDtypeStruct((2, 256, WAVLM_D), f32),
            jax.ShapeDtypeStruct((2, 256, WHISPER_D), f32),
        ],
        in_specs=[pl.BlockSpec((ROLES, 8, 16, OUT_COLS), lambda i: (0, i, 0, 0))]
        + [hbm] * len(held),
        out_specs=[
            pl.BlockSpec((1, 128, WAVLM_D), lambda i: (half(), i, 0)),
            pl.BlockSpec((1, 128, WHISPER_D), lambda i: (half(), i, 0)),
        ],
        input_output_aliases={1: 0, 2: 1} if held else {},
        name="place_partner" if partner else "place_own",
    )(piece, *held)


PLANE = [[z * 8 + y * 2 + c for z in range(4) for y in range(4)] for c in range(2)]
SLICE = [[r * 32 + i for r in range(ROLES) for i in plane] for plane in PLANE]


def per_device(
    wavlm_hidden,
    whisper_hidden,
    wavlm_qkv,
    whisper_qkv,
    wavlm_out,
    whisper_out,
    frames_valid,
    slot_clip,
    latent,
    wavlm_head,
    whisper_head,
):
    chunks = weight_chunks(wavlm_qkv.T, whisper_qkv.T)
    chunks = [chunks[0]] + [dp_send(chunks[k], k, 0, 0) for k in (1, 2, 3)]
    first, second = shares(chunks, latent)
    first, second = spread_line(first, second)
    pieces = spread_cross(first, second)
    pieces = pieces + [dp_send(x, 0, 0, 1) for x in pieces]
    norm_a, norm_w, mean_a, mean_w = norms(wavlm_hidden, whisper_hidden)

    pooled, lat = attend(frames_valid, slot_clip, pieces, norm_a, norm_w)
    parts = lax.all_to_all(pooled, "role", split_axis=0, concat_axis=0, tiled=True)
    pred_a = jnp.dot(lat[:ROWS], wavlm_head, preferred_element_type=f32)
    pred_w = jnp.dot(lat[:ROWS], whisper_head, preferred_element_type=f32)
    sloped = slopes(
        frames_valid, parts, wavlm_out, whisper_out, mean_a, mean_w, pred_a, pred_w
    )
    slope_own = lax.all_to_all(sloped, "role", split_axis=0, concat_axis=0, tiled=True)
    lat = passed(lat)
    lats = [lat] + [role_send(lat, k) for k in (1, 2, 3)]
    slope_other = dp_send(slope_own, 0, 0, 1)
    halves = outer(lats, slope_own, slope_other)
    arrived = lax.all_to_all(
        halves, "dp", split_axis=0, concat_axis=0, tiled=True, axis_index_groups=PLANE
    )
    summed = lax.all_to_all(
        reduce_parts(arrived),
        ("role", "dp"),
        split_axis=0,
        concat_axis=0,
        tiled=True,
        axis_index_groups=SLICE,
    ).reshape(ROLES, 16, 16, OUT_COLS)
    partner = dp_send(summed, 0, 0, 1)
    held = place(summed, 0)
    grad_a, grad_w = place(partner, 1, held)
    return grad_a.reshape(STU_D, WAVLM_D), grad_w.reshape(STU_D, WHISPER_D)


def solution(mesh):
    in_specs = (
        P("dp", None, None),
        P("dp", None, None),
        P(None, "dp"),
        P(None, "dp"),
        P(),
        P(),
        P(),
        P(),
        P(None, "dp", None, None),
        P(),
        P(),
    )
    out_specs = (P(), P())

    return jax.shard_map(
        per_device, mesh=mesh, in_specs=in_specs, out_specs=out_specs, check_vma=False
    )
```

```python
import jax
import jax.numpy as jnp
from jax import lax
from jax.experimental import pallas as pl
from jax.experimental.pallas import tpu as pltpu
from jax.sharding import PartitionSpec as P


WAVLM_D = 1024
WHISPER_D = 1280
STU_D = 512
HEAD = 64
FRAMES = 512
POOL = 4
POOLED = 128
CLIPS = 64
ROLES = 4
A_HEADS = WAVLM_D // HEAD // ROLES
W_HEADS = WHISPER_D // HEAD // ROLES
A_COLS = A_HEADS * HEAD
W_COLS = W_HEADS * HEAD
OUT_COLS = 640
ROWS = 64

epsilon_norm = 1e-05
epsilon_cos = 1e-06


bf16 = jnp.bfloat16
f32 = jnp.float32


def dp_send(x, dz, dy, dc):
    pairs = []
    for i in range(32):
        z, y, c = i // 8, (i // 2) % 4, i % 2
        target = ((z + dz) % 4) * 8 + ((y + dy) % 4) * 2 + (c + dc) % 2
        pairs.append((i, target))
    return lax.ppermute(x, "dp", pairs)


def role_send(x, k):
    return lax.ppermute(x, "role", [(i, (i + k) % ROLES) for i in range(ROLES)])


def place_of(column):
    return column // 8, (column // 2) % 4, column % 2


def norm_kernel(hidden, norm, mean):
    pool_mat = jnp.where(
        lax.broadcasted_iota(jnp.int32, (32, 128), 1) // POOL
        == lax.broadcasted_iota(jnp.int32, (32, 128), 0),
        1.0 / POOL,
        0.0,
    ).astype(bf16)
    rows = hidden[0].astype(f32)
    centred = rows - jnp.mean(rows, axis=-1, keepdims=True)
    variance = jnp.mean(centred * centred, axis=-1, keepdims=True)
    norm[0] = (centred * lax.rsqrt(variance + epsilon_norm)).astype(bf16)

    @pl.when(pl.program_id(1) == lax.axis_index("role"))
    def _():
        mean[...] = jnp.dot(pool_mat, hidden[0], preferred_element_type=f32)


def norms(hidden):
    width = hidden.shape[-1]
    rows = pl.BlockSpec((1, 128, width), lambda i, j: (i, j, 0))
    return pl.pallas_call(
        norm_kernel,
        grid=(2, 4),
        out_shape=[
            jax.ShapeDtypeStruct(hidden.shape, bf16),
            jax.ShapeDtypeStruct((ROWS, width), f32),
        ],
        in_specs=[rows],
        out_specs=[rows, pl.BlockSpec((32, width), lambda i, j: (i, 0))],
        cost_estimate=pl.CostEstimate(
            flops=30_000_000, bytes_accessed=12_000_000, transcendentals=2048
        ),
    )(hidden)


def chunk_kernel(qkv_a, qkv_w, *refs):
    outs, chunks = refs[:4], refs[4]
    z = place_of(lax.axis_index("dp"))[0]
    for part in range(4):
        for t in range(2):
            lane = (2 * part + t) * 128
            chunks[part, 8 * t : 8 * t + 3] = qkv_a[:, lane : lane + 128].reshape(3, 32, 128)
        for t in range(10):
            if part < 3:
                chunks[part, 3 + t + 3 * (t // 5)] = qkv_w[32 * part : 32 * part + 32, 128 * t : 128 * t + 128]
            else:
                chunks[part, 3 + t + 3 * (t // 5)] = jnp.concatenate(
                    [qkv_w[96:120, 128 * t : 128 * t + 128], jnp.zeros((8, 128), bf16)], axis=0
                )
    for k in range(4):
        outs[k][...] = chunks[(z + k) % 4]


def weight_chunks(qkv_a, qkv_w):
    vmem = pl.BlockSpec(memory_space=pltpu.VMEM)
    return pl.pallas_call(
        chunk_kernel,
        out_shape=[jax.ShapeDtypeStruct((16, 32, 128), bf16)] * 4,
        in_specs=[vmem, vmem],
        out_specs=[vmem] * 4,
        scratch_shapes=[pltpu.VMEM((4, 16, 32, 128), bf16)],
        name="weight_chunks",
    )(qkv_a, qkv_w)


def share_kernel(*refs):
    parts, latent, outs = refs[:4], refs[4], refs[5:]
    role = lax.axis_index("role")
    z, y, c = place_of(lax.axis_index("dp"))
    row = lax.broadcasted_iota(jnp.int32, (32, 128), 0)
    sources = [(role + 4 * ((s - role + 6) % 3)) // 3 for s in range(3)]
    for g in range(4):
        if g < 3:
            column, width = 96 * (2 * y + c) + 32 * g + row, A_COLS
        else:
            column, width = 120 * (2 * y + c) + 32 * z + row, W_COLS
        source = jnp.where(
            column < width, sources[0], jnp.where(column < 2 * width, sources[1], sources[2])
        )
        for half in range(2):
            for group in (g,) if g < 3 else range(3, 8):
                value = parts[0][8 * half + group].astype(f32)
                for k in range(1, 4):
                    other = parts[k][8 * half + group].astype(f32)
                    value = jnp.where(source == (z - k + 4) % 4, other, value)
                outs[half][group] = value.astype(bf16)
    for half in range(2):
        for t in range(4):
            outs[half][8 + t] = latent[half, 0, :, 128 * t : 128 * t + 128]


def shares(parts, latent):
    whole = pl.BlockSpec((16, 32, 128), lambda i: (0, 0, 0))
    half = pl.BlockSpec((12, 32, 128), lambda i: (0, 0, 0))
    return pl.pallas_call(
        share_kernel,
        grid=(1,),
        out_shape=[jax.ShapeDtypeStruct((12, 32, 128), bf16)] * 2,
        in_specs=[whole] * 4
        + [pl.BlockSpec((2, 1, 32, STU_D), lambda i: (0, 0, lax.axis_index("role"), 0))],
        out_specs=[half] * 2,
        name="shares",
    )(*parts, latent)


def spread_line(first, second):
    got = {}
    for k in (1, 3, 2):
        got[k] = dp_send(first, k, 0, 0), dp_send(second, 0, k, 0)
    lines = [first] + [got[k][0] for k in (1, 2, 3)], [second] + [got[k][1] for k in (1, 2, 3)]
    return jnp.stack(lines[0]), jnp.stack(lines[1])


def spread_cross(first, second):
    got = {}
    for k in (1, 3, 2):
        got[k] = dp_send(first, 0, k, 0), dp_send(second, k, 0, 0)
    return (
        [first] + [got[k][0] for k in (1, 2, 3)] + [second] + [got[k][1] for k in (1, 2, 3)]
    )


def pick_latents(slot_clip, rows, slots, out):
    column = lax.axis_index("dp")
    c = column % 2
    base = (column // 2) * 4

    def find(s, carry):
        local = slot_clip[s] - base

        @pl.when((local >= 0) & (local < 4))
        def _():
            slots[jnp.clip(local, 0, 3)] = s

        return carry

    lax.fori_loop(0, CLIPS, find, 0)
    for i in range(4):
        slot = slots[(2 * c + i) % 4]
        h, j = slot // 32, slot % 32
        out[i * 32 : i * 32 + 32] = jnp.concatenate(
            [rows[j, 12 * h + 8 + t] for t in range(4)], axis=1
        )


def attend_kernel(frames_valid, slot_clip, *refs):
    pieces = refs[:16]
    norm_a_hbm, norm_w_hbm, head_a_hbm, head_w_hbm = refs[16:20]
    pooled, lat, pred_a, pred_w = refs[20:24]
    norm_a, norm_w, rows_in, qkv_a, qkv_w, proj, att_a, att_w = refs[24:32]
    score_refs, slots, head_a, head_w, sems = refs[32:34], *refs[34:38]
    copy_head_a = pltpu.make_async_copy(head_a_hbm, head_a, sems.at[4])
    copy_head_w = pltpu.make_async_copy(head_w_hbm, head_w, sems.at[5])
    copy_a = pltpu.make_async_copy(norm_a_hbm, norm_a, sems.at[2])
    copy_w = pltpu.make_async_copy(norm_w_hbm, norm_w, sems.at[3])
    role = lax.axis_index("role")
    column = lax.axis_index("dp")
    z, y, c = place_of(column)
    for first, count, sem in ((0, 3, sems.at[0]), (3, 9, sems.at[1])):
        for n, piece in enumerate(pieces):
            core = (c + n // 8) % 2
            half, far = (n % 8) // 4, n % 4
            for e in range(piece.shape[0]):
                dz, dy = (e, far) if half == 0 else (far, e)
                device = ((z - dz) % 4) * 8 + ((y - dy) % 4) * 2 + core
                pltpu.make_async_copy(
                    piece.at[e, pl.ds(first, count)],
                    rows_in.at[device, pl.ds(12 * half + first, count)],
                    sem,
                ).start()
        if first == 0:
            copy_a.start()
    copy_w.start()
    copy_head_a.start()
    copy_head_w.start()
    wait_a = pltpu.make_async_copy(
        rows_in.at[:, pl.ds(0, 6)], rows_in.at[:, pl.ds(0, 6)], sems.at[0]
    )
    wait_w = pltpu.make_async_copy(
        rows_in.at[:, pl.ds(0, 18)], rows_in.at[:, pl.ds(0, 18)], sems.at[1]
    )
    ones_row = jnp.where(
        lax.broadcasted_iota(jnp.int32, (16, FRAMES), 0) == 0, 1.0, 0.0
    ).astype(bf16)
    pool_mat = jnp.where(
        lax.broadcasted_iota(jnp.int32, (POOLED, FRAMES), 1) // POOL
        == lax.broadcasted_iota(jnp.int32, (POOLED, FRAMES), 0),
        1.0 / POOL,
        0.0,
    ).astype(bf16)
    nt = (((1,), (1,)), ((), ()))
    tn = (((0,), (0,)), ((), ()))

    def put(qkv, kind, clip, head, value):
        scale = jnp.where(kind == 0, HEAD ** (-0.5), 1.0).astype(f32)
        qkv[kind, clip, head] = (value.astype(bf16).astype(f32) * scale).astype(bf16)

    def attention(qkv, att, heads):
        rows = lax.broadcasted_iota(jnp.int32, (16, FRAMES), 0)
        frame = lax.broadcasted_iota(jnp.int32, (16, FRAMES), 1)

        bias = [
            jnp.where(
                (rows == 0) & (frame >= frames_valid[column * 2 + clip]), -1e30, 0.0
            ).astype(bf16)
            for clip in range(2)
        ]

        def score(item, scores):
            clip, head = item % 2, item // 2
            key_x = jnp.concatenate([qkv[1, clip, head], bias[clip]], axis=0)
            query_x = jnp.concatenate([qkv[0, clip, head], ones_row], axis=0)
            value = lax.dot_general(key_x, query_x, tn, preferred_element_type=f32)
            scores[...] = value
            return jnp.max(value, axis=0, keepdims=True)

        def mix(item, scores, top):
            clip, head = item % 2, item // 2
            value_x = jnp.concatenate([qkv[2, clip, head], ones_row], axis=0)
            raised = jnp.exp(scores[...] - top).astype(bf16)
            mixed = jnp.dot(value_x, raised, preferred_element_type=f32)
            total = mixed[HEAD : HEAD + 1]
            att[clip, head] = (mixed[:HEAD] * (1.0 / total)).astype(bf16)

        top = score(0, score_refs[0])
        for item in range(2 * heads):
            if item + 1 < 2 * heads:
                next_top = score(item + 1, score_refs[(item + 1) % 2])
            mix(item, score_refs[item % 2], top)
            top = next_top

    wait_a.wait()
    copy_a.wait()
    for clip in range(2):
        lhs = jnp.concatenate(
            [
                jnp.concatenate(
                    [
                        rows_in[8 * (t // 2) + block, 12 * (t % 2) : 12 * (t % 2) + 3].reshape(
                            96, 128
                        )
                        for block in range(8)
                    ],
                    axis=0,
                )
                for t in range(8)
            ],
            axis=1,
        )
        value = lax.dot_general(lhs, norm_a[clip], nt, preferred_element_type=f32)
        for s in range(3):
            kind = (s - role + 6) % 3
            for h in range(A_HEADS):
                start = s * A_COLS + h * HEAD
                put(qkv_a, kind, clip, h, value[start : start + HEAD])
    attention(qkv_a, att_a, A_HEADS)
    for clip in range(2):
        rows = att_a[clip].reshape(A_COLS, FRAMES)
        mean = lax.dot_general(pool_mat, rows, nt, preferred_element_type=f32).astype(bf16)
        pooled[:, clip * 32 : clip * 32 + 32, :A_COLS] = mean.reshape(ROLES, 32, A_COLS)

    wait_w.wait()
    copy_w.wait()
    copy_head_a.wait()
    copy_head_w.wait()
    pick_latents(slot_clip, rows_in, slots, lat)
    pred_a[...] = jnp.dot(lat[:ROWS], head_a[...], preferred_element_type=f32)
    pred_w[...] = jnp.dot(lat[:ROWS], head_w[...], preferred_element_type=f32)
    for clip in range(2):
        lhs = jnp.concatenate(
            [
                jnp.concatenate(
                    [
                        rows_in[8 * zs + block, 12 * (t // 5) + 3 + t % 5]
                        for block in range(8)
                        for zs in range(4)
                    ],
                    axis=0,
                )
                for t in range(10)
            ],
            axis=1,
        )
        proj[...] = lax.dot_general(lhs, norm_w[clip], nt, preferred_element_type=f32)
        for s in range(3):
            kind = (s - role + 6) % 3
            for h in range(W_HEADS):
                start = s * W_COLS + h * HEAD
                parts = []
                while start < s * W_COLS + (h + 1) * HEAD:
                    block, inner = start // 120, start % 120
                    take = min(120 - inner, s * W_COLS + (h + 1) * HEAD - start)
                    parts.append(proj[block * 128 + inner : block * 128 + inner + take])
                    start += take
                value = parts[0] if len(parts) == 1 else jnp.concatenate(parts, axis=0)
                put(qkv_w, kind, clip, h, value)
    attention(qkv_w, att_w, W_HEADS)
    for clip in range(2):
        rows = att_w[clip].reshape(W_COLS, FRAMES)
        mean = lax.dot_general(pool_mat, rows, nt, preferred_element_type=f32).astype(bf16)
        mean = jnp.concatenate([mean, jnp.zeros((POOLED, 64), bf16)], axis=1)
        pooled[:, clip * 32 : clip * 32 + 32, A_COLS:] = mean.reshape(ROLES, 32, 384)


def attend(frames_valid, slot_clip, pieces, norm_a, norm_w, head_a, head_w):
    vmem = pl.BlockSpec(memory_space=pltpu.VMEM)
    return pl.pallas_call(
        attend_kernel,
        out_shape=[
            jax.ShapeDtypeStruct((ROLES, ROWS, OUT_COLS), bf16),
            jax.ShapeDtypeStruct((2 * ROWS, STU_D), bf16),
            jax.ShapeDtypeStruct((ROWS, WAVLM_D), f32),
            jax.ShapeDtypeStruct((ROWS, WHISPER_D), f32),
        ],
        in_specs=[pl.BlockSpec(memory_space=pltpu.SMEM)] * 2
        + [pl.BlockSpec(memory_space=pl.ANY)] * 20,
        out_specs=[vmem] * 4,
        scratch_shapes=[
            pltpu.VMEM((2, FRAMES, WAVLM_D), bf16),
            pltpu.VMEM((2, FRAMES, WHISPER_D), bf16),
            pltpu.VMEM((32, 24, 32, 128), bf16),
            pltpu.VMEM((3, 2, A_HEADS, HEAD, FRAMES), bf16),
            pltpu.VMEM((3, 2, W_HEADS, HEAD, FRAMES), bf16),
            pltpu.VMEM((1024, FRAMES), f32),
            pltpu.VMEM((2, A_HEADS, HEAD, FRAMES), bf16),
            pltpu.VMEM((2, W_HEADS, HEAD, FRAMES), bf16),
            pltpu.VMEM((FRAMES, FRAMES), f32),
            pltpu.VMEM((FRAMES, FRAMES), f32),
            pltpu.SMEM((4,), jnp.int32),
            pltpu.VMEM((STU_D, WAVLM_D), bf16),
            pltpu.VMEM((STU_D, WHISPER_D), bf16),
            pltpu.SemaphoreType.DMA((6,)),
        ],
        cost_estimate=pl.CostEstimate(
            flops=8_000_000_000, bytes_accessed=12_000_000, transcendentals=5_000_000
        ),
        name="attend",
    )(frames_valid, slot_clip, *pieces, norm_a, norm_w, head_a, head_w)


def slope_kernel(frames_valid, parts, out_a_hbm, out_w_hbm, *refs):
    mean_a, mean_w, pred_a, pred_w, grouped, out_a, out_w, sems = refs
    copy_a = pltpu.make_async_copy(out_a_hbm, out_a, sems.at[0])
    copy_w = pltpu.make_async_copy(out_w_hbm, out_w, sems.at[1])
    copy_a.start()
    copy_w.start()
    role = lax.axis_index("role")
    clip = lax.axis_index("dp") * 2
    row = lax.broadcasted_iota(jnp.int32, (ROWS, 1), 0)
    valid = jnp.where(row < 32, frames_valid[clip], frames_valid[clip + 1]) // POOL
    keep = (row % 32 + role * 32) < valid

    def slope_of(mean, copy, out, pred, cols, first):
        width = mean.shape[-1]
        attended = jnp.concatenate(
            [parts[r, :, first : first + cols] for r in range(ROLES)], axis=1
        )
        copy.wait()
        total = mean[...] + jnp.dot(attended, out[...], preferred_element_type=f32)
        target = total.astype(bf16).astype(f32)
        predicted = pred[...]
        pred_sq = jnp.sum(predicted * predicted, axis=-1, keepdims=True) + epsilon_cos
        targ_sq = jnp.sum(target * target, axis=-1, keepdims=True) + epsilon_cos
        pred_norm = jnp.sqrt(pred_sq)
        both = pred_norm * jnp.sqrt(targ_sq)
        cosine = jnp.sum(predicted * target, axis=-1, keepdims=True) / both
        slope = (cosine / (pred_norm * pred_norm)) * predicted - target / both
        slope = slope + (predicted - target) * (1.0 / width)
        return jnp.where(keep, slope, 0.0).astype(bf16)

    slope_a = slope_of(mean_a, copy_a, out_a, pred_a, A_COLS, 0)
    for g in range(ROLES):
        grouped[g, :, :A_COLS] = slope_a[:, g * A_COLS : (g + 1) * A_COLS]
    slope_w = slope_of(mean_w, copy_w, out_w, pred_w, W_COLS, A_COLS)
    for g in range(ROLES):
        grouped[g, :, A_COLS:] = jnp.concatenate(
            [slope_w[:, g * W_COLS : (g + 1) * W_COLS], jnp.zeros((ROWS, 64), bf16)], axis=1
        )


def slopes(frames_valid, parts, out_a, out_w, mean_a, mean_w, pred_a, pred_w):
    vmem = pl.BlockSpec(memory_space=pltpu.VMEM)
    hbm = pl.BlockSpec(memory_space=pl.ANY)
    return pl.pallas_call(
        slope_kernel,
        out_shape=jax.ShapeDtypeStruct((ROLES, ROWS, OUT_COLS), bf16),
        in_specs=[pl.BlockSpec(memory_space=pltpu.SMEM), vmem, hbm, hbm] + [vmem] * 4,
        out_specs=vmem,
        scratch_shapes=[
            pltpu.VMEM((WAVLM_D, WAVLM_D), bf16),
            pltpu.VMEM((WHISPER_D, WHISPER_D), bf16),
            pltpu.SemaphoreType.DMA((2,)),
        ],
        name="slopes",
    )(frames_valid, parts, out_a, out_w, mean_a, mean_w, pred_a, pred_w)


def outer_kernel(*refs):
    lats, own, other, out = refs[:4], refs[4], refs[5], refs[6]
    role = lax.axis_index("role")
    start = pl.multiple_of((lax.axis_index("dp") % 2) * 256, 256)
    lat = jnp.concatenate([lats[k][:, pl.ds(start, 256)] for k in range(ROLES)], axis=0)
    rows = []
    for k in range(ROLES):
        source = (role - k + ROLES) % ROLES
        rows += [own[source], other[source]]
    grad = lax.dot_general(
        lat, jnp.concatenate(rows, axis=0), (((0,), (0,)), ((), ())), preferred_element_type=f32
    )
    out[...] = grad.reshape(16, 16, OUT_COLS)


def outer(lats, own, other):
    vmem = pl.BlockSpec(memory_space=pltpu.VMEM)
    return pl.pallas_call(
        outer_kernel,
        out_shape=jax.ShapeDtypeStruct((16, 16, OUT_COLS), f32),
        in_specs=[vmem] * 6,
        out_specs=vmem,
        name="outer",
    )(*lats, own, other)


def sum_kernel(x, out):
    total = jnp.sum(x[...], axis=0).astype(bf16)
    out[...] = jnp.broadcast_to(total[None], out.shape)


def reduce_parts(x):
    vmem = pl.BlockSpec(memory_space=pltpu.VMEM)
    return pl.pallas_call(
        sum_kernel,
        out_shape=jax.ShapeDtypeStruct((64, 16, OUT_COLS), bf16),
        in_specs=[vmem],
        out_specs=vmem,
        name="reduce_parts",
    )(x)


def place_kernel(piece, *refs):
    out_a, out_w = refs[-2:]
    blocks = []
    for g in range(ROLES):
        block = piece[g].reshape(128, OUT_COLS).astype(f32)
        out_a[0, :, g * A_COLS : (g + 1) * A_COLS] = block[:, :A_COLS]
        blocks.append(block[:, A_COLS : A_COLS + W_COLS])
    out_w[0] = jnp.concatenate(blocks, axis=1)


def place(piece, partner, held=()):
    half = lambda: (lax.axis_index("dp") + partner) % 2
    hbm = pl.BlockSpec(memory_space=pl.ANY)
    return pl.pallas_call(
        place_kernel,
        grid=(2,),
        out_shape=[
            jax.ShapeDtypeStruct((2, 256, WAVLM_D), f32),
            jax.ShapeDtypeStruct((2, 256, WHISPER_D), f32),
        ],
        in_specs=[pl.BlockSpec((ROLES, 8, 16, OUT_COLS), lambda i: (0, i, 0, 0))]
        + [hbm] * len(held),
        out_specs=[
            pl.BlockSpec((1, 128, WAVLM_D), lambda i: (half(), i, 0)),
            pl.BlockSpec((1, 128, WHISPER_D), lambda i: (half(), i, 0)),
        ],
        input_output_aliases={1: 0, 2: 1} if held else {},
        name="place_partner" if partner else "place_own",
    )(piece, *held)


PLANE = [[z * 8 + y * 2 + c for z in range(4) for y in range(4)] for c in range(2)]
SLICE = [[r * 32 + i for r in range(ROLES) for i in plane] for plane in PLANE]


def per_device(
    wavlm_hidden,
    whisper_hidden,
    wavlm_qkv,
    whisper_qkv,
    wavlm_out,
    whisper_out,
    frames_valid,
    slot_clip,
    latent,
    wavlm_head,
    whisper_head,
):
    chunks = weight_chunks(wavlm_qkv.T, whisper_qkv.T)
    chunks = [chunks[0]] + [dp_send(chunks[k], k, 0, 0) for k in (1, 2, 3)]
    first, second = shares(chunks, latent)
    first, second = spread_line(first, second)
    pieces = spread_cross(first, second)
    pieces = pieces + [dp_send(x, 0, 0, 1) for x in pieces]
    norm_a, mean_a = norms(wavlm_hidden)
    norm_w, mean_w = norms(whisper_hidden)

    pooled, lat, pred_a, pred_w = attend(
        frames_valid, slot_clip, pieces, norm_a, norm_w, wavlm_head, whisper_head
    )
    parts = lax.all_to_all(pooled, "role", split_axis=0, concat_axis=0, tiled=True)
    lats = [lat] + [role_send(lat, k) for k in (1, 2, 3)]
    sloped = slopes(
        frames_valid, parts, wavlm_out, whisper_out, mean_a, mean_w, pred_a, pred_w
    )
    slope_own = lax.all_to_all(sloped, "role", split_axis=0, concat_axis=0, tiled=True)
    slope_other = dp_send(slope_own, 0, 0, 1)
    halves = outer(lats, slope_own, slope_other)
    arrived = lax.all_to_all(
        halves, "dp", split_axis=0, concat_axis=0, tiled=True, axis_index_groups=PLANE
    )
    summed = lax.all_to_all(
        reduce_parts(arrived),
        ("role", "dp"),
        split_axis=0,
        concat_axis=0,
        tiled=True,
        axis_index_groups=SLICE,
    ).reshape(ROLES, 16, 16, OUT_COLS)
    partner = dp_send(summed, 0, 0, 1)
    held = place(summed, 0)
    grad_a, grad_w = place(partner, 1, held)
    return grad_a.reshape(STU_D, WAVLM_D), grad_w.reshape(STU_D, WHISPER_D)


def solution(mesh):
    in_specs = (
        P("dp", None, None),
        P("dp", None, None),
        P(None, "dp"),
        P(None, "dp"),
        P(),
        P(),
        P(),
        P(),
        P(None, "dp", None, None),
        P(),
        P(),
    )
    out_specs = (P(), P())

    return jax.shard_map(
        per_device, mesh=mesh, in_specs=in_specs, out_specs=out_specs, check_vma=False
    )
```

```python
import jax
import jax.numpy as jnp
from jax import lax
from jax.experimental import pallas as pl
from jax.experimental.pallas import tpu as pltpu
from jax.sharding import PartitionSpec as P


WAVLM_D = 1024
WHISPER_D = 1280
STU_D = 512
HEAD = 64
FRAMES = 512
POOL = 4
POOLED = 128
CLIPS = 64
ROLES = 4
A_HEADS = WAVLM_D // HEAD // ROLES
W_HEADS = WHISPER_D // HEAD // ROLES
A_COLS = A_HEADS * HEAD
W_COLS = W_HEADS * HEAD
OUT_COLS = 640
ROWS = 64

epsilon_norm = 1e-05
epsilon_cos = 1e-06


bf16 = jnp.bfloat16
f32 = jnp.float32


def dp_send(x, dz, dy, dc):
    pairs = []
    for i in range(32):
        z, y, c = i // 8, (i // 2) % 4, i % 2
        target = ((z + dz) % 4) * 8 + ((y + dy) % 4) * 2 + (c + dc) % 2
        pairs.append((i, target))
    return lax.ppermute(x, "dp", pairs)


def role_send(x, k):
    return lax.ppermute(x, "role", [(i, (i + k) % ROLES) for i in range(ROLES)])


def place_of(column):
    return column // 8, (column // 2) % 4, column % 2


def norm_kernel(hidden, norm, mean):
    pool_mat = jnp.where(
        lax.broadcasted_iota(jnp.int32, (32, 128), 1) // POOL
        == lax.broadcasted_iota(jnp.int32, (32, 128), 0),
        1.0 / POOL,
        0.0,
    ).astype(bf16)
    rows = hidden[0].astype(f32)
    centred = rows - jnp.mean(rows, axis=-1, keepdims=True)
    variance = jnp.mean(centred * centred, axis=-1, keepdims=True)
    norm[0] = (centred * lax.rsqrt(variance + epsilon_norm)).astype(bf16)

    quarter = hidden[0, pl.ds(pl.multiple_of(lax.axis_index("role") * 128, 128), 128), :]
    mean[...] = jnp.dot(pool_mat, quarter, preferred_element_type=f32)


def norms(hidden):
    width = hidden.shape[-1]
    rows = pl.BlockSpec((1, FRAMES, width), lambda i: (i, 0, 0))
    return pl.pallas_call(
        norm_kernel,
        grid=(2,),
        out_shape=[
            jax.ShapeDtypeStruct(hidden.shape, bf16),
            jax.ShapeDtypeStruct((ROWS, width), f32),
        ],
        in_specs=[rows],
        out_specs=[rows, pl.BlockSpec((32, width), lambda i: (i, 0))],
        cost_estimate=pl.CostEstimate(
            flops=30_000_000, bytes_accessed=12_000_000, transcendentals=2048
        ),
    )(hidden)


def chunk_kernel(qkv_a, qkv_w, *refs):
    outs, chunks = refs[:4], refs[4]
    z = place_of(lax.axis_index("dp"))[0]
    for part in range(4):
        for t in range(2):
            lane = (2 * part + t) * 128
            chunks[part, 8 * t : 8 * t + 3] = qkv_a[:, lane : lane + 128].reshape(3, 32, 128)
        for t in range(10):
            if part < 3:
                chunks[part, 3 + t + 3 * (t // 5)] = qkv_w[32 * part : 32 * part + 32, 128 * t : 128 * t + 128]
            else:
                chunks[part, 3 + t + 3 * (t // 5)] = jnp.concatenate(
                    [qkv_w[96:120, 128 * t : 128 * t + 128], jnp.zeros((8, 128), bf16)], axis=0
                )
    for k in range(4):
        outs[k][...] = chunks[(z + k) % 4]


def weight_chunks(qkv_a, qkv_w):
    vmem = pl.BlockSpec(memory_space=pltpu.VMEM)
    return pl.pallas_call(
        chunk_kernel,
        out_shape=[jax.ShapeDtypeStruct((16, 32, 128), bf16)] * 4,
        in_specs=[vmem, vmem],
        out_specs=[vmem] * 4,
        scratch_shapes=[pltpu.VMEM((4, 16, 32, 128), bf16)],
        name="weight_chunks",
    )(qkv_a, qkv_w)


def share_kernel(*refs):
    parts, latent, outs = refs[:4], refs[4], refs[5:]
    role = lax.axis_index("role")
    z, y, c = place_of(lax.axis_index("dp"))
    row = lax.broadcasted_iota(jnp.int32, (32, 128), 0)
    sources = [(role + 4 * ((s - role + 6) % 3)) // 3 for s in range(3)]
    for g in range(4):
        if g < 3:
            column, width = 96 * (2 * y + c) + 32 * g + row, A_COLS
        else:
            column, width = 120 * (2 * y + c) + 32 * z + row, W_COLS
        source = jnp.where(
            column < width, sources[0], jnp.where(column < 2 * width, sources[1], sources[2])
        )
        for half in range(2):
            for group in (g,) if g < 3 else range(3, 8):
                value = parts[0][8 * half + group].astype(f32)
                for k in range(1, 4):
                    other = parts[k][8 * half + group].astype(f32)
                    value = jnp.where(source == (z - k + 4) % 4, other, value)
                outs[half][group] = value.astype(bf16)
    for half in range(2):
        for t in range(4):
            outs[half][8 + t] = latent[half, 0, :, 128 * t : 128 * t + 128]


def shares(parts, latent):
    whole = pl.BlockSpec((16, 32, 128), lambda i: (0, 0, 0))
    half = pl.BlockSpec((12, 32, 128), lambda i: (0, 0, 0))
    return pl.pallas_call(
        share_kernel,
        grid=(1,),
        out_shape=[jax.ShapeDtypeStruct((12, 32, 128), bf16)] * 2,
        in_specs=[whole] * 4
        + [pl.BlockSpec((2, 1, 32, STU_D), lambda i: (0, 0, lax.axis_index("role"), 0))],
        out_specs=[half] * 2,
        name="shares",
    )(*parts, latent)


def spread_line(first, second):
    got = {}
    for k in (1, 3, 2):
        got[k] = dp_send(first, k, 0, 0), dp_send(second, 0, k, 0)
    lines = [first] + [got[k][0] for k in (1, 2, 3)], [second] + [got[k][1] for k in (1, 2, 3)]
    return jnp.stack(lines[0]), jnp.stack(lines[1])


def spread_cross(first, second):
    got = {}
    for k in (1, 3, 2):
        got[k] = dp_send(first, 0, k, 0), dp_send(second, k, 0, 0)
    return (
        [first] + [got[k][0] for k in (1, 2, 3)] + [second] + [got[k][1] for k in (1, 2, 3)]
    )


def pick_latents(slot_clip, rows, slots, out):
    column = lax.axis_index("dp")
    c = column % 2
    base = (column // 2) * 4

    def find(s, carry):
        local = slot_clip[s] - base

        @pl.when((local >= 0) & (local < 4))
        def _():
            slots[jnp.clip(local, 0, 3)] = s

        return carry

    lax.fori_loop(0, CLIPS, find, 0)
    for i in range(4):
        slot = slots[(2 * c + i) % 4]
        h, j = slot // 32, slot % 32
        out[i * 32 : i * 32 + 32] = jnp.concatenate(
            [rows[j, 12 * h + 8 + t] for t in range(4)], axis=1
        )


def attend_kernel(frames_valid, slot_clip, *refs):
    pieces = refs[:16]
    norm_a_hbm, norm_w_hbm, head_a_hbm, head_w_hbm = refs[16:20]
    outs, lat, pred_a, pred_w = refs[20:24], *refs[24:27]
    norm_a, norm_w, rows_in, qkv_a, qkv_w, proj, att_a, att_w = refs[27:35]
    score_refs, slots, head_a, head_w, pooled, sems = refs[35:37], *refs[37:42]
    copy_head_a = pltpu.make_async_copy(head_a_hbm, head_a, sems.at[4])
    copy_head_w = pltpu.make_async_copy(head_w_hbm, head_w, sems.at[5])
    copy_a = pltpu.make_async_copy(norm_a_hbm, norm_a, sems.at[2])
    copy_w = pltpu.make_async_copy(norm_w_hbm, norm_w, sems.at[3])
    role = lax.axis_index("role")
    column = lax.axis_index("dp")
    z, y, c = place_of(column)
    for first, count, sem in ((0, 3, sems.at[0]), (3, 9, sems.at[1])):
        for n, piece in enumerate(pieces):
            core = (c + n // 8) % 2
            half, far = (n % 8) // 4, n % 4
            for e in range(piece.shape[0]):
                dz, dy = (e, far) if half == 0 else (far, e)
                device = ((z - dz) % 4) * 8 + ((y - dy) % 4) * 2 + core
                pltpu.make_async_copy(
                    piece.at[e, pl.ds(first, count)],
                    rows_in.at[device, pl.ds(12 * half + first, count)],
                    sem,
                ).start()
        if first == 0:
            copy_a.start()
    copy_w.start()
    copy_head_a.start()
    copy_head_w.start()
    wait_a = pltpu.make_async_copy(
        rows_in.at[:, pl.ds(0, 6)], rows_in.at[:, pl.ds(0, 6)], sems.at[0]
    )
    wait_w = pltpu.make_async_copy(
        rows_in.at[:, pl.ds(0, 18)], rows_in.at[:, pl.ds(0, 18)], sems.at[1]
    )
    ones_row = jnp.where(
        lax.broadcasted_iota(jnp.int32, (16, FRAMES), 0) == 0, 1.0, 0.0
    ).astype(bf16)
    pool_mat = jnp.where(
        lax.broadcasted_iota(jnp.int32, (POOLED, FRAMES), 1) // POOL
        == lax.broadcasted_iota(jnp.int32, (POOLED, FRAMES), 0),
        1.0 / POOL,
        0.0,
    ).astype(bf16)
    nt = (((1,), (1,)), ((), ()))
    tn = (((0,), (0,)), ((), ()))

    def put(qkv, kind, clip, head, value):
        scale = jnp.where(kind == 0, HEAD ** (-0.5), 1.0).astype(f32)
        qkv[kind, clip, head] = (value.astype(bf16).astype(f32) * scale).astype(bf16)

    def attention(qkv, att, heads):
        rows = lax.broadcasted_iota(jnp.int32, (16, FRAMES), 0)
        frame = lax.broadcasted_iota(jnp.int32, (16, FRAMES), 1)

        bias = [
            jnp.where(
                (rows == 0) & (frame >= frames_valid[column * 2 + clip]), -1e30, 0.0
            ).astype(bf16)
            for clip in range(2)
        ]

        def score(item, scores):
            clip, head = item % 2, item // 2
            key_x = jnp.concatenate([qkv[1, clip, head], bias[clip]], axis=0)
            query_x = jnp.concatenate([qkv[0, clip, head], ones_row], axis=0)
            value = lax.dot_general(key_x, query_x, tn, preferred_element_type=f32)
            scores[...] = value
            return jnp.max(value, axis=0, keepdims=True)

        def mix(item, scores, top):
            clip, head = item % 2, item // 2
            value_x = jnp.concatenate([qkv[2, clip, head], ones_row], axis=0)
            raised = jnp.exp(scores[...] - top).astype(bf16)
            mixed = jnp.dot(value_x, raised, preferred_element_type=f32)
            total = mixed[HEAD : HEAD + 1]
            att[clip, head] = (mixed[:HEAD] * (1.0 / total)).astype(bf16)

        top = score(0, score_refs[0])
        for item in range(2 * heads):
            if item + 1 < 2 * heads:
                next_top = score(item + 1, score_refs[(item + 1) % 2])
            mix(item, score_refs[item % 2], top)
            top = next_top

    wait_a.wait()
    copy_a.wait()
    for clip in range(2):
        lhs = jnp.concatenate(
            [
                jnp.concatenate(
                    [
                        rows_in[8 * (t // 2) + block, 12 * (t % 2) : 12 * (t % 2) + 3].reshape(
                            96, 128
                        )
                        for block in range(8)
                    ],
                    axis=0,
                )
                for t in range(8)
            ],
            axis=1,
        )
        value = lax.dot_general(lhs, norm_a[clip], nt, preferred_element_type=f32)
        for s in range(3):
            kind = (s - role + 6) % 3
            for h in range(A_HEADS):
                start = s * A_COLS + h * HEAD
                put(qkv_a, kind, clip, h, value[start : start + HEAD])
    attention(qkv_a, att_a, A_HEADS)
    for clip in range(2):
        rows = att_a[clip].reshape(A_COLS, FRAMES)
        mean = lax.dot_general(pool_mat, rows, nt, preferred_element_type=f32).astype(bf16)
        pooled[:, clip * 32 : clip * 32 + 32, :A_COLS] = mean.reshape(ROLES, 32, A_COLS)

    wait_w.wait()
    copy_w.wait()
    copy_head_a.wait()
    copy_head_w.wait()
    pick_latents(slot_clip, rows_in, slots, lat)
    pred_a[...] = jnp.dot(lat[:ROWS], head_a[...], preferred_element_type=f32)
    pred_w[...] = jnp.dot(lat[:ROWS], head_w[...], preferred_element_type=f32)
    for clip in range(2):
        lhs = jnp.concatenate(
            [
                jnp.concatenate(
                    [
                        rows_in[8 * zs + block, 12 * (t // 5) + 3 + t % 5]
                        for block in range(8)
                        for zs in range(4)
                    ],
                    axis=0,
                )
                for t in range(10)
            ],
            axis=1,
        )
        proj[...] = lax.dot_general(lhs, norm_w[clip], nt, preferred_element_type=f32)
        for s in range(3):
            kind = (s - role + 6) % 3
            for h in range(W_HEADS):
                start = s * W_COLS + h * HEAD
                parts = []
                while start < s * W_COLS + (h + 1) * HEAD:
                    block, inner = start // 120, start % 120
                    take = min(120 - inner, s * W_COLS + (h + 1) * HEAD - start)
                    parts.append(proj[block * 128 + inner : block * 128 + inner + take])
                    start += take
                value = parts[0] if len(parts) == 1 else jnp.concatenate(parts, axis=0)
                put(qkv_w, kind, clip, h, value)
    attention(qkv_w, att_w, W_HEADS)
    for clip in range(2):
        rows = att_w[clip].reshape(W_COLS, FRAMES)
        mean = lax.dot_general(pool_mat, rows, nt, preferred_element_type=f32).astype(bf16)
        mean = jnp.concatenate([mean, jnp.zeros((POOLED, 64), bf16)], axis=1)
        pooled[:, clip * 32 : clip * 32 + 32, A_COLS:] = mean.reshape(ROLES, 32, 384)
    for k in range(ROLES):
        outs[k][...] = pooled[(role + k) % ROLES]


def attend(frames_valid, slot_clip, pieces, norm_a, norm_w, head_a, head_w):
    vmem = pl.BlockSpec(memory_space=pltpu.VMEM)
    return pl.pallas_call(
        attend_kernel,
        out_shape=[jax.ShapeDtypeStruct((ROWS, OUT_COLS), bf16)] * ROLES
        + [
            jax.ShapeDtypeStruct((2 * ROWS, STU_D), bf16),
            jax.ShapeDtypeStruct((ROWS, WAVLM_D), f32),
            jax.ShapeDtypeStruct((ROWS, WHISPER_D), f32),
        ],
        in_specs=[pl.BlockSpec(memory_space=pltpu.SMEM)] * 2
        + [pl.BlockSpec(memory_space=pl.ANY)] * 20,
        out_specs=[vmem] * 7,
        scratch_shapes=[
            pltpu.VMEM((2, FRAMES, WAVLM_D), bf16),
            pltpu.VMEM((2, FRAMES, WHISPER_D), bf16),
            pltpu.VMEM((32, 24, 32, 128), bf16),
            pltpu.VMEM((3, 2, A_HEADS, HEAD, FRAMES), bf16),
            pltpu.VMEM((3, 2, W_HEADS, HEAD, FRAMES), bf16),
            pltpu.VMEM((1024, FRAMES), f32),
            pltpu.VMEM((2, A_HEADS, HEAD, FRAMES), bf16),
            pltpu.VMEM((2, W_HEADS, HEAD, FRAMES), bf16),
            pltpu.VMEM((FRAMES, FRAMES), f32),
            pltpu.VMEM((FRAMES, FRAMES), f32),
            pltpu.SMEM((4,), jnp.int32),
            pltpu.VMEM((STU_D, WAVLM_D), bf16),
            pltpu.VMEM((STU_D, WHISPER_D), bf16),
            pltpu.VMEM((ROLES, ROWS, OUT_COLS), bf16),
            pltpu.SemaphoreType.DMA((6,)),
        ],
        cost_estimate=pl.CostEstimate(
            flops=8_000_000_000, bytes_accessed=12_000_000, transcendentals=5_000_000
        ),
        name="attend",
    )(frames_valid, slot_clip, *pieces, norm_a, norm_w, head_a, head_w)


def slope_kernel(frames_valid, *refs):
    arrived = refs[:4]
    out_a_hbm, out_w_hbm, mean_a, mean_w, pred_a, pred_w = refs[4:10]
    outs, parts, grouped, out_a, out_w, sems = refs[10:14], *refs[14:19]
    copies = []
    for source, target in ((out_a_hbm, out_a), (out_w_hbm, out_w)):
        for start in range(0, source.shape[0], 256):
            rows = pl.ds(start, 256)
            copies.append(
                pltpu.make_async_copy(source.at[rows], target.at[rows], sems.at[len(copies)])
            )
            copies[-1].start()
    role = lax.axis_index("role")
    clip = lax.axis_index("dp") * 2
    for k in range(ROLES):
        parts[(role - k + ROLES) % ROLES] = arrived[k][...]
    row = lax.broadcasted_iota(jnp.int32, (ROWS, 1), 0)
    valid = jnp.where(row < 32, frames_valid[clip], frames_valid[clip + 1]) // POOL
    keep = (row % 32 + role * 32) < valid

    def slope_of(mean, waits, out, pred, cols, first):
        width = mean.shape[-1]
        attended = jnp.concatenate(
            [parts[r, :, first : first + cols] for r in range(ROLES)], axis=1
        )
        total = mean[...]
        for i, copy in enumerate(waits):
            copy.wait()
            rows = slice(256 * i, 256 * i + 256)
            total = total + jnp.dot(attended[:, rows], out[rows], preferred_element_type=f32)
        target = total.astype(bf16).astype(f32)
        predicted = pred[...]
        pred_sq = jnp.sum(predicted * predicted, axis=-1, keepdims=True) + epsilon_cos
        targ_sq = jnp.sum(target * target, axis=-1, keepdims=True) + epsilon_cos
        pred_norm = jnp.sqrt(pred_sq)
        both = pred_norm * jnp.sqrt(targ_sq)
        cosine = jnp.sum(predicted * target, axis=-1, keepdims=True) / both
        slope = (cosine / (pred_norm * pred_norm)) * predicted - target / both
        slope = slope + (predicted - target) * (1.0 / width)
        return jnp.where(keep, slope, 0.0).astype(bf16)

    slope_a = slope_of(mean_a, copies[:4], out_a, pred_a, A_COLS, 0)
    for g in range(ROLES):
        grouped[g, :, :A_COLS] = slope_a[:, g * A_COLS : (g + 1) * A_COLS]
    slope_w = slope_of(mean_w, copies[4:], out_w, pred_w, W_COLS, A_COLS)
    for g in range(ROLES):
        grouped[g, :, A_COLS:] = jnp.concatenate(
            [slope_w[:, g * W_COLS : (g + 1) * W_COLS], jnp.zeros((ROWS, 64), bf16)], axis=1
        )
    for k in range(ROLES):
        outs[k][...] = grouped[(role + k) % ROLES]


def slopes(frames_valid, parts, out_a, out_w, mean_a, mean_w, pred_a, pred_w):
    vmem = pl.BlockSpec(memory_space=pltpu.VMEM)
    return pl.pallas_call(
        slope_kernel,
        out_shape=[jax.ShapeDtypeStruct((ROWS, OUT_COLS), bf16)] * ROLES,
        in_specs=[pl.BlockSpec(memory_space=pltpu.SMEM)]
        + [vmem] * 4
        + [pl.BlockSpec(memory_space=pl.ANY)] * 2
        + [vmem] * 4,
        out_specs=[vmem] * ROLES,
        scratch_shapes=[pltpu.VMEM((ROLES, ROWS, OUT_COLS), bf16)] * 2
        + [
            pltpu.VMEM((WAVLM_D, WAVLM_D), bf16),
            pltpu.VMEM((WHISPER_D, WHISPER_D), bf16),
            pltpu.SemaphoreType.DMA((9,)),
        ],
        name="slopes",
    )(frames_valid, *parts, out_a, out_w, mean_a, mean_w, pred_a, pred_w)


def outer_kernel(*refs):
    lats, own, other, out = refs[:4], refs[4:8], refs[8:12], refs[12]
    start = pl.multiple_of((lax.axis_index("dp") % 2) * 256, 256)
    lat = jnp.concatenate([lats[k][:, pl.ds(start, 256)] for k in range(ROLES)], axis=0)
    rows = []
    for k in range(ROLES):
        rows += [own[k][...], other[k][...]]
    grad = lax.dot_general(
        lat, jnp.concatenate(rows, axis=0), (((0,), (0,)), ((), ())), preferred_element_type=f32
    )
    out[...] = grad.reshape(16, 16, OUT_COLS)


def outer(lats, own, other):
    vmem = pl.BlockSpec(memory_space=pltpu.VMEM)
    return pl.pallas_call(
        outer_kernel,
        out_shape=jax.ShapeDtypeStruct((16, 16, OUT_COLS), f32),
        in_specs=[vmem] * 12,
        out_specs=vmem,
        name="outer",
    )(*lats, *own, *other)


def sum_kernel(x, out):
    total = jnp.sum(x[...], axis=0).astype(bf16)
    out[...] = jnp.broadcast_to(total[None], out.shape)


def reduce_parts(x):
    vmem = pl.BlockSpec(memory_space=pltpu.VMEM)
    return pl.pallas_call(
        sum_kernel,
        out_shape=jax.ShapeDtypeStruct((64, 16, OUT_COLS), bf16),
        in_specs=[vmem],
        out_specs=vmem,
        name="reduce_parts",
    )(x)


def place_kernel(piece, *refs):
    out_a, out_w = refs[-2:]
    blocks = []
    step = pl.program_id(0) * 8
    for g in range(ROLES):
        block = piece[g, pl.ds(step, 8)].reshape(128, OUT_COLS).astype(f32)
        out_a[0, :, g * A_COLS : (g + 1) * A_COLS] = block[:, :A_COLS]
        blocks.append(block[:, A_COLS : A_COLS + W_COLS])
    out_w[0] = jnp.concatenate(blocks, axis=1)


def place(piece, partner, held=()):
    half = lambda: (lax.axis_index("dp") + partner) % 2
    hbm = pl.BlockSpec(memory_space=pl.ANY)
    return pl.pallas_call(
        place_kernel,
        grid=(2,),
        out_shape=[
            jax.ShapeDtypeStruct((2, 256, WAVLM_D), f32),
            jax.ShapeDtypeStruct((2, 256, WHISPER_D), f32),
        ],
        in_specs=[pl.BlockSpec(memory_space=pltpu.VMEM)]
        + [hbm] * len(held),
        out_specs=[
            pl.BlockSpec((1, 128, WAVLM_D), lambda i: (half(), i, 0)),
            pl.BlockSpec((1, 128, WHISPER_D), lambda i: (half(), i, 0)),
        ],
        input_output_aliases={1: 0, 2: 1} if held else {},
        name="place_partner" if partner else "place_own",
    )(piece, *held)


PLANE = [[z * 8 + y * 2 + c for z in range(4) for y in range(4)] for c in range(2)]
SLICE = [[r * 32 + i for r in range(ROLES) for i in plane] for plane in PLANE]


def per_device(
    wavlm_hidden,
    whisper_hidden,
    wavlm_qkv,
    whisper_qkv,
    wavlm_out,
    whisper_out,
    frames_valid,
    slot_clip,
    latent,
    wavlm_head,
    whisper_head,
):
    chunks = weight_chunks(wavlm_qkv.T, whisper_qkv.T)
    chunks = [chunks[0]] + [dp_send(chunks[k], k, 0, 0) for k in (1, 2, 3)]
    first, second = shares(chunks, latent)
    first, second = spread_line(first, second)
    pieces = spread_cross(first, second)
    pieces = pieces + [dp_send(x, 0, 0, 1) for x in pieces]
    norm_a, mean_a = norms(wavlm_hidden)
    norm_w, mean_w = norms(whisper_hidden)

    *pooled, lat, pred_a, pred_w = attend(
        frames_valid, slot_clip, pieces, norm_a, norm_w, wavlm_head, whisper_head
    )
    parts = [pooled[0]] + [role_send(pooled[k], k) for k in (1, 2, 3)]
    lats = [lat] + [role_send(lat, k) for k in (1, 2, 3)]
    sloped = slopes(
        frames_valid, parts, wavlm_out, whisper_out, mean_a, mean_w, pred_a, pred_w
    )
    slope_own = [sloped[0]] + [role_send(sloped[k], k) for k in (1, 2, 3)]
    slope_other = [dp_send(x, 0, 0, 1) for x in slope_own]
    halves = outer(lats, slope_own, slope_other)
    arrived = lax.all_to_all(
        halves, "dp", split_axis=0, concat_axis=0, tiled=True, axis_index_groups=PLANE
    )
    summed = lax.all_to_all(
        reduce_parts(arrived),
        ("role", "dp"),
        split_axis=0,
        concat_axis=0,
        tiled=True,
        axis_index_groups=SLICE,
    ).reshape(ROLES, 16, 16, OUT_COLS)
    partner = dp_send(summed, 0, 0, 1)
    held = place(summed, 0)
    grad_a, grad_w = place(partner, 1, held)
    return grad_a.reshape(STU_D, WAVLM_D), grad_w.reshape(STU_D, WHISPER_D)


def solution(mesh):
    in_specs = (
        P("dp", None, None),
        P("dp", None, None),
        P(None, "dp"),
        P(None, "dp"),
        P(),
        P(),
        P(),
        P(),
        P(None, "dp", None, None),
        P(),
        P(),
    )
    out_specs = (P(), P())

    return jax.shard_map(
        per_device, mesh=mesh, in_specs=in_specs, out_specs=out_specs, check_vma=False
    )
```

```python
import jax
import jax.numpy as jnp
from jax import lax
from jax.experimental import pallas as pl
from jax.experimental.pallas import tpu as pltpu
from jax.sharding import PartitionSpec as P


WAVLM_D = 1024
WHISPER_D = 1280
STU_D = 512
HEAD = 64
FRAMES = 512
POOL = 4
POOLED = 128
CLIPS = 64
ROLES = 4
A_HEADS = WAVLM_D // HEAD // ROLES
W_HEADS = WHISPER_D // HEAD // ROLES
A_COLS = A_HEADS * HEAD
W_COLS = W_HEADS * HEAD
OUT_COLS = 640
ROWS = 64

epsilon_norm = 1e-05
epsilon_cos = 1e-06


bf16 = jnp.bfloat16
f32 = jnp.float32


def dp_send(x, dz, dy, dc):
    pairs = []
    for i in range(32):
        z, y, c = i // 8, (i // 2) % 4, i % 2
        target = ((z + dz) % 4) * 8 + ((y + dy) % 4) * 2 + (c + dc) % 2
        pairs.append((i, target))
    return lax.ppermute(x, "dp", pairs)


def role_send(x, k):
    return lax.ppermute(x, "role", [(i, (i + k) % ROLES) for i in range(ROLES)])


def near(*arrays):
    return [pltpu.with_memory_space_constraint(x, pltpu.VMEM) for x in arrays]


def place_of(column):
    return column // 8, (column // 2) % 4, column % 2


def norm_kernel(hidden, norm, mean):
    pool_mat = jnp.where(
        lax.broadcasted_iota(jnp.int32, (32, 128), 1) // POOL
        == lax.broadcasted_iota(jnp.int32, (32, 128), 0),
        1.0 / POOL,
        0.0,
    ).astype(bf16)
    rows = hidden[0].astype(f32)
    centred = rows - jnp.mean(rows, axis=-1, keepdims=True)
    variance = jnp.mean(centred * centred, axis=-1, keepdims=True)
    norm[0] = (centred * lax.rsqrt(variance + epsilon_norm)).astype(bf16)

    quarter = hidden[0, pl.ds(pl.multiple_of(lax.axis_index("role") * 128, 128), 128), :]
    mean[...] = jnp.dot(pool_mat, quarter, preferred_element_type=f32)


def norms(hidden):
    width = hidden.shape[-1]
    rows = pl.BlockSpec((1, FRAMES, width), lambda i: (i, 0, 0))
    return pl.pallas_call(
        norm_kernel,
        grid=(2,),
        out_shape=[
            jax.ShapeDtypeStruct(hidden.shape, bf16),
            jax.ShapeDtypeStruct((ROWS, width), f32),
        ],
        in_specs=[rows],
        out_specs=[rows, pl.BlockSpec((32, width), lambda i: (i, 0))],
        cost_estimate=pl.CostEstimate(
            flops=30_000_000, bytes_accessed=12_000_000, transcendentals=2048
        ),
    )(hidden)


def chunk_kernel(qkv_a, qkv_w, *refs):
    outs, chunks = refs[:4], refs[4]
    z = place_of(lax.axis_index("dp"))[0]
    for part in range(4):
        for t in range(2):
            lane = (2 * part + t) * 128
            chunks[part, 8 * t : 8 * t + 3] = qkv_a[:, lane : lane + 128].reshape(3, 32, 128)
        for t in range(10):
            if part < 3:
                chunks[part, 3 + t + 3 * (t // 5)] = qkv_w[32 * part : 32 * part + 32, 128 * t : 128 * t + 128]
            else:
                chunks[part, 3 + t + 3 * (t // 5)] = jnp.concatenate(
                    [qkv_w[96:120, 128 * t : 128 * t + 128], jnp.zeros((8, 128), bf16)], axis=0
                )
    for k in range(4):
        outs[k][...] = chunks[(z + k) % 4]


def weight_chunks(qkv_a, qkv_w):
    vmem = pl.BlockSpec(memory_space=pltpu.VMEM)
    return pl.pallas_call(
        chunk_kernel,
        out_shape=[pltpu.VMEM((16, 32, 128), bf16)] * 4,
        in_specs=[vmem, vmem],
        out_specs=[vmem] * 4,
        scratch_shapes=[pltpu.VMEM((4, 16, 32, 128), bf16)],
        name="weight_chunks",
    )(qkv_a, qkv_w)


def share_kernel(*refs):
    parts, latent, outs = refs[:4], refs[4], refs[5:]
    role = lax.axis_index("role")
    z, y, c = place_of(lax.axis_index("dp"))
    row = lax.broadcasted_iota(jnp.int32, (32, 128), 0)
    sources = [(role + 4 * ((s - role + 6) % 3)) // 3 for s in range(3)]
    for g in range(4):
        if g < 3:
            column, width = 96 * (2 * y + c) + 32 * g + row, A_COLS
        else:
            column, width = 120 * (2 * y + c) + 32 * z + row, W_COLS
        source = jnp.where(
            column < width, sources[0], jnp.where(column < 2 * width, sources[1], sources[2])
        )
        for half in range(2):
            for group in (g,) if g < 3 else range(3, 8):
                value = parts[0][8 * half + group].astype(f32)
                for k in range(1, 4):
                    other = parts[k][8 * half + group].astype(f32)
                    value = jnp.where(source == (z - k + 4) % 4, other, value)
                outs[half][group] = value.astype(bf16)
    for half in range(2):
        for t in range(4):
            outs[half][8 + t] = latent[half, 0, :, 128 * t : 128 * t + 128]


def shares(parts, latent):
    half = pl.BlockSpec((12, 32, 128), lambda i: (0, 0, 0))
    return pl.pallas_call(
        share_kernel,
        grid=(1,),
        out_shape=[jax.ShapeDtypeStruct((12, 32, 128), bf16)] * 2,
        in_specs=[pl.BlockSpec(memory_space=pltpu.VMEM)] * 4
        + [pl.BlockSpec((2, 1, 32, STU_D), lambda i: (0, 0, lax.axis_index("role"), 0))],
        out_specs=[half] * 2,
        name="shares",
    )(*near(*parts), latent)


def spread_line(first, second):
    got = {}
    for k in (1, 3, 2):
        got[k] = dp_send(first, k, 0, 0), dp_send(second, 0, k, 0)
    lines = [first] + [got[k][0] for k in (1, 2, 3)], [second] + [got[k][1] for k in (1, 2, 3)]
    return jnp.stack(lines[0]), jnp.stack(lines[1])


def spread_cross(first, second):
    got = {}
    for k in (1, 3, 2):
        got[k] = dp_send(first, 0, k, 0), dp_send(second, k, 0, 0)
    return (
        [first] + [got[k][0] for k in (1, 2, 3)] + [second] + [got[k][1] for k in (1, 2, 3)]
    )


def pick_latents(slot_clip, rows, slots, out):
    column = lax.axis_index("dp")
    c = column % 2
    base = (column // 2) * 4

    def find(s, carry):
        local = slot_clip[s] - base

        @pl.when((local >= 0) & (local < 4))
        def _():
            slots[jnp.clip(local, 0, 3)] = s

        return carry

    lax.fori_loop(0, CLIPS, find, 0)
    for i in range(4):
        slot = slots[(2 * c + i) % 4]
        h, j = slot // 32, slot % 32
        out[i * 32 : i * 32 + 32] = jnp.concatenate(
            [rows[j, 12 * h + 8 + t] for t in range(4)], axis=1
        )


def attend_kernel(frames_valid, slot_clip, *refs):
    pieces = refs[:16]
    norm_a_hbm, norm_w_hbm, head_a_hbm, head_w_hbm = refs[16:20]
    outs, lat, pred_a, pred_w = refs[20:24], *refs[24:27]
    norm_a, norm_w, rows_in, qkv_a, qkv_w, proj, att_a, att_w = refs[27:35]
    score_refs, slots, head_a, head_w, pooled, sems = refs[35:37], *refs[37:42]
    copy_head_a = pltpu.make_async_copy(head_a_hbm, head_a, sems.at[4])
    copy_head_w = pltpu.make_async_copy(head_w_hbm, head_w, sems.at[5])
    copy_a = pltpu.make_async_copy(norm_a_hbm, norm_a, sems.at[2])
    copy_w = pltpu.make_async_copy(norm_w_hbm, norm_w, sems.at[3])
    role = lax.axis_index("role")
    column = lax.axis_index("dp")
    z, y, c = place_of(column)
    for first, count, sem in ((0, 3, sems.at[0]), (3, 9, sems.at[1])):
        for n, piece in enumerate(pieces):
            core = (c + n // 8) % 2
            half, far = (n % 8) // 4, n % 4
            for e in range(piece.shape[0]):
                dz, dy = (e, far) if half == 0 else (far, e)
                device = ((z - dz) % 4) * 8 + ((y - dy) % 4) * 2 + core
                pltpu.make_async_copy(
                    piece.at[e, pl.ds(first, count)],
                    rows_in.at[device, pl.ds(12 * half + first, count)],
                    sem,
                ).start()
        if first == 0:
            copy_a.start()
    copy_w.start()
    copy_head_a.start()
    copy_head_w.start()
    wait_a = pltpu.make_async_copy(
        rows_in.at[:, pl.ds(0, 6)], rows_in.at[:, pl.ds(0, 6)], sems.at[0]
    )
    wait_w = pltpu.make_async_copy(
        rows_in.at[:, pl.ds(0, 18)], rows_in.at[:, pl.ds(0, 18)], sems.at[1]
    )
    ones_row = jnp.where(
        lax.broadcasted_iota(jnp.int32, (16, FRAMES), 0) == 0, 1.0, 0.0
    ).astype(bf16)
    pool_mat = jnp.where(
        lax.broadcasted_iota(jnp.int32, (POOLED, FRAMES), 1) // POOL
        == lax.broadcasted_iota(jnp.int32, (POOLED, FRAMES), 0),
        1.0 / POOL,
        0.0,
    ).astype(bf16)
    nt = (((1,), (1,)), ((), ()))
    tn = (((0,), (0,)), ((), ()))

    def put(qkv, kind, clip, head, value):
        scale = jnp.where(kind == 0, HEAD ** (-0.5), 1.0).astype(f32)
        qkv[kind, clip, head] = (value.astype(bf16).astype(f32) * scale).astype(bf16)

    def attention(qkv, att, heads):
        rows = lax.broadcasted_iota(jnp.int32, (16, FRAMES), 0)
        frame = lax.broadcasted_iota(jnp.int32, (16, FRAMES), 1)

        bias = [
            jnp.where(
                (rows == 0) & (frame >= frames_valid[column * 2 + clip]), -1e30, 0.0
            ).astype(bf16)
            for clip in range(2)
        ]

        def score(item, scores):
            clip, head = item % 2, item // 2
            key_x = jnp.concatenate([qkv[1, clip, head], bias[clip]], axis=0)
            query_x = jnp.concatenate([qkv[0, clip, head], ones_row], axis=0)
            value = lax.dot_general(key_x, query_x, tn, preferred_element_type=f32)
            scores[...] = value
            return jnp.max(value, axis=0, keepdims=True)

        def mix(item, scores, top):
            clip, head = item % 2, item // 2
            value_x = jnp.concatenate([qkv[2, clip, head], ones_row], axis=0)
            raised = jnp.exp(scores[...] - top).astype(bf16)
            mixed = jnp.dot(value_x, raised, preferred_element_type=f32)
            total = mixed[HEAD : HEAD + 1]
            att[clip, head] = (mixed[:HEAD] * (1.0 / total)).astype(bf16)

        top = score(0, score_refs[0])
        for item in range(2 * heads):
            if item + 1 < 2 * heads:
                next_top = score(item + 1, score_refs[(item + 1) % 2])
            mix(item, score_refs[item % 2], top)
            top = next_top

    wait_a.wait()
    copy_a.wait()
    for clip in range(2):
        lhs = jnp.concatenate(
            [
                jnp.concatenate(
                    [
                        rows_in[8 * (t // 2) + block, 12 * (t % 2) : 12 * (t % 2) + 3].reshape(
                            96, 128
                        )
                        for block in range(8)
                    ],
                    axis=0,
                )
                for t in range(8)
            ],
            axis=1,
        )
        value = lax.dot_general(lhs, norm_a[clip], nt, preferred_element_type=f32)
        for s in range(3):
            kind = (s - role + 6) % 3
            for h in range(A_HEADS):
                start = s * A_COLS + h * HEAD
                put(qkv_a, kind, clip, h, value[start : start + HEAD])
    attention(qkv_a, att_a, A_HEADS)
    for clip in range(2):
        rows = att_a[clip].reshape(A_COLS, FRAMES)
        mean = lax.dot_general(pool_mat, rows, nt, preferred_element_type=f32).astype(bf16)
        pooled[:, clip * 32 : clip * 32 + 32, :A_COLS] = mean.reshape(ROLES, 32, A_COLS)

    wait_w.wait()
    copy_w.wait()
    copy_head_a.wait()
    copy_head_w.wait()
    pick_latents(slot_clip, rows_in, slots, lat)
    pred_a[...] = jnp.dot(lat[:ROWS], head_a[...], preferred_element_type=f32)
    pred_w[...] = jnp.dot(lat[:ROWS], head_w[...], preferred_element_type=f32)
    for clip in range(2):
        lhs = jnp.concatenate(
            [
                jnp.concatenate(
                    [
                        rows_in[8 * zs + block, 12 * (t // 5) + 3 + t % 5]
                        for block in range(8)
                        for zs in range(4)
                    ],
                    axis=0,
                )
                for t in range(10)
            ],
            axis=1,
        )
        proj[...] = lax.dot_general(lhs, norm_w[clip], nt, preferred_element_type=f32)
        for s in range(3):
            kind = (s - role + 6) % 3
            for h in range(W_HEADS):
                start = s * W_COLS + h * HEAD
                parts = []
                while start < s * W_COLS + (h + 1) * HEAD:
                    block, inner = start // 120, start % 120
                    take = min(120 - inner, s * W_COLS + (h + 1) * HEAD - start)
                    parts.append(proj[block * 128 + inner : block * 128 + inner + take])
                    start += take
                value = parts[0] if len(parts) == 1 else jnp.concatenate(parts, axis=0)
                put(qkv_w, kind, clip, h, value)
    attention(qkv_w, att_w, W_HEADS)
    for clip in range(2):
        rows = att_w[clip].reshape(W_COLS, FRAMES)
        mean = lax.dot_general(pool_mat, rows, nt, preferred_element_type=f32).astype(bf16)
        mean = jnp.concatenate([mean, jnp.zeros((POOLED, 64), bf16)], axis=1)
        pooled[:, clip * 32 : clip * 32 + 32, A_COLS:] = mean.reshape(ROLES, 32, 384)
    for k in range(ROLES):
        outs[k][...] = pooled[(role + k) % ROLES]


def attend(frames_valid, slot_clip, pieces, norm_a, norm_w, head_a, head_w):
    vmem = pl.BlockSpec(memory_space=pltpu.VMEM)
    return pl.pallas_call(
        attend_kernel,
        out_shape=[pltpu.VMEM((ROWS, OUT_COLS), bf16)] * ROLES
        + [
            pltpu.VMEM((2 * ROWS, STU_D), bf16),
            pltpu.VMEM((ROWS, WAVLM_D), f32),
            pltpu.VMEM((ROWS, WHISPER_D), f32),
        ],
        in_specs=[pl.BlockSpec(memory_space=pltpu.SMEM)] * 2
        + [pl.BlockSpec(memory_space=pl.ANY)] * 20,
        out_specs=[vmem] * 7,
        scratch_shapes=[
            pltpu.VMEM((2, FRAMES, WAVLM_D), bf16),
            pltpu.VMEM((2, FRAMES, WHISPER_D), bf16),
            pltpu.VMEM((32, 24, 32, 128), bf16),
            pltpu.VMEM((3, 2, A_HEADS, HEAD, FRAMES), bf16),
            pltpu.VMEM((3, 2, W_HEADS, HEAD, FRAMES), bf16),
            pltpu.VMEM((1024, FRAMES), f32),
            pltpu.VMEM((2, A_HEADS, HEAD, FRAMES), bf16),
            pltpu.VMEM((2, W_HEADS, HEAD, FRAMES), bf16),
            pltpu.VMEM((FRAMES, FRAMES), f32),
            pltpu.VMEM((FRAMES, FRAMES), f32),
            pltpu.SMEM((4,), jnp.int32),
            pltpu.VMEM((STU_D, WAVLM_D), bf16),
            pltpu.VMEM((STU_D, WHISPER_D), bf16),
            pltpu.VMEM((ROLES, ROWS, OUT_COLS), bf16),
            pltpu.SemaphoreType.DMA((6,)),
        ],
        cost_estimate=pl.CostEstimate(
            flops=8_000_000_000, bytes_accessed=12_000_000, transcendentals=5_000_000
        ),
        name="attend",
    )(frames_valid, slot_clip, *pieces, norm_a, norm_w, head_a, head_w)


def slope_kernel(frames_valid, *refs):
    arrived = refs[:4]
    out_a_hbm, out_w_hbm, mean_a, mean_w, pred_a, pred_w = refs[4:10]
    outs, parts, grouped, out_a, out_w, sems = refs[10:14], *refs[14:19]
    copies = []
    for source, target in ((out_a_hbm, out_a), (out_w_hbm, out_w)):
        for start in range(0, source.shape[0], 256):
            rows = pl.ds(start, 256)
            copies.append(
                pltpu.make_async_copy(source.at[rows], target.at[rows], sems.at[len(copies)])
            )
            copies[-1].start()
    role = lax.axis_index("role")
    clip = lax.axis_index("dp") * 2
    for k in range(ROLES):
        parts[(role - k + ROLES) % ROLES] = arrived[k][...]
    row = lax.broadcasted_iota(jnp.int32, (ROWS, 1), 0)
    valid = jnp.where(row < 32, frames_valid[clip], frames_valid[clip + 1]) // POOL
    keep = (row % 32 + role * 32) < valid

    def slope_of(mean, waits, out, pred, cols, first):
        width = mean.shape[-1]
        attended = jnp.concatenate(
            [parts[r, :, first : first + cols] for r in range(ROLES)], axis=1
        )
        total = mean[...]
        for i, copy in enumerate(waits):
            copy.wait()
            rows = slice(256 * i, 256 * i + 256)
            total = total + jnp.dot(attended[:, rows], out[rows], preferred_element_type=f32)
        target = total.astype(bf16).astype(f32)
        predicted = pred[...]
        pred_sq = jnp.sum(predicted * predicted, axis=-1, keepdims=True) + epsilon_cos
        targ_sq = jnp.sum(target * target, axis=-1, keepdims=True) + epsilon_cos
        pred_norm = jnp.sqrt(pred_sq)
        both = pred_norm * jnp.sqrt(targ_sq)
        cosine = jnp.sum(predicted * target, axis=-1, keepdims=True) / both
        slope = (cosine / (pred_norm * pred_norm)) * predicted - target / both
        slope = slope + (predicted - target) * (1.0 / width)
        return jnp.where(keep, slope, 0.0).astype(bf16)

    slope_a = slope_of(mean_a, copies[:4], out_a, pred_a, A_COLS, 0)
    for g in range(ROLES):
        grouped[g, :, :A_COLS] = slope_a[:, g * A_COLS : (g + 1) * A_COLS]
    slope_w = slope_of(mean_w, copies[4:], out_w, pred_w, W_COLS, A_COLS)
    for g in range(ROLES):
        grouped[g, :, A_COLS:] = jnp.concatenate(
            [slope_w[:, g * W_COLS : (g + 1) * W_COLS], jnp.zeros((ROWS, 64), bf16)], axis=1
        )
    for k in range(ROLES):
        outs[k][...] = grouped[(role + k) % ROLES]


def slopes(frames_valid, parts, out_a, out_w, mean_a, mean_w, pred_a, pred_w):
    vmem = pl.BlockSpec(memory_space=pltpu.VMEM)
    return pl.pallas_call(
        slope_kernel,
        out_shape=[pltpu.VMEM((ROWS, OUT_COLS), bf16)] * ROLES,
        in_specs=[pl.BlockSpec(memory_space=pltpu.SMEM)]
        + [vmem] * 4
        + [pl.BlockSpec(memory_space=pl.ANY)] * 2
        + [vmem] * 4,
        out_specs=[vmem] * ROLES,
        scratch_shapes=[pltpu.VMEM((ROLES, ROWS, OUT_COLS), bf16)] * 2
        + [
            pltpu.VMEM((WAVLM_D, WAVLM_D), bf16),
            pltpu.VMEM((WHISPER_D, WHISPER_D), bf16),
            pltpu.SemaphoreType.DMA((9,)),
        ],
        name="slopes",
    )(frames_valid, *near(*parts), out_a, out_w, *near(mean_a, mean_w, pred_a, pred_w))


def outer_kernel(*refs):
    lats, own, other, out = refs[:4], refs[4:8], refs[8:12], refs[12]
    start = pl.multiple_of((lax.axis_index("dp") % 2) * 256, 256)
    lat = jnp.concatenate([lats[k][:, pl.ds(start, 256)] for k in range(ROLES)], axis=0)
    rows = []
    for k in range(ROLES):
        rows += [own[k][...], other[k][...]]
    grad = lax.dot_general(
        lat, jnp.concatenate(rows, axis=0), (((0,), (0,)), ((), ())), preferred_element_type=f32
    )
    out[...] = grad.reshape(16, 16, OUT_COLS)


def outer(lats, own, other):
    vmem = pl.BlockSpec(memory_space=pltpu.VMEM)
    return pl.pallas_call(
        outer_kernel,
        out_shape=pltpu.VMEM((16, 16, OUT_COLS), f32),
        in_specs=[vmem] * 12,
        out_specs=vmem,
        name="outer",
    )(*near(*lats, *own, *other))


def sum_kernel(x, out):
    total = jnp.sum(x[...], axis=0).astype(bf16)
    out[...] = jnp.broadcast_to(total[None], out.shape)


def reduce_parts(x):
    vmem = pl.BlockSpec(memory_space=pltpu.VMEM)
    return pl.pallas_call(
        sum_kernel,
        out_shape=pltpu.VMEM((64, 16, OUT_COLS), bf16),
        in_specs=[vmem],
        out_specs=vmem,
        name="reduce_parts",
    )(*near(x))


def place_kernel(piece, *refs):
    out_a, out_w = refs[-2:]
    blocks = []
    step = pl.program_id(0) * 8
    for g in range(ROLES):
        block = piece[g, pl.ds(step, 8)].reshape(128, OUT_COLS).astype(f32)
        out_a[0, :, g * A_COLS : (g + 1) * A_COLS] = block[:, :A_COLS]
        blocks.append(block[:, A_COLS : A_COLS + W_COLS])
    out_w[0] = jnp.concatenate(blocks, axis=1)


def place(piece, partner, held=()):
    half = lambda: (lax.axis_index("dp") + partner) % 2
    hbm = pl.BlockSpec(memory_space=pl.ANY)
    return pl.pallas_call(
        place_kernel,
        grid=(2,),
        out_shape=[
            jax.ShapeDtypeStruct((2, 256, WAVLM_D), f32),
            jax.ShapeDtypeStruct((2, 256, WHISPER_D), f32),
        ],
        in_specs=[pl.BlockSpec(memory_space=pltpu.VMEM)]
        + [hbm] * len(held),
        out_specs=[
            pl.BlockSpec((1, 128, WAVLM_D), lambda i: (half(), i, 0)),
            pl.BlockSpec((1, 128, WHISPER_D), lambda i: (half(), i, 0)),
        ],
        input_output_aliases={1: 0, 2: 1} if held else {},
        name="place_partner" if partner else "place_own",
    )(*near(piece), *held)


PLANE = [[z * 8 + y * 2 + c for z in range(4) for y in range(4)] for c in range(2)]
SLICE = [[r * 32 + i for r in range(ROLES) for i in plane] for plane in PLANE]


def per_device(
    wavlm_hidden,
    whisper_hidden,
    wavlm_qkv,
    whisper_qkv,
    wavlm_out,
    whisper_out,
    frames_valid,
    slot_clip,
    latent,
    wavlm_head,
    whisper_head,
):
    chunks = weight_chunks(wavlm_qkv.T, whisper_qkv.T)
    chunks = [chunks[0]] + [dp_send(chunks[k], k, 0, 0) for k in (1, 2, 3)]
    first, second = shares(chunks, latent)
    first, second = spread_line(first, second)
    pieces = spread_cross(first, second)
    pieces = pieces + [dp_send(x, 0, 0, 1) for x in pieces]
    norm_a, mean_a = norms(wavlm_hidden)
    norm_w, mean_w = norms(whisper_hidden)

    *pooled, lat, pred_a, pred_w = attend(
        frames_valid, slot_clip, pieces, norm_a, norm_w, wavlm_head, whisper_head
    )
    parts = [pooled[0]] + [role_send(pooled[k], k) for k in (1, 2, 3)]
    lats = [lat] + [role_send(lat, k) for k in (1, 2, 3)]
    sloped = slopes(
        frames_valid, parts, wavlm_out, whisper_out, mean_a, mean_w, pred_a, pred_w
    )
    slope_own = [sloped[0]] + [role_send(sloped[k], k) for k in (1, 2, 3)]
    slope_other = [dp_send(x, 0, 0, 1) for x in slope_own]
    halves = outer(lats, slope_own, slope_other)
    arrived = lax.all_to_all(
        halves, "dp", split_axis=0, concat_axis=0, tiled=True, axis_index_groups=PLANE
    )
    summed = lax.all_to_all(
        reduce_parts(arrived),
        ("role", "dp"),
        split_axis=0,
        concat_axis=0,
        tiled=True,
        axis_index_groups=SLICE,
    ).reshape(ROLES, 16, 16, OUT_COLS)
    partner = dp_send(summed, 0, 0, 1)
    held = place(summed, 0)
    grad_a, grad_w = place(partner, 1, held)
    return grad_a.reshape(STU_D, WAVLM_D), grad_w.reshape(STU_D, WHISPER_D)


def solution(mesh):
    in_specs = (
        P("dp", None, None),
        P("dp", None, None),
        P(None, "dp"),
        P(None, "dp"),
        P(),
        P(),
        P(),
        P(),
        P(None, "dp", None, None),
        P(),
        P(),
    )
    out_specs = (P(), P())

    return jax.shard_map(
        per_device, mesh=mesh, in_specs=in_specs, out_specs=out_specs, check_vma=False
    )
```

```python
import jax
import jax.numpy as jnp
from jax import lax
from jax.experimental import pallas as pl
from jax.experimental.pallas import tpu as pltpu
from jax.sharding import PartitionSpec as P


WAVLM_D = 1024
WHISPER_D = 1280
STU_D = 512
HEAD = 64
FRAMES = 512
POOL = 4
POOLED = 128
CLIPS = 64
ROLES = 4
A_HEADS = WAVLM_D // HEAD // ROLES
W_HEADS = WHISPER_D // HEAD // ROLES
A_COLS = A_HEADS * HEAD
W_COLS = W_HEADS * HEAD
OUT_COLS = 640
ROWS = 64

epsilon_norm = 1e-05
epsilon_cos = 1e-06


bf16 = jnp.bfloat16
f32 = jnp.float32


def dp_send(x, dz, dy, dc):
    pairs = []
    for i in range(32):
        z, y, c = i // 8, (i // 2) % 4, i % 2
        target = ((z + dz) % 4) * 8 + ((y + dy) % 4) * 2 + (c + dc) % 2
        pairs.append((i, target))
    return lax.ppermute(x, "dp", pairs)


def role_send(x, k):
    return lax.ppermute(x, "role", [(i, (i + k) % ROLES) for i in range(ROLES)])


def near(*arrays):
    return [pltpu.with_memory_space_constraint(x, pltpu.VMEM) for x in arrays]


def place_of(column):
    return column // 8, (column // 2) % 4, column % 2


def norm_kernel(hidden, norm, mean):
    pool_mat = jnp.where(
        lax.broadcasted_iota(jnp.int32, (32, 128), 1) // POOL
        == lax.broadcasted_iota(jnp.int32, (32, 128), 0),
        1.0 / POOL,
        0.0,
    ).astype(bf16)
    rows = hidden[0].astype(f32)
    centred = rows - jnp.mean(rows, axis=-1, keepdims=True)
    variance = jnp.mean(centred * centred, axis=-1, keepdims=True)
    norm[0] = (centred * lax.rsqrt(variance + epsilon_norm)).astype(bf16)

    quarter = hidden[0, pl.ds(pl.multiple_of(lax.axis_index("role") * 128, 128), 128), :]
    mean[...] = jnp.dot(pool_mat, quarter, preferred_element_type=f32)


def norms(hidden):
    width = hidden.shape[-1]
    rows = pl.BlockSpec((1, FRAMES, width), lambda i: (i, 0, 0))
    return pl.pallas_call(
        norm_kernel,
        grid=(2,),
        out_shape=[
            jax.ShapeDtypeStruct(hidden.shape, bf16),
            jax.ShapeDtypeStruct((ROWS, width), f32),
        ],
        in_specs=[rows],
        out_specs=[rows, pl.BlockSpec((32, width), lambda i: (i, 0))],
        cost_estimate=pl.CostEstimate(
            flops=30_000_000, bytes_accessed=12_000_000, transcendentals=2048
        ),
    )(hidden)


def chunk_kernel(qkv_a, qkv_w, *refs):
    outs, chunks = refs[:4], refs[4]
    z = place_of(lax.axis_index("dp"))[0]
    for part in range(4):
        for t in range(2):
            lane = (2 * part + t) * 128
            chunks[part, 8 * t : 8 * t + 3] = qkv_a[:, lane : lane + 128].reshape(3, 32, 128)
        for t in range(10):
            if part < 3:
                chunks[part, 3 + t + 3 * (t // 5)] = qkv_w[32 * part : 32 * part + 32, 128 * t : 128 * t + 128]
            else:
                chunks[part, 3 + t + 3 * (t // 5)] = jnp.concatenate(
                    [qkv_w[96:120, 128 * t : 128 * t + 128], jnp.zeros((8, 128), bf16)], axis=0
                )
    for k in range(4):
        outs[k][...] = chunks[(z + k) % 4]


def weight_chunks(qkv_a, qkv_w):
    vmem = pl.BlockSpec(memory_space=pltpu.VMEM)
    return pl.pallas_call(
        chunk_kernel,
        out_shape=[pltpu.VMEM((16, 32, 128), bf16)] * 4,
        in_specs=[vmem, vmem],
        out_specs=[vmem] * 4,
        scratch_shapes=[pltpu.VMEM((4, 16, 32, 128), bf16)],
        name="weight_chunks",
    )(qkv_a, qkv_w)


def share_kernel(*refs):
    parts, latent, outs = refs[:4], refs[4], refs[5:]
    role = lax.axis_index("role")
    z, y, c = place_of(lax.axis_index("dp"))
    row = lax.broadcasted_iota(jnp.int32, (32, 128), 0)
    sources = [(role + 4 * ((s - role + 6) % 3)) // 3 for s in range(3)]
    for g in range(4):
        if g < 3:
            column, width = 96 * (2 * y + c) + 32 * g + row, A_COLS
        else:
            column, width = 120 * (2 * y + c) + 32 * z + row, W_COLS
        source = jnp.where(
            column < width, sources[0], jnp.where(column < 2 * width, sources[1], sources[2])
        )
        for half in range(2):
            for group in (g,) if g < 3 else range(3, 8):
                value = parts[0][8 * half + group].astype(f32)
                for k in range(1, 4):
                    other = parts[k][8 * half + group].astype(f32)
                    value = jnp.where(source == (z - k + 4) % 4, other, value)
                outs[half][group] = value.astype(bf16)
    for half in range(2):
        for t in range(4):
            outs[half][8 + t] = latent[half, 0, :, 128 * t : 128 * t + 128]


def shares(parts, latent):
    half = pl.BlockSpec((12, 32, 128), lambda i: (0, 0, 0))
    return pl.pallas_call(
        share_kernel,
        grid=(1,),
        out_shape=[jax.ShapeDtypeStruct((12, 32, 128), bf16)] * 2,
        in_specs=[pl.BlockSpec(memory_space=pltpu.VMEM)] * 4
        + [pl.BlockSpec((2, 1, 32, STU_D), lambda i: (0, 0, lax.axis_index("role"), 0))],
        out_specs=[half] * 2,
        name="shares",
    )(*near(*parts), latent)


def spread_line(first, second):
    got = {}
    for k in (1, 3, 2):
        got[k] = dp_send(first, k, 0, 0), dp_send(second, 0, k, 0)
    lines = [first] + [got[k][0] for k in (1, 2, 3)], [second] + [got[k][1] for k in (1, 2, 3)]
    return jnp.stack(lines[0]), jnp.stack(lines[1])


def spread_cross(first, second):
    got = {}
    for k in (1, 3, 2):
        got[k] = dp_send(first, 0, k, 0), dp_send(second, k, 0, 0)
    return (
        [first] + [got[k][0] for k in (1, 2, 3)] + [second] + [got[k][1] for k in (1, 2, 3)]
    )


def pick_latents(slot_clip, rows, slots, out):
    column = lax.axis_index("dp")
    c = column % 2
    base = (column // 2) * 4

    def find(s, carry):
        local = slot_clip[s] - base

        @pl.when((local >= 0) & (local < 4))
        def _():
            slots[jnp.clip(local, 0, 3)] = s

        return carry

    lax.fori_loop(0, CLIPS, find, 0)
    for i in range(4):
        slot = slots[(2 * c + i) % 4]
        h, j = slot // 32, slot % 32
        out[i * 32 : i * 32 + 32] = jnp.concatenate(
            [rows[j, 12 * h + 8 + t] for t in range(4)], axis=1
        )


def attend_kernel(frames_valid, slot_clip, *refs):
    pieces = refs[:16]
    norm_a_hbm, norm_w_hbm, head_a_hbm, head_w_hbm = refs[16:20]
    outs, lat, pred_a, pred_w = refs[20:24], *refs[24:27]
    norm_a, norm_w, rows_in, qkv_a, qkv_w, proj, att_a, att_w = refs[27:35]
    score_refs, slots, head_a, head_w, pooled, sems = refs[35:37], *refs[37:42]
    copy_head_a = pltpu.make_async_copy(head_a_hbm, head_a, sems.at[4])
    copy_head_w = pltpu.make_async_copy(head_w_hbm, head_w, sems.at[5])
    copy_a = pltpu.make_async_copy(norm_a_hbm, norm_a, sems.at[2])
    copy_w = pltpu.make_async_copy(norm_w_hbm, norm_w, sems.at[3])
    role = lax.axis_index("role")
    column = lax.axis_index("dp")
    z, y, c = place_of(column)
    for first, count, sem in ((0, 3, sems.at[0]), (3, 9, sems.at[1])):
        for n, piece in enumerate(pieces):
            core = (c + n // 8) % 2
            half, far = (n % 8) // 4, n % 4
            for e in range(piece.shape[0]):
                dz, dy = (e, far) if half == 0 else (far, e)
                device = ((z - dz) % 4) * 8 + ((y - dy) % 4) * 2 + core
                pltpu.make_async_copy(
                    piece.at[e, pl.ds(first, count)],
                    rows_in.at[device, pl.ds(12 * half + first, count)],
                    sem,
                ).start()
        if first == 0:
            copy_a.start()
    copy_w.start()
    copy_head_a.start()
    copy_head_w.start()
    wait_a = pltpu.make_async_copy(
        rows_in.at[:, pl.ds(0, 6)], rows_in.at[:, pl.ds(0, 6)], sems.at[0]
    )
    wait_w = pltpu.make_async_copy(
        rows_in.at[:, pl.ds(0, 18)], rows_in.at[:, pl.ds(0, 18)], sems.at[1]
    )
    ones_row = jnp.where(
        lax.broadcasted_iota(jnp.int32, (16, FRAMES), 0) == 0, 1.0, 0.0
    ).astype(bf16)
    pool_mat = jnp.where(
        lax.broadcasted_iota(jnp.int32, (POOLED, FRAMES), 1) // POOL
        == lax.broadcasted_iota(jnp.int32, (POOLED, FRAMES), 0),
        1.0 / POOL,
        0.0,
    ).astype(bf16)
    nt = (((1,), (1,)), ((), ()))
    tn = (((0,), (0,)), ((), ()))

    def put(qkv, kind, clip, head, value):
        scale = jnp.where(kind == 0, HEAD ** (-0.5), 1.0).astype(f32)
        qkv[kind, clip, head] = (value.astype(bf16).astype(f32) * scale).astype(bf16)

    def attention(qkv, att, heads):
        rows = lax.broadcasted_iota(jnp.int32, (16, FRAMES), 0)
        frame = lax.broadcasted_iota(jnp.int32, (16, FRAMES), 1)

        bias = [
            jnp.where(
                (rows == 0) & (frame >= frames_valid[column * 2 + clip]), -1e30, 0.0
            ).astype(bf16)
            for clip in range(2)
        ]

        def score(item, scores):
            clip, head = item % 2, item // 2
            key_x = jnp.concatenate([qkv[1, clip, head], bias[clip]], axis=0)
            query_x = jnp.concatenate([qkv[0, clip, head], ones_row], axis=0)
            value = lax.dot_general(key_x, query_x, tn, preferred_element_type=f32)
            scores[...] = value
            return jnp.max(value, axis=0, keepdims=True)

        def mix(item, scores, top):
            clip, head = item % 2, item // 2
            value_x = jnp.concatenate([qkv[2, clip, head], ones_row], axis=0)
            raised = jnp.exp(scores[...] - top).astype(bf16)
            mixed = jnp.dot(value_x, raised, preferred_element_type=f32)
            total = mixed[HEAD : HEAD + 1]
            att[clip, head] = (mixed[:HEAD] * (1.0 / total)).astype(bf16)

        top = score(0, score_refs[0])
        for item in range(2 * heads):
            if item + 1 < 2 * heads:
                next_top = score(item + 1, score_refs[(item + 1) % 2])
            mix(item, score_refs[item % 2], top)
            top = next_top

    wait_a.wait()
    copy_a.wait()
    for clip in range(2):
        lhs = jnp.concatenate(
            [
                jnp.concatenate(
                    [
                        rows_in[8 * (t // 2) + block, 12 * (t % 2) : 12 * (t % 2) + 3].reshape(
                            96, 128
                        )
                        for block in range(8)
                    ],
                    axis=0,
                )
                for t in range(8)
            ],
            axis=1,
        )
        value = lax.dot_general(lhs, norm_a[clip], nt, preferred_element_type=f32)
        for s in range(3):
            kind = (s - role + 6) % 3
            for h in range(A_HEADS):
                start = s * A_COLS + h * HEAD
                put(qkv_a, kind, clip, h, value[start : start + HEAD])
    attention(qkv_a, att_a, A_HEADS)
    for clip in range(2):
        rows = att_a[clip].reshape(A_COLS, FRAMES)
        mean = lax.dot_general(pool_mat, rows, nt, preferred_element_type=f32).astype(bf16)
        pooled[:, clip * 32 : clip * 32 + 32, :A_COLS] = mean.reshape(ROLES, 32, A_COLS)

    wait_w.wait()
    copy_w.wait()
    copy_head_a.wait()
    copy_head_w.wait()
    pick_latents(slot_clip, rows_in, slots, lat)
    pred_a[...] = jnp.dot(lat[:ROWS], head_a[...], preferred_element_type=f32)
    pred_w[...] = jnp.dot(lat[:ROWS], head_w[...], preferred_element_type=f32)
    for clip in range(2):
        lhs = jnp.concatenate(
            [
                jnp.concatenate(
                    [
                        rows_in[8 * zs + block, 12 * (t // 5) + 3 + t % 5]
                        for block in range(8)
                        for zs in range(4)
                    ],
                    axis=0,
                )
                for t in range(10)
            ],
            axis=1,
        )
        proj[...] = lax.dot_general(lhs, norm_w[clip], nt, preferred_element_type=f32)
        for s in range(3):
            kind = (s - role + 6) % 3
            for h in range(W_HEADS):
                start = s * W_COLS + h * HEAD
                parts = []
                while start < s * W_COLS + (h + 1) * HEAD:
                    block, inner = start // 120, start % 120
                    take = min(120 - inner, s * W_COLS + (h + 1) * HEAD - start)
                    parts.append(proj[block * 128 + inner : block * 128 + inner + take])
                    start += take
                value = parts[0] if len(parts) == 1 else jnp.concatenate(parts, axis=0)
                put(qkv_w, kind, clip, h, value)
    attention(qkv_w, att_w, W_HEADS)
    for clip in range(2):
        rows = att_w[clip].reshape(W_COLS, FRAMES)
        mean = lax.dot_general(pool_mat, rows, nt, preferred_element_type=f32).astype(bf16)
        mean = jnp.concatenate([mean, jnp.zeros((POOLED, 64), bf16)], axis=1)
        pooled[:, clip * 32 : clip * 32 + 32, A_COLS:] = mean.reshape(ROLES, 32, 384)
    for k in range(ROLES):
        outs[k][...] = pooled[(role + k) % ROLES]


def attend(frames_valid, slot_clip, pieces, norm_a, norm_w, head_a, head_w):
    vmem = pl.BlockSpec(memory_space=pltpu.VMEM)
    return pl.pallas_call(
        attend_kernel,
        out_shape=[pltpu.VMEM((ROWS, OUT_COLS), bf16)] * ROLES
        + [
            pltpu.VMEM((2 * ROWS, STU_D), bf16),
            pltpu.VMEM((ROWS, WAVLM_D), f32),
            pltpu.VMEM((ROWS, WHISPER_D), f32),
        ],
        in_specs=[pl.BlockSpec(memory_space=pltpu.SMEM)] * 2
        + [pl.BlockSpec(memory_space=pl.ANY)] * 20,
        out_specs=[vmem] * 7,
        scratch_shapes=[
            pltpu.VMEM((2, FRAMES, WAVLM_D), bf16),
            pltpu.VMEM((2, FRAMES, WHISPER_D), bf16),
            pltpu.VMEM((32, 24, 32, 128), bf16),
            pltpu.VMEM((3, 2, A_HEADS, HEAD, FRAMES), bf16),
            pltpu.VMEM((3, 2, W_HEADS, HEAD, FRAMES), bf16),
            pltpu.VMEM((1024, FRAMES), f32),
            pltpu.VMEM((2, A_HEADS, HEAD, FRAMES), bf16),
            pltpu.VMEM((2, W_HEADS, HEAD, FRAMES), bf16),
            pltpu.VMEM((FRAMES, FRAMES), f32),
            pltpu.VMEM((FRAMES, FRAMES), f32),
            pltpu.SMEM((4,), jnp.int32),
            pltpu.VMEM((STU_D, WAVLM_D), bf16),
            pltpu.VMEM((STU_D, WHISPER_D), bf16),
            pltpu.VMEM((ROLES, ROWS, OUT_COLS), bf16),
            pltpu.SemaphoreType.DMA((6,)),
        ],
        cost_estimate=pl.CostEstimate(
            flops=8_000_000_000, bytes_accessed=12_000_000, transcendentals=5_000_000
        ),
        name="attend",
    )(frames_valid, slot_clip, *pieces, norm_a, norm_w, head_a, head_w)


def slope_kernel(frames_valid, *refs):
    arrived = refs[:4]
    out_a_hbm, out_w_hbm, mean_a, mean_w, pred_a, pred_w = refs[4:10]
    outs, parts, grouped, out_a, out_w, sems = refs[10:14], *refs[14:19]
    copies = []
    for source, target in ((out_a_hbm, out_a), (out_w_hbm, out_w)):
        for start in range(0, source.shape[0], 256):
            rows = pl.ds(start, 256)
            copies.append(
                pltpu.make_async_copy(source.at[rows], target.at[rows], sems.at[len(copies)])
            )
            copies[-1].start()
    role = lax.axis_index("role")
    clip = lax.axis_index("dp") * 2
    for k in range(ROLES):
        parts[(role - k + ROLES) % ROLES] = arrived[k][...]
    row = lax.broadcasted_iota(jnp.int32, (ROWS, 1), 0)
    valid = jnp.where(row < 32, frames_valid[clip], frames_valid[clip + 1]) // POOL
    keep = (row % 32 + role * 32) < valid

    def slope_of(mean, waits, out, pred, cols, first):
        width = mean.shape[-1]
        attended = jnp.concatenate(
            [parts[r, :, first : first + cols] for r in range(ROLES)], axis=1
        )
        total = mean[...]
        for i, copy in enumerate(waits):
            copy.wait()
            rows = slice(256 * i, 256 * i + 256)
            total = total + jnp.dot(attended[:, rows], out[rows], preferred_element_type=f32)
        target = total.astype(bf16).astype(f32)
        predicted = pred[...]
        pred_sq = jnp.sum(predicted * predicted, axis=-1, keepdims=True) + epsilon_cos
        targ_sq = jnp.sum(target * target, axis=-1, keepdims=True) + epsilon_cos
        pred_norm = jnp.sqrt(pred_sq)
        both = pred_norm * jnp.sqrt(targ_sq)
        cosine = jnp.sum(predicted * target, axis=-1, keepdims=True) / both
        slope = (cosine / (pred_norm * pred_norm)) * predicted - target / both
        slope = slope + (predicted - target) * (1.0 / width)
        return jnp.where(keep, slope, 0.0).astype(bf16)

    slope_a = slope_of(mean_a, copies[:4], out_a, pred_a, A_COLS, 0)
    for g in range(ROLES):
        grouped[g, :, :A_COLS] = slope_a[:, g * A_COLS : (g + 1) * A_COLS]
    slope_w = slope_of(mean_w, copies[4:], out_w, pred_w, W_COLS, A_COLS)
    for g in range(ROLES):
        grouped[g, :, A_COLS:] = jnp.concatenate(
            [slope_w[:, g * W_COLS : (g + 1) * W_COLS], jnp.zeros((ROWS, 64), bf16)], axis=1
        )
    for k in range(ROLES):
        outs[k][...] = grouped[(role + k) % ROLES]


def slopes(frames_valid, parts, out_a, out_w, mean_a, mean_w, pred_a, pred_w):
    vmem = pl.BlockSpec(memory_space=pltpu.VMEM)
    return pl.pallas_call(
        slope_kernel,
        out_shape=[pltpu.VMEM((ROWS, OUT_COLS), bf16)] * ROLES,
        in_specs=[pl.BlockSpec(memory_space=pltpu.SMEM)]
        + [vmem] * 4
        + [pl.BlockSpec(memory_space=pl.ANY)] * 2
        + [vmem] * 4,
        out_specs=[vmem] * ROLES,
        scratch_shapes=[pltpu.VMEM((ROLES, ROWS, OUT_COLS), bf16)] * 2
        + [
            pltpu.VMEM((WAVLM_D, WAVLM_D), bf16),
            pltpu.VMEM((WHISPER_D, WHISPER_D), bf16),
            pltpu.SemaphoreType.DMA((9,)),
        ],
        name="slopes",
    )(frames_valid, *near(*parts), out_a, out_w, *near(mean_a, mean_w, pred_a, pred_w))


def outer_kernel(*refs):
    lats, own, other, out = refs[:4], refs[4:8], refs[8:12], refs[12]
    start = pl.multiple_of((lax.axis_index("dp") % 2) * 256, 256)
    lat = jnp.concatenate([lats[k][:, pl.ds(start, 256)] for k in range(ROLES)], axis=0)
    rows = []
    for k in range(ROLES):
        rows += [own[k][...], other[k][...]]
    grad = lax.dot_general(
        lat, jnp.concatenate(rows, axis=0), (((0,), (0,)), ((), ())), preferred_element_type=f32
    )
    grad = grad.reshape(16, 16, OUT_COLS)
    for t in range(4):
        out[:, 16 * t : 16 * t + 16] = grad[:, :, 128 * t : 128 * t + 128]
    out[:, 64:] = jnp.concatenate([grad[:, :8, 512:576], grad[:, 8:, 512:576]], axis=-1)


def outer(lats, own, other):
    vmem = pl.BlockSpec(memory_space=pltpu.VMEM)
    return pl.pallas_call(
        outer_kernel,
        out_shape=pltpu.VMEM((16, 72, 128), f32),
        in_specs=[vmem] * 12,
        out_specs=vmem,
        name="outer",
    )(*near(*lats, *own, *other))


def sum_kernel(x, out):
    total = jnp.sum(x[...], axis=0).astype(bf16)
    out[...] = jnp.broadcast_to(total[None], out.shape)


def reduce_parts(x):
    vmem = pl.BlockSpec(memory_space=pltpu.VMEM)
    return pl.pallas_call(
        sum_kernel,
        out_shape=pltpu.VMEM((64, 72, 128), bf16),
        in_specs=[vmem],
        out_specs=vmem,
        name="reduce_parts",
    )(*near(x))


def place_kernel(piece, *refs):
    out_a, out_w = refs[-2:]
    blocks = []
    step = pl.program_id(0) * 8
    for g in range(ROLES):
        block = piece[g, pl.ds(step, 8)].astype(f32)
        for t in range(2):
            lane = g * A_COLS + 128 * t
            out_a[0, :, lane : lane + 128] = block[:, 16 * t : 16 * t + 16].reshape(128, 128)
            blocks.append(block[:, 32 + 16 * t : 48 + 16 * t].reshape(128, 128))
        last = block[:, 64:]
        last = jnp.concatenate([last[:, :, :64], last[:, :, 64:]], axis=1)
        blocks.append(last.reshape(128, 64))
    out_w[0] = jnp.concatenate(blocks, axis=1)


def place(piece, partner, held=()):
    half = lambda: (lax.axis_index("dp") + partner) % 2
    hbm = pl.BlockSpec(memory_space=pl.ANY)
    return pl.pallas_call(
        place_kernel,
        grid=(2,),
        out_shape=[
            jax.ShapeDtypeStruct((2, 256, WAVLM_D), f32),
            jax.ShapeDtypeStruct((2, 256, WHISPER_D), f32),
        ],
        in_specs=[pl.BlockSpec(memory_space=pltpu.VMEM)]
        + [hbm] * len(held),
        out_specs=[
            pl.BlockSpec((1, 128, WAVLM_D), lambda i: (half(), i, 0)),
            pl.BlockSpec((1, 128, WHISPER_D), lambda i: (half(), i, 0)),
        ],
        input_output_aliases={1: 0, 2: 1} if held else {},
        name="place_partner" if partner else "place_own",
    )(*near(piece), *held)


PLANE = [[z * 8 + y * 2 + c for z in range(4) for y in range(4)] for c in range(2)]
SLICE = [[r * 32 + i for r in range(ROLES) for i in plane] for plane in PLANE]


def per_device(
    wavlm_hidden,
    whisper_hidden,
    wavlm_qkv,
    whisper_qkv,
    wavlm_out,
    whisper_out,
    frames_valid,
    slot_clip,
    latent,
    wavlm_head,
    whisper_head,
):
    chunks = weight_chunks(wavlm_qkv.T, whisper_qkv.T)
    chunks = [chunks[0]] + [dp_send(chunks[k], k, 0, 0) for k in (1, 2, 3)]
    first, second = shares(chunks, latent)
    first, second = spread_line(first, second)
    pieces = spread_cross(first, second)
    pieces = pieces + [dp_send(x, 0, 0, 1) for x in pieces]
    norm_a, mean_a = norms(wavlm_hidden)
    norm_w, mean_w = norms(whisper_hidden)

    *pooled, lat, pred_a, pred_w = attend(
        frames_valid, slot_clip, pieces, norm_a, norm_w, wavlm_head, whisper_head
    )
    parts = [pooled[0]] + [role_send(pooled[k], k) for k in (1, 2, 3)]
    lats = [lat] + [role_send(lat, k) for k in (1, 2, 3)]
    sloped = slopes(
        frames_valid, parts, wavlm_out, whisper_out, mean_a, mean_w, pred_a, pred_w
    )
    slope_own = [sloped[0]] + [role_send(sloped[k], k) for k in (1, 2, 3)]
    slope_other = [dp_send(x, 0, 0, 1) for x in slope_own]
    halves = outer(lats, slope_own, slope_other)
    arrived = lax.all_to_all(
        halves, "dp", split_axis=0, concat_axis=0, tiled=True, axis_index_groups=PLANE
    )
    summed = lax.all_to_all(
        reduce_parts(arrived),
        ("role", "dp"),
        split_axis=0,
        concat_axis=0,
        tiled=True,
        axis_index_groups=SLICE,
    ).reshape(ROLES, 16, 72, 128)
    partner = dp_send(summed, 0, 0, 1)
    held = place(summed, 0)
    grad_a, grad_w = place(partner, 1, held)
    return grad_a.reshape(STU_D, WAVLM_D), grad_w.reshape(STU_D, WHISPER_D)


def solution(mesh):
    in_specs = (
        P("dp", None, None),
        P("dp", None, None),
        P(None, "dp"),
        P(None, "dp"),
        P(),
        P(),
        P(),
        P(),
        P(None, "dp", None, None),
        P(),
        P(),
    )
    out_specs = (P(), P())

    return jax.shard_map(
        per_device, mesh=mesh, in_specs=in_specs, out_specs=out_specs, check_vma=False
    )
```

```python
import jax
import jax.numpy as jnp
from jax import lax
from jax.experimental import pallas as pl
from jax.experimental.pallas import tpu as pltpu
from jax.sharding import PartitionSpec as P


WAVLM_D = 1024
WHISPER_D = 1280
STU_D = 512
HEAD = 64
FRAMES = 512
POOL = 4
POOLED = 128
CLIPS = 64
ROLES = 4
A_HEADS = WAVLM_D // HEAD // ROLES
W_HEADS = WHISPER_D // HEAD // ROLES
A_COLS = A_HEADS * HEAD
W_COLS = W_HEADS * HEAD
OUT_COLS = 640
ROWS = 64

epsilon_norm = 1e-05
epsilon_cos = 1e-06


bf16 = jnp.bfloat16
f32 = jnp.float32


def dp_send(x, dz, dy, dc):
    pairs = []
    for i in range(32):
        z, y, c = i // 8, (i // 2) % 4, i % 2
        target = ((z + dz) % 4) * 8 + ((y + dy) % 4) * 2 + (c + dc) % 2
        pairs.append((i, target))
    return lax.ppermute(x, "dp", pairs)


def role_send(x, k):
    return lax.ppermute(x, "role", [(i, (i + k) % ROLES) for i in range(ROLES)])


def near(*arrays):
    return [pltpu.with_memory_space_constraint(x, pltpu.VMEM) for x in arrays]


def place_of(column):
    return column // 8, (column // 2) % 4, column % 2


def norm_kernel(hidden, norm, mean):
    pool_mat = jnp.where(
        lax.broadcasted_iota(jnp.int32, (32, 128), 1) // POOL
        == lax.broadcasted_iota(jnp.int32, (32, 128), 0),
        1.0 / POOL,
        0.0,
    ).astype(bf16)
    rows = hidden[0].astype(f32)
    centred = rows - jnp.mean(rows, axis=-1, keepdims=True)
    variance = jnp.mean(centred * centred, axis=-1, keepdims=True)
    norm[0] = (centred * lax.rsqrt(variance + epsilon_norm)).astype(bf16)

    quarter = hidden[0, pl.ds(pl.multiple_of(lax.axis_index("role") * 128, 128), 128), :]
    mean[...] = jnp.dot(pool_mat, quarter, preferred_element_type=f32)


def norms(hidden):
    width = hidden.shape[-1]
    rows = pl.BlockSpec((1, FRAMES, width), lambda i: (i, 0, 0))
    return pl.pallas_call(
        norm_kernel,
        grid=(2,),
        out_shape=[
            jax.ShapeDtypeStruct(hidden.shape, bf16),
            jax.ShapeDtypeStruct((ROWS, width), f32),
        ],
        in_specs=[rows],
        out_specs=[rows, pl.BlockSpec((32, width), lambda i: (i, 0))],
        cost_estimate=pl.CostEstimate(
            flops=30_000_000, bytes_accessed=12_000_000, transcendentals=2048
        ),
    )(hidden)


def chunk_kernel(qkv_a, qkv_w, latent, raw, *refs):
    outs, chunks = refs[:4], refs[4]
    z = place_of(lax.axis_index("dp"))[0]
    for part in range(4):
        for t in range(2):
            lane = (2 * part + t) * 128
            chunks[part, 8 * t : 8 * t + 3] = qkv_a[:, lane : lane + 128].reshape(3, 32, 128)
        for t in range(10):
            if part < 3:
                rows = qkv_w[32 * part : 32 * part + 32, 128 * t : 128 * t + 128]
            else:
                rows = jnp.concatenate(
                    [qkv_w[96:120, 128 * t : 128 * t + 128], jnp.zeros((8, 128), bf16)], axis=0
                )
            chunks[part, 3 + t + 3 * (t // 5)] = rows
        raw[8 * part : 8 * part + 8] = chunks[part, :8]
    for t in range(4):
        raw[32 + t] = latent[0, 0, :, 128 * t : 128 * t + 128]
    for k in range(4):
        outs[k][...] = chunks[(z + k) % 4, pl.ds(8, 8)]


def weight_chunks(qkv_a, qkv_w, latent):
    block = lambda shape: pl.BlockSpec(shape, lambda i: (0,) * len(shape))
    return pl.pallas_call(
        chunk_kernel,
        grid=(1,),
        out_shape=[pltpu.VMEM((36, 32, 128), bf16)] + [pltpu.VMEM((8, 32, 128), bf16)] * 4,
        in_specs=[
            block((96, WAVLM_D)),
            block((120, WHISPER_D)),
            pl.BlockSpec((1, 1, 32, STU_D), lambda i: (0, 0, lax.axis_index("role"), 0)),
        ],
        out_specs=[pl.BlockSpec(memory_space=pltpu.VMEM)] * 5,
        scratch_shapes=[pltpu.VMEM((4, 16, 32, 128), bf16)],
        name="weight_chunks",
    )(qkv_a, qkv_w, latent)


def needed_source(group, part):
    role = lax.axis_index("role")
    _, y, c = place_of(lax.axis_index("dp"))
    row = lax.broadcasted_iota(jnp.int32, (32, 128), 0)
    sources = [(role + 4 * ((s - role + 6) % 3)) // 3 for s in range(3)]
    if group < 3:
        column, width = 96 * (2 * y + c) + 32 * group + row, A_COLS
    else:
        column, width = 120 * (2 * y + c) + 32 * part + row, W_COLS
    return jnp.where(
        column < width, sources[0], jnp.where(column < 2 * width, sources[1], sources[2])
    )


def choose(parts, index, source, z):
    value = parts[0][index].astype(f32)
    for k in range(1, 4):
        value = jnp.where(source == (z - k + 4) % 4, parts[k][index].astype(f32), value)
    return value.astype(bf16)


def first_kernel(*refs):
    parts, out = refs[:4], refs[4]
    z = place_of(lax.axis_index("dp"))[0]
    for e in range(4):
        part = (z - e + 4) % 4
        for group in range(8):
            if group < 4:
                source = needed_source(group, part)
            out[e, group] = choose(parts, 8 * part + group, source, z)
        out[e, 8:] = parts[e][32:]


def second_kernel(*refs):
    parts, latent, out = refs[:4], refs[4], refs[5]
    z = place_of(lax.axis_index("dp"))[0]
    for group in range(8):
        if group < 4:
            source = needed_source(group, z)
        out[group] = choose(parts, group, source, z)
    for t in range(4):
        out[8 + t] = latent[0, 0, :, 128 * t : 128 * t + 128]


def first_shares(parts):
    vmem = pl.BlockSpec(memory_space=pltpu.VMEM)
    return pl.pallas_call(
        first_kernel,
        out_shape=pltpu.VMEM((4, 12, 32, 128), bf16),
        in_specs=[vmem] * 4,
        out_specs=vmem,
        name="first_shares",
    )(*near(*parts))


def second_shares(parts, latent):
    vmem = pl.BlockSpec(memory_space=pltpu.VMEM)
    return pl.pallas_call(
        second_kernel,
        grid=(1,),
        out_shape=pltpu.VMEM((12, 32, 128), bf16),
        in_specs=[vmem] * 4
        + [pl.BlockSpec((1, 1, 32, STU_D), lambda i: (1, 0, lax.axis_index("role"), 0))],
        out_specs=vmem,
        name="second_shares",
    )(*near(*parts), latent)


def stack_kernel(*refs):
    for k in range(4):
        refs[4][k] = refs[k][...]


def stacked(parts):
    vmem = pl.BlockSpec(memory_space=pltpu.VMEM)
    return pl.pallas_call(
        stack_kernel,
        out_shape=pltpu.VMEM((4,) + parts[0].shape, bf16),
        in_specs=[vmem] * 4,
        out_specs=vmem,
        name="stacked",
    )(*near(*parts))


def spread_cross(first, second):
    got = {}
    for k in (1, 3, 2):
        got[k] = dp_send(first, 0, k, 0), dp_send(second, k, 0, 0)
    return (
        [first] + [got[k][0] for k in (1, 2, 3)] + [second] + [got[k][1] for k in (1, 2, 3)]
    )


def pick_latents(slot_clip, rows, slots, out):
    column = lax.axis_index("dp")
    c = column % 2
    base = (column // 2) * 4

    def find(s, carry):
        local = slot_clip[s] - base

        @pl.when((local >= 0) & (local < 4))
        def _():
            slots[jnp.clip(local, 0, 3)] = s

        return carry

    lax.fori_loop(0, CLIPS, find, 0)
    for i in range(4):
        slot = slots[(2 * c + i) % 4]
        h, j = slot // 32, slot % 32
        out[i * 32 : i * 32 + 32] = jnp.concatenate(
            [rows[j, 12 * h + 8 + t] for t in range(4)], axis=1
        )


def attend_kernel(frames_valid, slot_clip, *refs):
    pieces = refs[:16]
    norm_a_hbm, norm_w_hbm, head_a_hbm, head_w_hbm = refs[16:20]
    outs, lat, pred_a, pred_w = refs[20:24], *refs[24:27]
    norm_a, norm_w, rows_in, qkv_a, qkv_w, proj, att_a, att_w = refs[27:35]
    score_refs, slots, head_a, head_w, pooled, sems = refs[35:37], *refs[37:42]
    copy_head_a = pltpu.make_async_copy(head_a_hbm, head_a, sems.at[4])
    copy_head_w = pltpu.make_async_copy(head_w_hbm, head_w, sems.at[5])
    copy_a = pltpu.make_async_copy(norm_a_hbm, norm_a, sems.at[2])
    copy_w = pltpu.make_async_copy(norm_w_hbm, norm_w, sems.at[3])
    role = lax.axis_index("role")
    column = lax.axis_index("dp")
    z, y, c = place_of(column)
    for first, count, sem in ((0, 3, sems.at[0]), (3, 9, sems.at[1])):
        for n, piece in enumerate(pieces):
            core = (c + n // 8) % 2
            half, far = (n % 8) // 4, n % 4
            for e in range(piece.shape[0]):
                dz, dy = (e, far) if half == 0 else (far, e)
                device = ((z - dz) % 4) * 8 + ((y - dy) % 4) * 2 + core
                pltpu.make_async_copy(
                    piece.at[e, pl.ds(first, count)],
                    rows_in.at[device, pl.ds(12 * half + first, count)],
                    sem,
                ).start()
        if first == 0:
            copy_a.start()
    copy_w.start()
    copy_head_a.start()
    copy_head_w.start()
    wait_a = pltpu.make_async_copy(
        rows_in.at[:, pl.ds(0, 6)], rows_in.at[:, pl.ds(0, 6)], sems.at[0]
    )
    wait_w = pltpu.make_async_copy(
        rows_in.at[:, pl.ds(0, 18)], rows_in.at[:, pl.ds(0, 18)], sems.at[1]
    )
    ones_row = jnp.where(
        lax.broadcasted_iota(jnp.int32, (16, FRAMES), 0) == 0, 1.0, 0.0
    ).astype(bf16)
    pool_mat = jnp.where(
        lax.broadcasted_iota(jnp.int32, (POOLED, FRAMES), 1) // POOL
        == lax.broadcasted_iota(jnp.int32, (POOLED, FRAMES), 0),
        1.0 / POOL,
        0.0,
    ).astype(bf16)
    nt = (((1,), (1,)), ((), ()))
    tn = (((0,), (0,)), ((), ()))

    def put(qkv, kind, clip, head, value):
        scale = jnp.where(kind == 0, HEAD ** (-0.5), 1.0).astype(f32)
        qkv[kind, clip, head] = (value.astype(bf16).astype(f32) * scale).astype(bf16)

    def attention(qkv, att, heads):
        rows = lax.broadcasted_iota(jnp.int32, (16, FRAMES), 0)
        frame = lax.broadcasted_iota(jnp.int32, (16, FRAMES), 1)

        bias = [
            jnp.where(
                (rows == 0) & (frame >= frames_valid[column * 2 + clip]), -1e30, 0.0
            ).astype(bf16)
            for clip in range(2)
        ]

        def score(item, scores):
            clip, head = item % 2, item // 2
            key_x = jnp.concatenate([qkv[1, clip, head], bias[clip]], axis=0)
            query_x = jnp.concatenate([qkv[0, clip, head], ones_row], axis=0)
            value = lax.dot_general(key_x, query_x, tn, preferred_element_type=f32)
            scores[...] = value
            return jnp.max(value, axis=0, keepdims=True)

        def mix(item, scores, top):
            clip, head = item % 2, item // 2
            value_x = jnp.concatenate([qkv[2, clip, head], ones_row], axis=0)
            raised = jnp.exp(scores[...] - top).astype(bf16)
            mixed = jnp.dot(value_x, raised, preferred_element_type=f32)
            total = mixed[HEAD : HEAD + 1]
            att[clip, head] = (mixed[:HEAD] * (1.0 / total)).astype(bf16)

        top = score(0, score_refs[0])
        for item in range(2 * heads):
            if item + 1 < 2 * heads:
                next_top = score(item + 1, score_refs[(item + 1) % 2])
            mix(item, score_refs[item % 2], top)
            top = next_top

    wait_a.wait()
    copy_a.wait()
    for clip in range(2):
        lhs = jnp.concatenate(
            [
                jnp.concatenate(
                    [
                        rows_in[8 * (t // 2) + block, 12 * (t % 2) : 12 * (t % 2) + 3].reshape(
                            96, 128
                        )
                        for block in range(8)
                    ],
                    axis=0,
                )
                for t in range(8)
            ],
            axis=1,
        )
        value = lax.dot_general(lhs, norm_a[clip], nt, preferred_element_type=f32)
        for s in range(3):
            kind = (s - role + 6) % 3
            for h in range(A_HEADS):
                start = s * A_COLS + h * HEAD
                put(qkv_a, kind, clip, h, value[start : start + HEAD])
    attention(qkv_a, att_a, A_HEADS)
    for clip in range(2):
        rows = att_a[clip].reshape(A_COLS, FRAMES)
        mean = lax.dot_general(pool_mat, rows, nt, preferred_element_type=f32).astype(bf16)
        pooled[:, clip * 32 : clip * 32 + 32, :A_COLS] = mean.reshape(ROLES, 32, A_COLS)

    wait_w.wait()
    copy_w.wait()
    copy_head_a.wait()
    copy_head_w.wait()
    pick_latents(slot_clip, rows_in, slots, lat)
    pred_a[...] = jnp.dot(lat[:ROWS], head_a[...], preferred_element_type=f32)
    pred_w[...] = jnp.dot(lat[:ROWS], head_w[...], preferred_element_type=f32)
    for clip in range(2):
        lhs = jnp.concatenate(
            [
                jnp.concatenate(
                    [
                        rows_in[8 * zs + block, 12 * (t // 5) + 3 + t % 5]
                        for block in range(8)
                        for zs in range(4)
                    ],
                    axis=0,
                )
                for t in range(10)
            ],
            axis=1,
        )
        proj[...] = lax.dot_general(lhs, norm_w[clip], nt, preferred_element_type=f32)
        for s in range(3):
            kind = (s - role + 6) % 3
            for h in range(W_HEADS):
                start = s * W_COLS + h * HEAD
                parts = []
                while start < s * W_COLS + (h + 1) * HEAD:
                    block, inner = start // 120, start % 120
                    take = min(120 - inner, s * W_COLS + (h + 1) * HEAD - start)
                    parts.append(proj[block * 128 + inner : block * 128 + inner + take])
                    start += take
                value = parts[0] if len(parts) == 1 else jnp.concatenate(parts, axis=0)
                put(qkv_w, kind, clip, h, value)
    attention(qkv_w, att_w, W_HEADS)
    for clip in range(2):
        rows = att_w[clip].reshape(W_COLS, FRAMES)
        mean = lax.dot_general(pool_mat, rows, nt, preferred_element_type=f32).astype(bf16)
        mean = jnp.concatenate([mean, jnp.zeros((POOLED, 64), bf16)], axis=1)
        pooled[:, clip * 32 : clip * 32 + 32, A_COLS:] = mean.reshape(ROLES, 32, 384)
    for k in range(ROLES):
        outs[k][...] = pooled[(role + k) % ROLES]


def attend(frames_valid, slot_clip, pieces, norm_a, norm_w, head_a, head_w):
    vmem = pl.BlockSpec(memory_space=pltpu.VMEM)
    return pl.pallas_call(
        attend_kernel,
        out_shape=[pltpu.VMEM((ROWS, OUT_COLS), bf16)] * ROLES
        + [
            pltpu.VMEM((2 * ROWS, STU_D), bf16),
            pltpu.VMEM((ROWS, WAVLM_D), f32),
            pltpu.VMEM((ROWS, WHISPER_D), f32),
        ],
        in_specs=[pl.BlockSpec(memory_space=pltpu.SMEM)] * 2
        + [pl.BlockSpec(memory_space=pl.ANY)] * 20,
        out_specs=[vmem] * 7,
        scratch_shapes=[
            pltpu.VMEM((2, FRAMES, WAVLM_D), bf16),
            pltpu.VMEM((2, FRAMES, WHISPER_D), bf16),
            pltpu.VMEM((32, 24, 32, 128), bf16),
            pltpu.VMEM((3, 2, A_HEADS, HEAD, FRAMES), bf16),
            pltpu.VMEM((3, 2, W_HEADS, HEAD, FRAMES), bf16),
            pltpu.VMEM((1024, FRAMES), f32),
            pltpu.VMEM((2, A_HEADS, HEAD, FRAMES), bf16),
            pltpu.VMEM((2, W_HEADS, HEAD, FRAMES), bf16),
            pltpu.VMEM((FRAMES, FRAMES), f32),
            pltpu.VMEM((FRAMES, FRAMES), f32),
            pltpu.SMEM((4,), jnp.int32),
            pltpu.VMEM((STU_D, WAVLM_D), bf16),
            pltpu.VMEM((STU_D, WHISPER_D), bf16),
            pltpu.VMEM((ROLES, ROWS, OUT_COLS), bf16),
            pltpu.SemaphoreType.DMA((6,)),
        ],
        cost_estimate=pl.CostEstimate(
            flops=8_000_000_000, bytes_accessed=12_000_000, transcendentals=5_000_000
        ),
        name="attend",
    )(frames_valid, slot_clip, *pieces, norm_a, norm_w, head_a, head_w)


def slope_kernel(frames_valid, *refs):
    arrived = refs[:4]
    out_a_hbm, out_w_hbm, mean_a, mean_w, pred_a, pred_w = refs[4:10]
    outs, parts, grouped, out_a, out_w, sems = refs[10:14], *refs[14:19]
    copies = []
    for source, target in ((out_a_hbm, out_a), (out_w_hbm, out_w)):
        for start in range(0, source.shape[0], 256):
            rows = pl.ds(start, 256)
            copies.append(
                pltpu.make_async_copy(source.at[rows], target.at[rows], sems.at[len(copies)])
            )
            copies[-1].start()
    role = lax.axis_index("role")
    clip = lax.axis_index("dp") * 2
    for k in range(ROLES):
        parts[(role - k + ROLES) % ROLES] = arrived[k][...]
    row = lax.broadcasted_iota(jnp.int32, (ROWS, 1), 0)
    valid = jnp.where(row < 32, frames_valid[clip], frames_valid[clip + 1]) // POOL
    keep = (row % 32 + role * 32) < valid

    def slope_of(mean, waits, out, pred, cols, first):
        width = mean.shape[-1]
        attended = jnp.concatenate(
            [parts[r, :, first : first + cols] for r in range(ROLES)], axis=1
        )
        total = mean[...]
        for i, copy in enumerate(waits):
            copy.wait()
            rows = slice(256 * i, 256 * i + 256)
            total = total + jnp.dot(attended[:, rows], out[rows], preferred_element_type=f32)
        target = total.astype(bf16).astype(f32)
        predicted = pred[...]
        pred_sq = jnp.sum(predicted * predicted, axis=-1, keepdims=True) + epsilon_cos
        targ_sq = jnp.sum(target * target, axis=-1, keepdims=True) + epsilon_cos
        pred_norm = jnp.sqrt(pred_sq)
        both = pred_norm * jnp.sqrt(targ_sq)
        cosine = jnp.sum(predicted * target, axis=-1, keepdims=True) / both
        slope = (cosine / (pred_norm * pred_norm)) * predicted - target / both
        slope = slope + (predicted - target) * (1.0 / width)
        return jnp.where(keep, slope, 0.0).astype(bf16)

    slope_a = slope_of(mean_a, copies[:4], out_a, pred_a, A_COLS, 0)
    for g in range(ROLES):
        grouped[g, :, :A_COLS] = slope_a[:, g * A_COLS : (g + 1) * A_COLS]
    slope_w = slope_of(mean_w, copies[4:], out_w, pred_w, W_COLS, A_COLS)
    for g in range(ROLES):
        grouped[g, :, A_COLS:] = jnp.concatenate(
            [slope_w[:, g * W_COLS : (g + 1) * W_COLS], jnp.zeros((ROWS, 64), bf16)], axis=1
        )
    for k in range(ROLES):
        outs[k][...] = grouped[(role + k) % ROLES]


def slopes(frames_valid, parts, out_a, out_w, mean_a, mean_w, pred_a, pred_w):
    vmem = pl.BlockSpec(memory_space=pltpu.VMEM)
    return pl.pallas_call(
        slope_kernel,
        out_shape=[pltpu.VMEM((ROWS, OUT_COLS), bf16)] * ROLES,
        in_specs=[pl.BlockSpec(memory_space=pltpu.SMEM)]
        + [vmem] * 4
        + [pl.BlockSpec(memory_space=pl.ANY)] * 2
        + [vmem] * 4,
        out_specs=[vmem] * ROLES,
        scratch_shapes=[pltpu.VMEM((ROLES, ROWS, OUT_COLS), bf16)] * 2
        + [
            pltpu.VMEM((WAVLM_D, WAVLM_D), bf16),
            pltpu.VMEM((WHISPER_D, WHISPER_D), bf16),
            pltpu.SemaphoreType.DMA((9,)),
        ],
        name="slopes",
    )(frames_valid, *near(*parts), out_a, out_w, *near(mean_a, mean_w, pred_a, pred_w))


def outer_kernel(*refs):
    lats, own, other, out = refs[:4], refs[4:8], refs[8:12], refs[12]
    start = pl.multiple_of((lax.axis_index("dp") % 2) * 256, 256)
    lat = jnp.concatenate([lats[k][:, pl.ds(start, 256)] for k in range(ROLES)], axis=0)
    rows = []
    for k in range(ROLES):
        rows += [own[k][...], other[k][...]]
    grad = lax.dot_general(
        lat, jnp.concatenate(rows, axis=0), (((0,), (0,)), ((), ())), preferred_element_type=f32
    )
    grad = grad.reshape(16, 16, OUT_COLS)
    for t in range(4):
        out[:, 16 * t : 16 * t + 16] = grad[:, :, 128 * t : 128 * t + 128]
    out[:, 64:] = jnp.concatenate([grad[:, :8, 512:576], grad[:, 8:, 512:576]], axis=-1)


def outer(lats, own, other):
    vmem = pl.BlockSpec(memory_space=pltpu.VMEM)
    return pl.pallas_call(
        outer_kernel,
        out_shape=pltpu.VMEM((16, 72, 128), f32),
        in_specs=[vmem] * 12,
        out_specs=vmem,
        name="outer",
    )(*near(*lats, *own, *other))


def sum_kernel(x, out):
    total = jnp.sum(x[...], axis=0).astype(bf16)
    out[...] = jnp.broadcast_to(total[None], out.shape)


def reduce_parts(x):
    vmem = pl.BlockSpec(memory_space=pltpu.VMEM)
    return pl.pallas_call(
        sum_kernel,
        out_shape=pltpu.VMEM((64, 72, 128), bf16),
        in_specs=[vmem],
        out_specs=vmem,
        name="reduce_parts",
    )(*near(x))


def place_kernel(piece, *refs):
    out_a, out_w = refs[-2:]
    blocks = []
    step = pl.program_id(0) * 8
    for g in range(ROLES):
        block = piece[g, pl.ds(step, 8)].astype(f32)
        for t in range(2):
            lane = g * A_COLS + 128 * t
            out_a[0, :, lane : lane + 128] = block[:, 16 * t : 16 * t + 16].reshape(128, 128)
            blocks.append(block[:, 32 + 16 * t : 48 + 16 * t].reshape(128, 128))
        last = block[:, 64:]
        last = jnp.concatenate([last[:, :, :64], last[:, :, 64:]], axis=1)
        blocks.append(last.reshape(128, 64))
    out_w[0] = jnp.concatenate(blocks, axis=1)


def place(piece, partner, held=()):
    half = lambda: (lax.axis_index("dp") + partner) % 2
    hbm = pl.BlockSpec(memory_space=pl.ANY)
    return pl.pallas_call(
        place_kernel,
        grid=(2,),
        out_shape=[
            jax.ShapeDtypeStruct((2, 256, WAVLM_D), f32),
            jax.ShapeDtypeStruct((2, 256, WHISPER_D), f32),
        ],
        in_specs=[pl.BlockSpec(memory_space=pltpu.VMEM)]
        + [hbm] * len(held),
        out_specs=[
            pl.BlockSpec((1, 128, WAVLM_D), lambda i: (half(), i, 0)),
            pl.BlockSpec((1, 128, WHISPER_D), lambda i: (half(), i, 0)),
        ],
        input_output_aliases={1: 0, 2: 1} if held else {},
        name="place_partner" if partner else "place_own",
    )(*near(piece), *held)


PLANE = [[z * 8 + y * 2 + c for z in range(4) for y in range(4)] for c in range(2)]
SLICE = [[r * 32 + i for r in range(ROLES) for i in plane] for plane in PLANE]


def per_device(
    wavlm_hidden,
    whisper_hidden,
    wavlm_qkv,
    whisper_qkv,
    wavlm_out,
    whisper_out,
    frames_valid,
    slot_clip,
    latent,
    wavlm_head,
    whisper_head,
):
    raw, *chunks = weight_chunks(wavlm_qkv.T, whisper_qkv.T, latent)
    chunks = [chunks[0]] + [dp_send(chunks[k], k, 0, 0) for k in (1, 2, 3)]
    raws = [raw] + [dp_send(raw, k, 0, 0) for k in (1, 2, 3)]
    second = second_shares(chunks, latent)
    seconds = [second] + [dp_send(second, 0, k, 0) for k in (1, 2, 3)]
    first = first_shares(raws)
    second = stacked(seconds)
    pieces = spread_cross(first, second)
    pieces = pieces + [dp_send(x, 0, 0, 1) for x in pieces]
    norm_a, mean_a = norms(wavlm_hidden)
    norm_w, mean_w = norms(whisper_hidden)

    *pooled, lat, pred_a, pred_w = attend(
        frames_valid, slot_clip, pieces, norm_a, norm_w, wavlm_head, whisper_head
    )
    parts = [pooled[0]] + [role_send(pooled[k], k) for k in (1, 2, 3)]
    lats = [lat] + [role_send(lat, k) for k in (1, 2, 3)]
    sloped = slopes(
        frames_valid, parts, wavlm_out, whisper_out, mean_a, mean_w, pred_a, pred_w
    )
    slope_own = [sloped[0]] + [role_send(sloped[k], k) for k in (1, 2, 3)]
    slope_other = [dp_send(x, 0, 0, 1) for x in slope_own]
    halves = outer(lats, slope_own, slope_other)
    arrived = lax.all_to_all(
        halves, "dp", split_axis=0, concat_axis=0, tiled=True, axis_index_groups=PLANE
    )
    summed = lax.all_to_all(
        reduce_parts(arrived),
        ("role", "dp"),
        split_axis=0,
        concat_axis=0,
        tiled=True,
        axis_index_groups=SLICE,
    ).reshape(ROLES, 16, 72, 128)
    partner = dp_send(summed, 0, 0, 1)
    held = place(summed, 0)
    grad_a, grad_w = place(partner, 1, held)
    return grad_a.reshape(STU_D, WAVLM_D), grad_w.reshape(STU_D, WHISPER_D)


def solution(mesh):
    in_specs = (
        P("dp", None, None),
        P("dp", None, None),
        P(None, "dp"),
        P(None, "dp"),
        P(),
        P(),
        P(),
        P(),
        P(None, "dp", None, None),
        P(),
        P(),
    )
    out_specs = (P(), P())

    return jax.shard_map(
        per_device, mesh=mesh, in_specs=in_specs, out_specs=out_specs, check_vma=False
    )
```

```python
import jax
import jax.numpy as jnp
from jax import lax
from jax.experimental import pallas as pl
from jax.experimental.pallas import tpu as pltpu
from jax.sharding import PartitionSpec as P


WAVLM_D = 1024
WHISPER_D = 1280
STU_D = 512
HEAD = 64
FRAMES = 512
POOL = 4
POOLED = 128
CLIPS = 64
ROLES = 4
A_HEADS = WAVLM_D // HEAD // ROLES
W_HEADS = WHISPER_D // HEAD // ROLES
A_COLS = A_HEADS * HEAD
W_COLS = W_HEADS * HEAD
OUT_COLS = 640
ROWS = 64

epsilon_norm = 1e-05
epsilon_cos = 1e-06


bf16 = jnp.bfloat16
f32 = jnp.float32


def dp_send(x, dz, dy, dc):
    pairs = []
    for i in range(32):
        z, y, c = i // 8, (i // 2) % 4, i % 2
        target = ((z + dz) % 4) * 8 + ((y + dy) % 4) * 2 + (c + dc) % 2
        pairs.append((i, target))
    return lax.ppermute(x, "dp", pairs)


def role_send(x, k):
    return lax.ppermute(x, "role", [(i, (i + k) % ROLES) for i in range(ROLES)])


def near(*arrays):
    return [pltpu.with_memory_space_constraint(x, pltpu.VMEM) for x in arrays]


def place_of(column):
    return column // 8, (column // 2) % 4, column % 2


def norm_kernel(hidden, norm, mean):
    pool_mat = jnp.where(
        lax.broadcasted_iota(jnp.int32, (32, 128), 1) // POOL
        == lax.broadcasted_iota(jnp.int32, (32, 128), 0),
        1.0 / POOL,
        0.0,
    ).astype(bf16)
    rows = hidden[0].astype(f32)
    centred = rows - jnp.mean(rows, axis=-1, keepdims=True)
    variance = jnp.mean(centred * centred, axis=-1, keepdims=True)
    norm[0] = (centred * lax.rsqrt(variance + epsilon_norm)).astype(bf16)

    quarter = hidden[0, pl.ds(pl.multiple_of(lax.axis_index("role") * 128, 128), 128), :]
    mean[...] = jnp.dot(pool_mat, quarter, preferred_element_type=f32)


def norms(hidden):
    width = hidden.shape[-1]
    rows = pl.BlockSpec((1, FRAMES, width), lambda i: (i, 0, 0))
    return pl.pallas_call(
        norm_kernel,
        grid=(2,),
        out_shape=[
            jax.ShapeDtypeStruct(hidden.shape, bf16),
            jax.ShapeDtypeStruct((ROWS, width), f32),
        ],
        in_specs=[rows],
        out_specs=[rows, pl.BlockSpec((32, width), lambda i: (i, 0))],
        cost_estimate=pl.CostEstimate(
            flops=30_000_000, bytes_accessed=12_000_000, transcendentals=2048
        ),
    )(hidden)


def chunk_kernel(qkv_a, qkv_w, latent, raw, *refs):
    outs, chunks = refs[:4], refs[4]
    z = place_of(lax.axis_index("dp"))[0]
    for part in range(4):
        for t in range(2):
            lane = (2 * part + t) * 128
            chunks[part, 8 * t : 8 * t + 3] = qkv_a[:, lane : lane + 128].reshape(3, 32, 128)
        for t in range(10):
            if part < 3:
                rows = qkv_w[32 * part : 32 * part + 32, 128 * t : 128 * t + 128]
            else:
                rows = jnp.concatenate(
                    [qkv_w[96:120, 128 * t : 128 * t + 128], jnp.zeros((8, 128), bf16)], axis=0
                )
            chunks[part, 3 + t + 3 * (t // 5)] = rows
        raw[8 * part : 8 * part + 8] = chunks[part, :8]
    for t in range(4):
        raw[32 + t] = latent[0, 0, :, 128 * t : 128 * t + 128]
    for k in range(4):
        outs[k][...] = chunks[(z + k) % 4, pl.ds(8, 8)]


def weight_chunks(qkv_a, qkv_w, latent):
    block = lambda shape: pl.BlockSpec(shape, lambda i: (0,) * len(shape))
    return pl.pallas_call(
        chunk_kernel,
        grid=(1,),
        out_shape=[pltpu.VMEM((36, 32, 128), bf16)] + [pltpu.VMEM((8, 32, 128), bf16)] * 4,
        in_specs=[
            block((96, WAVLM_D)),
            block((120, WHISPER_D)),
            pl.BlockSpec((1, 1, 32, STU_D), lambda i: (0, 0, lax.axis_index("role"), 0)),
        ],
        out_specs=[pl.BlockSpec(memory_space=pltpu.VMEM)] * 5,
        scratch_shapes=[pltpu.VMEM((4, 16, 32, 128), bf16)],
        name="weight_chunks",
    )(qkv_a, qkv_w, latent)


def needed_source(group, part):
    role = lax.axis_index("role")
    _, y, c = place_of(lax.axis_index("dp"))
    row = lax.broadcasted_iota(jnp.int32, (32, 128), 0)
    sources = [(role + 4 * ((s - role + 6) % 3)) // 3 for s in range(3)]
    if group < 3:
        column, width = 96 * (2 * y + c) + 32 * group + row, A_COLS
    else:
        column, width = 120 * (2 * y + c) + 32 * part + row, W_COLS
    return jnp.where(
        column < width, sources[0], jnp.where(column < 2 * width, sources[1], sources[2])
    )


def choose(parts, index, source, z):
    value = parts[0][index].astype(f32)
    for k in range(1, 4):
        value = jnp.where(source == (z - k + 4) % 4, parts[k][index].astype(f32), value)
    return value.astype(bf16)


def first_kernel(*refs):
    parts, out = refs[:4], refs[4]
    z = place_of(lax.axis_index("dp"))[0]
    for e in range(4):
        part = (z - e + 4) % 4
        for group in range(8):
            if group < 4:
                source = needed_source(group, part)
            out[e, group] = choose(parts, 8 * part + group, source, z)
        out[e, 8:] = parts[e][32:]


def second_kernel(*refs):
    parts, latent, out = refs[:4], refs[4], refs[5]
    z = place_of(lax.axis_index("dp"))[0]
    for group in range(8):
        if group < 4:
            source = needed_source(group, z)
        out[group] = choose(parts, group, source, z)
    for t in range(4):
        out[8 + t] = latent[0, 0, :, 128 * t : 128 * t + 128]


def first_shares(parts):
    vmem = pl.BlockSpec(memory_space=pltpu.VMEM)
    return pl.pallas_call(
        first_kernel,
        out_shape=pltpu.VMEM((4, 12, 32, 128), bf16),
        in_specs=[vmem] * 4,
        out_specs=vmem,
        name="first_shares",
    )(*near(*parts))


def second_shares(parts, latent):
    vmem = pl.BlockSpec(memory_space=pltpu.VMEM)
    return pl.pallas_call(
        second_kernel,
        grid=(1,),
        out_shape=pltpu.VMEM((12, 32, 128), bf16),
        in_specs=[vmem] * 4
        + [pl.BlockSpec((1, 1, 32, STU_D), lambda i: (1, 0, lax.axis_index("role"), 0))],
        out_specs=vmem,
        name="second_shares",
    )(*near(*parts), latent)


def stack_kernel(*refs):
    for k in range(4):
        refs[4][k] = refs[k][...]


def stacked(parts):
    vmem = pl.BlockSpec(memory_space=pltpu.VMEM)
    return pl.pallas_call(
        stack_kernel,
        out_shape=pltpu.VMEM((4,) + parts[0].shape, bf16),
        in_specs=[vmem] * 4,
        out_specs=vmem,
        name="stacked",
    )(*near(*parts))


def spread_cross(first, second):
    got = {}
    for k in (1, 3, 2):
        got[k] = dp_send(first, 0, k, 0), dp_send(second, k, 0, 0)
    return (
        [first] + [got[k][0] for k in (1, 2, 3)] + [second] + [got[k][1] for k in (1, 2, 3)]
    )


def pick_latents(slots, rows, out):
    c = lax.axis_index("dp") % 2
    for i in range(4):
        slot = slots[(2 * c + i) % 4]
        h, j = slot // 32, slot % 32
        out[i * 32 : i * 32 + 32] = jnp.concatenate(
            [rows[j, 12 * h + 8 + t] for t in range(4)], axis=1
        )


def attend_kernel(frames_valid, slots, *refs):
    pieces = refs[:16]
    norm_a_hbm, norm_w_hbm, head_a_hbm, head_w_hbm = refs[16:20]
    outs, lat, pred_a, pred_w = refs[20:24], *refs[24:27]
    norm_a, norm_w, rows_in, qkv_a, qkv_w, proj, att_a, att_w = refs[27:35]
    score_refs, head_a, head_w, pooled, sems = refs[35:37], *refs[37:41]
    copy_head_a = pltpu.make_async_copy(head_a_hbm, head_a, sems.at[4])
    copy_head_w = pltpu.make_async_copy(head_w_hbm, head_w, sems.at[5])
    copy_a = [
        pltpu.make_async_copy(norm_a_hbm.at[i], norm_a.at[i], sems.at[2 + i]) for i in range(2)
    ]
    copy_w = [
        pltpu.make_async_copy(norm_w_hbm.at[i], norm_w.at[i], sems.at[6 + i]) for i in range(2)
    ]
    role = lax.axis_index("role")
    column = lax.axis_index("dp")
    z, y, c = place_of(column)
    for first, count, sem in ((0, 3, sems.at[0]), (3, 9, sems.at[1])):
        for n, piece in enumerate(pieces):
            core = (c + n // 8) % 2
            half, far = (n % 8) // 4, n % 4
            for e in range(piece.shape[0]):
                dz, dy = (e, far) if half == 0 else (far, e)
                device = ((z - dz) % 4) * 8 + ((y - dy) % 4) * 2 + core
                pltpu.make_async_copy(
                    piece.at[e, pl.ds(first, count)],
                    rows_in.at[device, pl.ds(12 * half + first, count)],
                    sem,
                ).start()
        if first == 0:
            copy_a[0].start()
            copy_a[1].start()
    copy_w[0].start()
    copy_w[1].start()
    copy_head_a.start()
    copy_head_w.start()
    wait_a = pltpu.make_async_copy(
        rows_in.at[:, pl.ds(0, 6)], rows_in.at[:, pl.ds(0, 6)], sems.at[0]
    )
    wait_w = pltpu.make_async_copy(
        rows_in.at[:, pl.ds(0, 18)], rows_in.at[:, pl.ds(0, 18)], sems.at[1]
    )
    ones_row = jnp.where(
        lax.broadcasted_iota(jnp.int32, (16, FRAMES), 0) == 0, 1.0, 0.0
    ).astype(bf16)
    pool_mat = jnp.where(
        lax.broadcasted_iota(jnp.int32, (POOLED, FRAMES), 1) // POOL
        == lax.broadcasted_iota(jnp.int32, (POOLED, FRAMES), 0),
        1.0 / POOL,
        0.0,
    ).astype(bf16)
    nt = (((1,), (1,)), ((), ()))
    tn = (((0,), (0,)), ((), ()))

    def put(qkv, kind, clip, head, value):
        scale = jnp.where(kind == 0, HEAD ** (-0.5), 1.0).astype(f32)
        qkv[kind, clip, head] = (value.astype(bf16).astype(f32) * scale).astype(bf16)

    def attention(qkv, att, heads):
        rows = lax.broadcasted_iota(jnp.int32, (16, FRAMES), 0)
        frame = lax.broadcasted_iota(jnp.int32, (16, FRAMES), 1)

        bias = [
            jnp.where(
                (rows == 0) & (frame >= frames_valid[column * 2 + clip]), -1e30, 0.0
            ).astype(bf16)
            for clip in range(2)
        ]

        def score(item, scores):
            clip, head = item % 2, item // 2
            key_x = jnp.concatenate([qkv[1, clip, head], bias[clip]], axis=0)
            query_x = jnp.concatenate([qkv[0, clip, head], ones_row], axis=0)
            value = lax.dot_general(key_x, query_x, tn, preferred_element_type=f32)
            scores[...] = value
            return jnp.max(value, axis=0, keepdims=True)

        def mix(item, scores, top):
            clip, head = item % 2, item // 2
            value_x = jnp.concatenate([qkv[2, clip, head], ones_row], axis=0)
            raised = jnp.exp(scores[...] - top).astype(bf16)
            mixed = jnp.dot(value_x, raised, preferred_element_type=f32)
            total = mixed[HEAD : HEAD + 1]
            att[clip, head] = (mixed[:HEAD] * (1.0 / total)).astype(bf16)

        top = score(0, score_refs[0])
        for item in range(2 * heads):
            if item + 1 < 2 * heads:
                next_top = score(item + 1, score_refs[(item + 1) % 2])
            mix(item, score_refs[item % 2], top)
            top = next_top

    wait_a.wait()
    for clip in range(2):
        copy_a[clip].wait()
        lhs = jnp.concatenate(
            [
                jnp.concatenate(
                    [
                        rows_in[8 * (t // 2) + block, 12 * (t % 2) : 12 * (t % 2) + 3].reshape(
                            96, 128
                        )
                        for block in range(8)
                    ],
                    axis=0,
                )
                for t in range(8)
            ],
            axis=1,
        )
        value = lax.dot_general(lhs, norm_a[clip], nt, preferred_element_type=f32)
        for s in range(3):
            kind = (s - role + 6) % 3
            for h in range(A_HEADS):
                start = s * A_COLS + h * HEAD
                put(qkv_a, kind, clip, h, value[start : start + HEAD])
    attention(qkv_a, att_a, A_HEADS)
    for clip in range(2):
        rows = att_a[clip].reshape(A_COLS, FRAMES)
        mean = lax.dot_general(pool_mat, rows, nt, preferred_element_type=f32).astype(bf16)
        pooled[:, clip * 32 : clip * 32 + 32, :A_COLS] = mean.reshape(ROLES, 32, A_COLS)

    wait_w.wait()
    copy_head_a.wait()
    copy_head_w.wait()
    pick_latents(slots, rows_in, lat)
    pred_a[...] = jnp.dot(lat[:ROWS], head_a[...], preferred_element_type=f32)
    pred_w[...] = jnp.dot(lat[:ROWS], head_w[...], preferred_element_type=f32)
    for clip in range(2):
        copy_w[clip].wait()
        lhs = jnp.concatenate(
            [
                jnp.concatenate(
                    [
                        rows_in[8 * zs + block, 12 * (t // 5) + 3 + t % 5]
                        for block in range(8)
                        for zs in range(4)
                    ],
                    axis=0,
                )
                for t in range(10)
            ],
            axis=1,
        )
        proj[...] = lax.dot_general(lhs, norm_w[clip], nt, preferred_element_type=f32)
        for s in range(3):
            kind = (s - role + 6) % 3
            for h in range(W_HEADS):
                start = s * W_COLS + h * HEAD
                parts = []
                while start < s * W_COLS + (h + 1) * HEAD:
                    block, inner = start // 120, start % 120
                    take = min(120 - inner, s * W_COLS + (h + 1) * HEAD - start)
                    parts.append(proj[block * 128 + inner : block * 128 + inner + take])
                    start += take
                value = parts[0] if len(parts) == 1 else jnp.concatenate(parts, axis=0)
                put(qkv_w, kind, clip, h, value)
    attention(qkv_w, att_w, W_HEADS)
    for clip in range(2):
        rows = att_w[clip].reshape(W_COLS, FRAMES)
        mean = lax.dot_general(pool_mat, rows, nt, preferred_element_type=f32).astype(bf16)
        mean = jnp.concatenate([mean, jnp.zeros((POOLED, 64), bf16)], axis=1)
        pooled[:, clip * 32 : clip * 32 + 32, A_COLS:] = mean.reshape(ROLES, 32, 384)
    for k in range(ROLES):
        outs[k][...] = pooled[(role + k) % ROLES]


def attend(frames_valid, slots, pieces, norm_a, norm_w, head_a, head_w):
    vmem = pl.BlockSpec(memory_space=pltpu.VMEM)
    return pl.pallas_call(
        attend_kernel,
        out_shape=[pltpu.VMEM((ROWS, OUT_COLS), bf16)] * ROLES
        + [
            pltpu.VMEM((2 * ROWS, STU_D), bf16),
            pltpu.VMEM((ROWS, WAVLM_D), f32),
            pltpu.VMEM((ROWS, WHISPER_D), f32),
        ],
        in_specs=[pl.BlockSpec(memory_space=pltpu.SMEM)] * 2
        + [pl.BlockSpec(memory_space=pl.ANY)] * 20,
        out_specs=[vmem] * 7,
        scratch_shapes=[
            pltpu.VMEM((2, FRAMES, WAVLM_D), bf16),
            pltpu.VMEM((2, FRAMES, WHISPER_D), bf16),
            pltpu.VMEM((32, 24, 32, 128), bf16),
            pltpu.VMEM((3, 2, A_HEADS, HEAD, FRAMES), bf16),
            pltpu.VMEM((3, 2, W_HEADS, HEAD, FRAMES), bf16),
            pltpu.VMEM((1024, FRAMES), f32),
            pltpu.VMEM((2, A_HEADS, HEAD, FRAMES), bf16),
            pltpu.VMEM((2, W_HEADS, HEAD, FRAMES), bf16),
            pltpu.VMEM((FRAMES, FRAMES), f32),
            pltpu.VMEM((FRAMES, FRAMES), f32),
            pltpu.VMEM((STU_D, WAVLM_D), bf16),
            pltpu.VMEM((STU_D, WHISPER_D), bf16),
            pltpu.VMEM((ROLES, ROWS, OUT_COLS), bf16),
            pltpu.SemaphoreType.DMA((8,)),
        ],
        cost_estimate=pl.CostEstimate(
            flops=8_000_000_000, bytes_accessed=12_000_000, transcendentals=5_000_000
        ),
        name="attend",
    )(frames_valid, slots, *pieces, norm_a, norm_w, head_a, head_w)


def slope_kernel(frames_valid, *refs):
    arrived = refs[:4]
    out_a_hbm, out_w_hbm, mean_a, mean_w, pred_a, pred_w = refs[4:10]
    outs, parts, grouped, out_a, out_w, sems = refs[10:14], *refs[14:19]
    copies = []
    for source, target in ((out_a_hbm, out_a), (out_w_hbm, out_w)):
        for start in range(0, source.shape[0], 256):
            rows = pl.ds(start, 256)
            copies.append(
                pltpu.make_async_copy(source.at[rows], target.at[rows], sems.at[len(copies)])
            )
            copies[-1].start()
    role = lax.axis_index("role")
    clip = lax.axis_index("dp") * 2
    for k in range(ROLES):
        parts[(role - k + ROLES) % ROLES] = arrived[k][...]
    row = lax.broadcasted_iota(jnp.int32, (ROWS, 1), 0)
    valid = jnp.where(row < 32, frames_valid[clip], frames_valid[clip + 1]) // POOL
    keep = (row % 32 + role * 32) < valid

    def slope_of(mean, waits, out, pred, cols, first):
        width = mean.shape[-1]
        attended = jnp.concatenate(
            [parts[r, :, first : first + cols] for r in range(ROLES)], axis=1
        )
        total = mean[...]
        for i, copy in enumerate(waits):
            copy.wait()
            rows = slice(256 * i, 256 * i + 256)
            total = total + jnp.dot(attended[:, rows], out[rows], preferred_element_type=f32)
        target = total.astype(bf16).astype(f32)
        predicted = pred[...]
        pred_sq = jnp.sum(predicted * predicted, axis=-1, keepdims=True) + epsilon_cos
        targ_sq = jnp.sum(target * target, axis=-1, keepdims=True) + epsilon_cos
        pred_norm = jnp.sqrt(pred_sq)
        both = pred_norm * jnp.sqrt(targ_sq)
        cosine = jnp.sum(predicted * target, axis=-1, keepdims=True) / both
        slope = (cosine / (pred_norm * pred_norm)) * predicted - target / both
        slope = slope + (predicted - target) * (1.0 / width)
        return jnp.where(keep, slope, 0.0).astype(bf16)

    slope_a = slope_of(mean_a, copies[:4], out_a, pred_a, A_COLS, 0)
    for g in range(ROLES):
        grouped[g, :, :A_COLS] = slope_a[:, g * A_COLS : (g + 1) * A_COLS]
    slope_w = slope_of(mean_w, copies[4:], out_w, pred_w, W_COLS, A_COLS)
    for g in range(ROLES):
        grouped[g, :, A_COLS:] = jnp.concatenate(
            [slope_w[:, g * W_COLS : (g + 1) * W_COLS], jnp.zeros((ROWS, 64), bf16)], axis=1
        )
    for k in range(ROLES):
        outs[k][...] = grouped[(role + k) % ROLES]


def slopes(frames_valid, parts, out_a, out_w, mean_a, mean_w, pred_a, pred_w):
    vmem = pl.BlockSpec(memory_space=pltpu.VMEM)
    return pl.pallas_call(
        slope_kernel,
        out_shape=[pltpu.VMEM((ROWS, OUT_COLS), bf16)] * ROLES,
        in_specs=[pl.BlockSpec(memory_space=pltpu.SMEM)]
        + [vmem] * 4
        + [pl.BlockSpec(memory_space=pl.ANY)] * 2
        + [vmem] * 4,
        out_specs=[vmem] * ROLES,
        scratch_shapes=[pltpu.VMEM((ROLES, ROWS, OUT_COLS), bf16)] * 2
        + [
            pltpu.VMEM((WAVLM_D, WAVLM_D), bf16),
            pltpu.VMEM((WHISPER_D, WHISPER_D), bf16),
            pltpu.SemaphoreType.DMA((9,)),
        ],
        name="slopes",
    )(frames_valid, *near(*parts), out_a, out_w, *near(mean_a, mean_w, pred_a, pred_w))


def outer_kernel(*refs):
    lats, own, other, out = refs[:4], refs[4:8], refs[8:12], refs[12]
    start = pl.multiple_of((lax.axis_index("dp") % 2) * 256, 256)
    lat = jnp.concatenate([lats[k][:, pl.ds(start, 256)] for k in range(ROLES)], axis=0)
    rows = []
    for k in range(ROLES):
        rows += [own[k][...], other[k][...]]
    grad = lax.dot_general(
        lat, jnp.concatenate(rows, axis=0), (((0,), (0,)), ((), ())), preferred_element_type=f32
    )
    grad = grad.reshape(16, 16, OUT_COLS)
    for t in range(4):
        out[:, 16 * t : 16 * t + 16] = grad[:, :, 128 * t : 128 * t + 128]
    out[:, 64:] = jnp.concatenate([grad[:, :8, 512:576], grad[:, 8:, 512:576]], axis=-1)


def outer(lats, own, other):
    vmem = pl.BlockSpec(memory_space=pltpu.VMEM)
    return pl.pallas_call(
        outer_kernel,
        out_shape=pltpu.VMEM((16, 72, 128), f32),
        in_specs=[vmem] * 12,
        out_specs=vmem,
        name="outer",
    )(*near(*lats, *own, *other))


def sum_kernel(x, out):
    total = jnp.sum(x[...], axis=0).astype(bf16)
    out[...] = jnp.broadcast_to(total[None], out.shape)


def reduce_parts(x):
    vmem = pl.BlockSpec(memory_space=pltpu.VMEM)
    return pl.pallas_call(
        sum_kernel,
        out_shape=pltpu.VMEM((64, 72, 128), bf16),
        in_specs=[vmem],
        out_specs=vmem,
        name="reduce_parts",
    )(*near(x))


def place_kernel(piece, *refs):
    out_a, out_w = refs[-2:]
    blocks = []
    step = pl.program_id(0) * 8
    for g in range(ROLES):
        block = piece[g, pl.ds(step, 8)].astype(f32)
        for t in range(2):
            lane = g * A_COLS + 128 * t
            out_a[0, :, lane : lane + 128] = block[:, 16 * t : 16 * t + 16].reshape(128, 128)
            blocks.append(block[:, 32 + 16 * t : 48 + 16 * t].reshape(128, 128))
        last = block[:, 64:]
        last = jnp.concatenate([last[:, :, :64], last[:, :, 64:]], axis=1)
        blocks.append(last.reshape(128, 64))
    out_w[0] = jnp.concatenate(blocks, axis=1)


def place(piece, partner, held=()):
    half = lambda: (lax.axis_index("dp") + partner) % 2
    hbm = pl.BlockSpec(memory_space=pl.ANY)
    return pl.pallas_call(
        place_kernel,
        grid=(2,),
        out_shape=[
            jax.ShapeDtypeStruct((2, 256, WAVLM_D), f32),
            jax.ShapeDtypeStruct((2, 256, WHISPER_D), f32),
        ],
        in_specs=[pl.BlockSpec(memory_space=pltpu.VMEM)]
        + [hbm] * len(held),
        out_specs=[
            pl.BlockSpec((1, 128, WAVLM_D), lambda i: (half(), i, 0)),
            pl.BlockSpec((1, 128, WHISPER_D), lambda i: (half(), i, 0)),
        ],
        input_output_aliases={1: 0, 2: 1} if held else {},
        name="place_partner" if partner else "place_own",
    )(*near(piece), *held)


PLANE = [[z * 8 + y * 2 + c for z in range(4) for y in range(4)] for c in range(2)]
SLICE = [[r * 32 + i for r in range(ROLES) for i in plane] for plane in PLANE]


def per_device(
    wavlm_hidden,
    whisper_hidden,
    wavlm_qkv,
    whisper_qkv,
    wavlm_out,
    whisper_out,
    frames_valid,
    slot_clip,
    latent,
    wavlm_head,
    whisper_head,
):
    chip_clips = lax.axis_index("dp") // 2 * 4 + jnp.arange(4)
    match = slot_clip[None, :] == chip_clips[:, None]
    slots = jnp.sum(jnp.where(match, jnp.arange(CLIPS)[None, :], 0), axis=1).astype(jnp.int32)
    raw, *chunks = weight_chunks(wavlm_qkv.T, whisper_qkv.T, latent)
    chunks = [chunks[0]] + [dp_send(chunks[k], k, 0, 0) for k in (1, 2, 3)]
    raws = [raw] + [dp_send(raw, k, 0, 0) for k in (1, 2, 3)]
    second = second_shares(chunks, latent)
    seconds = [second] + [dp_send(second, 0, k, 0) for k in (1, 2, 3)]
    first = first_shares(raws)
    second = stacked(seconds)
    pieces = spread_cross(first, second)
    pieces = pieces + [dp_send(x, 0, 0, 1) for x in pieces]
    norm_a, mean_a = norms(wavlm_hidden)
    norm_w, mean_w = norms(whisper_hidden)

    *pooled, lat, pred_a, pred_w = attend(
        frames_valid, slots, pieces, norm_a, norm_w, wavlm_head, whisper_head
    )
    parts = [pooled[0]] + [role_send(pooled[k], k) for k in (1, 2, 3)]
    lats = [lat] + [role_send(lat, k) for k in (1, 2, 3)]
    sloped = slopes(
        frames_valid, parts, wavlm_out, whisper_out, mean_a, mean_w, pred_a, pred_w
    )
    slope_own = [sloped[0]] + [role_send(sloped[k], k) for k in (1, 2, 3)]
    slope_other = [dp_send(x, 0, 0, 1) for x in slope_own]
    halves = outer(lats, slope_own, slope_other)
    arrived = lax.all_to_all(
        halves, "dp", split_axis=0, concat_axis=0, tiled=True, axis_index_groups=PLANE
    )
    summed = lax.all_to_all(
        reduce_parts(arrived),
        ("role", "dp"),
        split_axis=0,
        concat_axis=0,
        tiled=True,
        axis_index_groups=SLICE,
    ).reshape(ROLES, 16, 72, 128)
    partner = dp_send(summed, 0, 0, 1)
    held = place(summed, 0)
    grad_a, grad_w = place(partner, 1, held)
    return grad_a.reshape(STU_D, WAVLM_D), grad_w.reshape(STU_D, WHISPER_D)


def solution(mesh):
    in_specs = (
        P("dp", None, None),
        P("dp", None, None),
        P(None, "dp"),
        P(None, "dp"),
        P(),
        P(),
        P(),
        P(),
        P(None, "dp", None, None),
        P(),
        P(),
    )
    out_specs = (P(), P())

    return jax.shard_map(
        per_device, mesh=mesh, in_specs=in_specs, out_specs=out_specs, check_vma=False
    )
```
